32 devices in a mesh: group: 4 (over y, core), span: 8 (over z, x).
Axes of the slice: x: 2, y: 2, z: 4, core: 2. Of those that a mesh axis runs over, the one named last changes fastest.
Arguments:
- tokens: bfloat16 [4096, 1024], P(('group', 'span')), may hold values from -32 to 32
- query_weight: bfloat16 [1024, 1024], replicated, may hold values from -0.1875 to 0.1875
- key_weight: bfloat16 [1024, 1024], replicated, may hold values from -0.1875 to 0.1875
- value_weight: bfloat16 [1024, 1024], replicated, may hold values from -0.1875 to 0.1875
- log_decay: float32 [16, 4096], P(None, ('group', 'span')), may hold values from -0.6 to 0
- neighbour_blocks: int32 [32, 4], P(('group', 'span')), may hold values from 0 to 31, as said below
- cotangent: bfloat16 [4096, 1024], P(('group', 'span')), may hold values from -6 to 6
Outputs:
- layer_out: bfloat16 [4096, 1024], P(('group', 'span'))
- tokens_grad: bfloat16 [4096, 1024], P(('group', 'span'))
- query_grad: bfloat16 [1024, 1024], replicated
- key_grad: bfloat16 [1024, 1024], replicated
- value_grad: bfloat16 [1024, 1024], replicated
The draws below stay inside these ranges and needn't reach their ends.
Inputs may be any that keep to these rules, and one draw needn't show every extreme that they name: `neighbour_blocks`: row b is [b, b - 1, b - 1, b - 1]; any entry that would fall before block 0 is block 0.
All inputs are finite; a program needn't handle non-finite values.
Results may differ from the reference program's by a relative error of at most 0.0077.
Values may be sent and summed in bfloat16 or wider, within the bound.
A program may use at most 192 MiB of HBM per device.

```python
import math
import jax
import jax.numpy as jnp
from jax import lax

D = 1024
ATTENDER_NUMBER = 16
DH = 64
TOK_DEV = 128
BLK = 128
NB = 4
FRAME_ELEMENTS = 4096


def draw_tokens(key, part):
    base_vals = jnp.clip(jax.random.normal(jax.random.fold_in(key, 1), (FRAME_ELEMENTS, D), jnp.float32), -4.5, 4.5)
    return base_vals.astype(jnp.bfloat16)


def attention_pair(key):
    first_matrix = jnp.clip(jax.random.normal(jax.random.fold_in(key, 11), (D, D), jnp.float32), -6.0, 6.0) / math.sqrt(D)
    other_matrix = jnp.clip(jax.random.normal(jax.random.fold_in(key, 12), (D, D), jnp.float32), -6.0, 6.0) / math.sqrt(D)
    second_matrix = other_matrix
    return (first_matrix, second_matrix)


def draw_query_weight(key, part):
    return attention_pair(key)[0].astype(jnp.bfloat16)


def draw_key_weight(key, part):
    return attention_pair(key)[1].astype(jnp.bfloat16)


def draw_log_decay(key, part):
    lookup_fragments = jax.random.split(key, 6)
    fast_share = 0.5
    seg_count = FRAME_ELEMENTS // TOK_DEV
    is_fast = jax.random.uniform(lookup_fragments[0], (ATTENDER_NUMBER, 1, 1), jnp.float32) < fast_share
    fast_rate = jnp.exp(jax.random.uniform(lookup_fragments[1], (ATTENDER_NUMBER, 1, 1), jnp.float32, math.log(1.0 / 50.0), math.log(1.0 / 30.0)))
    slow_rate = jnp.exp(jax.random.uniform(lookup_fragments[2], (ATTENDER_NUMBER, 1, 1), jnp.float32, math.log(0.1), math.log(0.4))) / FRAME_ELEMENTS
    device_factor = jnp.exp(jax.random.uniform(lookup_fragments[3], (ATTENDER_NUMBER, seg_count, 1), jnp.float32, math.log(0.5), math.log(2.0)))
    default_forget_factors = -jnp.broadcast_to(jnp.where(is_fast, fast_rate, slow_rate) * device_factor, (ATTENDER_NUMBER, seg_count, TOK_DEV)).reshape(ATTENDER_NUMBER, FRAME_ELEMENTS)
    pulse_volley_locations = jax.random.randint(lookup_fragments[4], (2,), 0, FRAME_ELEMENTS)
    pulse_volley_extent = jax.random.uniform(lookup_fragments[5], (ATTENDER_NUMBER, 2), jnp.float32, 0.22, 0.5)
    pairing_tallies = (jnp.arange(FRAME_ELEMENTS)[None, :, None] == pulse_volley_locations[None, None, :]).astype(jnp.float32)
    return default_forget_factors - jnp.sum(pairing_tallies * pulse_volley_extent[:, None, :], axis=2)


def draw_neighbour_blocks(key, part):
    block_total = FRAME_ELEMENTS // BLK
    per_dev = TOK_DEV // BLK
    own_block = jnp.arange(block_total, dtype=jnp.int32)[:, None]
    reach_back = jax.random.randint(key, (block_total, NB - 2), 1, per_dev + 1)
    far_block = jnp.maximum(own_block - per_dev, 0)
    near_block = jnp.maximum(own_block - reach_back, 0)
    return jnp.concatenate([own_block, far_block, near_block], axis=1).astype(jnp.int32)


def steps_of(stream_key, shape, cuts, least, largest):
    level, own = 1.0, jax.random.fold_in(stream_key, 6)
    for axis_at, shards_of in cuts:
        heights = jnp.exp(jax.random.uniform(jax.random.fold_in(own, axis_at), (shards_of,), jnp.float32, least / len(cuts), largest / len(cuts)))
        level = level * jnp.repeat(heights, shape[axis_at] // shards_of).reshape([-1 if axis == axis_at else 1 for axis in range(len(shape))])
    return level


def scatter_about(own_key, shape, width, most, pieces=(), kind=jnp.bfloat16):
    level = steps_of(own_key, shape, pieces, -0.22, 0.18) if pieces else 1.0
    drawn = jax.random.normal(own_key, shape, jnp.float32) * width * level
    return jnp.minimum(jnp.maximum(drawn, -most), most).astype(kind)


def setup_inputs(seed: int = 0) -> dict:
    arg_keys = jax.random.split(jax.random.key(seed), 8)
    tokens = draw_tokens(jax.random.fold_in(arg_keys[7], 71), 0)
    query_weight = draw_query_weight(jax.random.fold_in(arg_keys[7], 71), 0)
    key_weight = draw_key_weight(jax.random.fold_in(arg_keys[7], 71), 0)
    value_weight = scatter_about(arg_keys[3], (D, D), D ** -0.5, 0.1875)
    log_decay = draw_log_decay(jax.random.fold_in(arg_keys[7], 71), 0)
    neighbour_blocks = draw_neighbour_blocks(jax.random.fold_in(arg_keys[7], 71), 0)
    cotangent = scatter_about(arg_keys[6], (FRAME_ELEMENTS, D), 1.0, 6.0, ((0, 32),))
    return {"tokens": tokens, "query_weight": query_weight, "key_weight": key_weight, "value_weight": value_weight, "log_decay": log_decay, "neighbour_blocks": neighbour_blocks, "cotangent": cotangent}


def rounded(values):
    return lax.optimization_barrier(values.astype(jnp.bfloat16)).astype(jnp.float32)

def summarize(rate_seg, query, key, value, grad_out):
    row_count, feat_width = query.shape
    head_count = rate_seg.shape[0]
    head_size = feat_width // head_count
    lin_scale = 1.0 / (head_size * math.sqrt(row_count))
    running = jnp.cumsum(rate_seg, axis=1)
    seg_total = running[:, -1]
    fading = jnp.exp(seg_total[:, None] - running).T[:, :, None]
    growth = jnp.exp(running).T[:, :, None]
    q_heads = query.reshape(row_count, head_count, head_size).astype(jnp.float32)
    k_heads = key.reshape(row_count, head_count, head_size).astype(jnp.float32)
    v_heads = value.reshape(row_count, head_count, head_size).astype(jnp.float32)
    g_heads = grad_out.reshape(row_count, head_count, head_size).astype(jnp.float32)
    weighted = rounded(v_heads * fading)
    local_state = jnp.einsum('shd,she->hde', k_heads, weighted)
    scaled_grad = rounded(g_heads * growth)
    head_grad = lin_scale * jnp.einsum('thd,the->hde', q_heads, scaled_grad)
    return (seg_total, local_state, head_grad)

def segment_work(rate_seg, query, keyval, prev_keyval, grad_out, local_ids, state_in, later):
    row_count, feat_width = query.shape
    head_count = rate_seg.shape[0]
    head_size = feat_width // head_count
    blocks = row_count // BLK
    lin_scale = 1.0 / (head_size * math.sqrt(row_count))
    soft_scale = 1.0 / math.sqrt(head_size)
    running = jnp.cumsum(rate_seg, axis=1)
    seg_total = running[:, -1]
    growth = jnp.exp(running).T[:, :, None]
    fading = jnp.exp(seg_total[:, None] - running).T[:, :, None]
    places = jnp.arange(row_count, dtype=jnp.int32)
    is_lower = places[:, None] >= places[None, :]
    decay_mat = jnp.where(is_lower[None], jnp.exp(jnp.minimum(running[:, :, None] - running[:, None, :], 0.0)), 0.0)
    q_heads = query.reshape(row_count, head_count, head_size).astype(jnp.float32)
    k_heads = keyval[:, :feat_width].reshape(row_count, head_count, head_size).astype(jnp.float32)
    v_heads = keyval[:, feat_width:].reshape(row_count, head_count, head_size).astype(jnp.float32)
    g_heads = grad_out.reshape(row_count, head_count, head_size).astype(jnp.float32)
    intra_mat = rounded(jnp.einsum('thd,shd->hts', q_heads, k_heads) * decay_mat)
    state_bf = rounded(state_in)
    linear_out = jnp.einsum('hts,she->the', intra_mat, v_heads) + growth * jnp.einsum('thd,hde->the', q_heads, state_bf)
    extended = jnp.concatenate([prev_keyval, keyval], axis=0).reshape(2 * blocks, BLK, 2 * feat_width)
    picked = jnp.take(extended, local_ids, axis=0).reshape(blocks, NB * BLK, 2 * feat_width).astype(jnp.float32)
    near_key = picked[:, :, :feat_width].reshape(blocks, NB * BLK, head_count, head_size)
    near_val = picked[:, :, feat_width:].reshape(blocks, NB * BLK, head_count, head_size)
    q_blocks = q_heads.reshape(blocks, BLK, head_count, head_size)
    g_blocks = g_heads.reshape(blocks, BLK, head_count, head_size)
    logits = jnp.einsum('bthd,bshd->bhts', q_blocks, near_key) * soft_scale
    row_peak = lax.optimization_barrier(jnp.max(logits, axis=-1, keepdims=True))
    exp_terms = jnp.exp(logits - row_peak)
    soft_probs = exp_terms / lax.optimization_barrier(jnp.sum(exp_terms, axis=-1, keepdims=True))
    probs_bf = rounded(soft_probs)
    near_out = jnp.einsum('bhts,bshd->bthd', probs_bf, near_val).reshape(row_count, head_count, head_size)
    layer_out = (lin_scale * linear_out + near_out).reshape(row_count, feat_width).astype(jnp.bfloat16)
    prob_grad = jnp.einsum('bthd,bshd->bhts', g_blocks, near_val)
    inner_sum = lax.optimization_barrier(jnp.sum(soft_probs * prob_grad, axis=-1, keepdims=True))
    dlogit = rounded(soft_probs * (prob_grad - inner_sum) * soft_scale)
    dq_near = jnp.einsum('bhts,bshd->bthd', dlogit, near_key).reshape(row_count, head_count, head_size)
    dk_near = jnp.einsum('bhts,bthd->bshd', dlogit, q_blocks).reshape(blocks * NB, BLK, feat_width)
    dv_near = jnp.einsum('bhts,bthd->bshd', probs_bf, g_blocks).reshape(blocks * NB, BLK, feat_width)
    dpicked = jnp.concatenate([dk_near, dv_near], axis=-1)
    onehot = (local_ids.reshape(-1)[:, None] == jnp.arange(2 * blocks, dtype=jnp.int32)[None, :]).astype(jnp.float32)
    ext_grad = jnp.einsum('nm,ntc->mtc', onehot, dpicked, precision=lax.Precision.HIGHEST).reshape(2 * row_count, 2 * feat_width)
    back_mat = rounded(jnp.einsum('thd,shd->hts', g_heads, v_heads) * decay_mat)
    later_bf = rounded(later)
    dq_lin = lin_scale * (jnp.einsum('hts,shd->thd', back_mat, k_heads) + growth * jnp.einsum('the,hde->thd', g_heads, state_bf))
    dk_lin = lin_scale * jnp.einsum('hts,thd->shd', back_mat, q_heads) + fading * jnp.einsum('she,hde->shd', v_heads, later_bf)
    dv_lin = lin_scale * jnp.einsum('hts,the->she', intra_mat, g_heads) + fading * jnp.einsum('shd,hde->she', k_heads, later_bf)
    query_delta = (dq_lin + dq_near).reshape(row_count, feat_width).astype(jnp.bfloat16)
    lin_kv = jnp.concatenate([dk_lin.reshape(row_count, feat_width), dv_lin.reshape(row_count, feat_width)], axis=1)
    own_grad = (lin_kv + ext_grad[row_count:]).astype(jnp.bfloat16)
    prev_grad = ext_grad[:row_count].astype(jnp.bfloat16)
    return (layer_out, query_delta, own_grad, prev_grad)

def reference(tokens, query_weight, key_weight, value_weight, log_decay, neighbour_blocks, cotangent):
    query = jnp.dot(tokens, query_weight, preferred_element_type=jnp.float32).astype(jnp.bfloat16)
    key = jnp.dot(tokens, key_weight, preferred_element_type=jnp.float32).astype(jnp.bfloat16)
    value = jnp.dot(tokens, value_weight, preferred_element_type=jnp.float32).astype(jnp.bfloat16)
    keyval = jnp.concatenate([key, value], axis=1)
    seg_count = FRAME_ELEMENTS // TOK_DEV
    per_dev = TOK_DEV // BLK
    rate_segs = log_decay.reshape(ATTENDER_NUMBER, seg_count, TOK_DEV).transpose(1, 0, 2)
    q_segs = query.reshape(seg_count, TOK_DEV, D)
    k_segs = key.reshape(seg_count, TOK_DEV, D)
    v_segs = value.reshape(seg_count, TOK_DEV, D)
    kv_segs = keyval.reshape(seg_count, TOK_DEV, 2 * D)
    g_segs = cotangent.reshape(seg_count, TOK_DEV, D)

    def summary_entry(entry):
        return summarize(entry[0], entry[1], entry[2], entry[3], entry[4])
    totals, states, head_grads = lax.map(summary_entry, (rate_segs, q_segs, k_segs, v_segs, g_segs))

    def advance(running_state, entry):
        return (jnp.exp(entry[0])[:, None, None] * running_state + entry[1], running_state)
    zero_state = jnp.zeros((ATTENDER_NUMBER, DH, DH), jnp.float32)
    _, state_in = lax.scan(advance, zero_state, (totals, states))
    _, later = lax.scan(advance, zero_state, (totals, head_grads), reverse=True)
    padded = jnp.concatenate([jnp.zeros((TOK_DEV, 2 * D), jnp.bfloat16), keyval], axis=0)
    block_ids = neighbour_blocks.reshape(seg_count, per_dev, NB)

    def work_entry(entry):
        seg_index = entry[0]
        prev_keyval = lax.dynamic_slice_in_dim(padded, (seg_index * TOK_DEV).astype(jnp.int32), TOK_DEV, 0)
        local_ids = (entry[5] - (seg_index - 1) * per_dev).astype(jnp.int32)
        return segment_work(entry[1], entry[2], entry[3], prev_keyval, entry[4], local_ids, entry[6], entry[7])
    outs_seg, delta_seg, own_seg, prev_seg = lax.map(work_entry, (jnp.arange(seg_count, dtype=jnp.int32), rate_segs, q_segs, kv_segs, g_segs, block_ids, state_in, later))
    layer_out = outs_seg.reshape(FRAME_ELEMENTS, D)
    query_delta = delta_seg.reshape(FRAME_ELEMENTS, D)
    own_grad = own_seg.reshape(FRAME_ELEMENTS, 2 * D)
    next_grad = jnp.concatenate([prev_seg[1:], jnp.zeros_like(prev_seg[:1])], axis=0).reshape(FRAME_ELEMENTS, 2 * D)
    tokens_grad = jnp.dot(query_delta, query_weight.T, preferred_element_type=jnp.float32)
    tokens_grad = tokens_grad + jnp.dot(own_grad[:, :D], key_weight.T, preferred_element_type=jnp.float32)
    tokens_grad = tokens_grad + jnp.dot(own_grad[:, D:], value_weight.T, preferred_element_type=jnp.float32)
    tokens_grad = tokens_grad + jnp.dot(next_grad[:, :D], key_weight.T, preferred_element_type=jnp.float32)
    tokens_grad = tokens_grad + jnp.dot(next_grad[:, D:], value_weight.T, preferred_element_type=jnp.float32)
    grad_norm = 1.0 / math.sqrt(FRAME_ELEMENTS)
    query_grad = jnp.dot(tokens.T, query_delta, preferred_element_type=jnp.float32) * grad_norm
    key_grad = (jnp.dot(tokens.T, own_grad[:, :D], preferred_element_type=jnp.float32) + jnp.dot(tokens.T, next_grad[:, :D], preferred_element_type=jnp.float32)) * grad_norm
    value_grad = (jnp.dot(tokens.T, own_grad[:, D:], preferred_element_type=jnp.float32) + jnp.dot(tokens.T, next_grad[:, D:], preferred_element_type=jnp.float32)) * grad_norm
    return (layer_out, tokens_grad.astype(jnp.bfloat16), query_grad.astype(jnp.bfloat16), key_grad.astype(jnp.bfloat16), value_grad.astype(jnp.bfloat16))
```

```python
import functools
import math

import jax
import jax.numpy as jnp
from jax import lax
from jax.experimental import pallas as pl
from jax.experimental.pallas import tpu as pltpu
from jax.sharding import PartitionSpec as P

AXES = ("group", "span")
F32 = jnp.float32
BF16 = jnp.bfloat16
ROWS = (((0,), (0,)), ((), ()))
MESH = pl.DeviceIdType.MESH
COLS = (((1,), (1,)), ((), ()))


def shifted(block, axis, distance):
    devices = range(lax.axis_size(axis))
    route = [(i - distance, i) for i in devices if i - distance in devices]
    return lax.ppermute(block, axis, route)


def dot(a, b, dims=(((1,), (0,)), ((), ()))):
    return lax.dot_general(a, b, dims, preferred_element_type=F32)


def summary_kernel(lin_scale, size, q, k, v, g, col, out):
    heads = q.shape[1] // size
    states, grads = [], []
    for j in range(heads):
        cut = slice(j * size, (j + 1) * size)
        run = col[0, :, j : j + 1]
        fading = jnp.exp(run[run.shape[0] - 1 :, :] - run)
        weighted = (v[:, cut].astype(F32) * fading).astype(BF16)
        scaled = (g[:, cut].astype(F32) * jnp.exp(run)).astype(BF16)
        states.append(dot(k[:, cut], weighted, ROWS))
        grads.append(lin_scale * dot(q[:, cut], scaled, ROWS))
    out[:size, :] = jnp.concatenate(states, axis=1).astype(BF16)
    out[size:, :] = jnp.concatenate(grads, axis=1).astype(BF16)


def near_pair(lin_scale, soft_scale, size, q, k, v, g, pk, pv, col, row, times):
    rows = q.shape[0]
    heads = q.shape[1] // size
    t = lax.broadcasted_iota(jnp.int32, (rows, rows), 0)
    s = lax.broadcasted_iota(jnp.int32, (rows, rows), 1)
    lower = t >= s
    outs, dqs, dkv, dvv = [], [], [], []
    for j in range(heads):
        cut = slice(j * size, (j + 1) * size)
        qh, gh = q[:, cut], g[:, cut]
        kh = jnp.concatenate([k[:, cut], pk[:, cut]], axis=0)
        vh = jnp.concatenate([v[:, cut], pv[:, cut]], axis=0)
        decay = jnp.where(
            lower, jnp.exp(jnp.minimum(col[:, j : j + 1] - row[j : j + 1, :], 0.0)), 0.0
        ) * lin_scale
        score = dot(qh, kh, COLS)
        grad = dot(gh, vh, COLS)
        logits = jnp.where(times > 0.0, score * soft_scale, -1e30)
        peak = jnp.max(logits, axis=1, keepdims=True)
        terms = jnp.exp(logits - peak) * times
        probs = terms / jnp.sum(terms, axis=1, keepdims=True)
        inner = jnp.sum(probs * grad, axis=1, keepdims=True)
        dlogit = probs * (grad - inner) * soft_scale
        mix = jnp.concatenate(
            [probs[:, :rows] + score[:, :rows] * decay, probs[:, rows:]], axis=1
        ).astype(BF16)
        dmix = jnp.concatenate(
            [dlogit[:, :rows] + grad[:, :rows] * decay, dlogit[:, rows:]], axis=1
        ).astype(BF16)
        outs.append(dot(mix, vh))
        dqs.append(dot(dmix, kh))
        dkv.append(dot(dmix, qh, ROWS))
        dvv.append(dot(mix, gh, ROWS))
    dk = jnp.concatenate(dkv, axis=1)
    dv = jnp.concatenate(dvv, axis=1)
    return (
        jnp.concatenate(outs, axis=1),
        jnp.concatenate(dqs, axis=1),
        dk[:rows],
        dv[:rows],
        dk[rows:].astype(BF16),
        dv[rows:].astype(BF16),
    )


def state_kernel(
    lin_scale, size, q, k, v, g, col, carry, out, dq, own_k, own_v,
    layer, delta, grad_k, grad_v,
):
    heads = q.shape[1] // size
    state, later = carry[:size, :], carry[size:, :]
    outs, dqs, dks, dvs = [], [], [], []
    for j in range(heads):
        cut = slice(j * size, (j + 1) * size)
        run = col[0, :, j : j + 1]
        growth = lin_scale * jnp.exp(run)
        fading = jnp.exp(run[run.shape[0] - 1 :, :] - run)
        st, lt = state[:, cut], later[:, cut]
        outs.append(growth * dot(q[:, cut], st))
        dqs.append(growth * dot(g[:, cut], st, COLS))
        dks.append(fading * dot(v[:, cut], lt, COLS))
        dvs.append(fading * dot(k[:, cut], lt))
    layer[...] = (out[...] + jnp.concatenate(outs, axis=1)).astype(BF16)
    delta[...] = (dq[...] + jnp.concatenate(dqs, axis=1)).astype(BF16)
    grad_k[...] = (own_k[...] + jnp.concatenate(dks, axis=1)).astype(BF16)
    grad_v[...] = (own_v[...] + jnp.concatenate(dvs, axis=1)).astype(BF16)


def attention_parts(row_count, feat_width, head_count):
    size = feat_width // head_count
    pair = 256 // size
    steps = head_count // pair
    lanes = pair * size
    wide = pl.BlockSpec((row_count, lanes), lambda i: (0, i))
    col = pl.BlockSpec((1, row_count, pair), lambda i: (i, 0, 0))
    row = pl.BlockSpec((1, pair, row_count), lambda i: (i, 0, 0))
    return size, pair, steps, lanes, wide, col, row


def project(inputs, weight):
    return dot(inputs, weight).astype(BF16)


def shards(tokens, query_weight, key_weight, value_weight, log_decay, neighbour_blocks, cotangent):
    row_count, feat_width = tokens.shape
    head_count = log_decay.shape[0]
    size, pair, steps, lanes, wide, col_spec, row_spec = attention_parts(
        row_count, feat_width, head_count
    )
    lin_scale = 1.0 / (size * math.sqrt(row_count))
    soft_scale = 1.0 / math.sqrt(size)
    sizes = tuple(lax.axis_size(name) for name in AXES)
    devices = sizes[0] * sizes[1]
    position = lax.axis_index(AXES)
    shape = lambda dtype: jax.ShapeDtypeStruct((row_count, feat_width), dtype)

    prev_tokens = shifted(tokens, AXES, 1)
    places = jnp.arange(row_count)
    upto = (places[:, None] <= places[None, :]).astype(F32)
    running = jnp.dot(log_decay, upto, precision=lax.Precision.HIGHEST)
    row = running.reshape(steps, pair, row_count)
    col = row.transpose(0, 2, 1)
    query = project(tokens, query_weight)
    key = project(tokens, key_weight)
    value = project(tokens, value_weight)

    summary = pl.pallas_call(
        functools.partial(summary_kernel, lin_scale, size),
        grid=(steps,),
        in_specs=[wide] * 4 + [col_spec],
        out_specs=pl.BlockSpec((2 * size, lanes), lambda i: (0, i)),
        out_shape=jax.ShapeDtypeStruct((2 * size, feat_width), BF16),
        cost_estimate=pl.CostEstimate(flops=10**8, bytes_accessed=10**6, transcendentals=0),
    )(query, key, value, cotangent, col)
    total = jnp.broadcast_to(jnp.repeat(running[:, -1], size)[None, :], (8, feat_width))

    prev_key = project(prev_tokens, key_weight)
    prev_value = project(prev_tokens, value_weight)
    own_times = jnp.sum(neighbour_blocks == position).astype(F32)
    prev_times = jnp.sum(neighbour_blocks == position - 1).astype(F32)
    times = jnp.where(jnp.arange(2 * row_count) < row_count, own_times, prev_times)[None, :]
    near = functools.partial(near_pair, lin_scale, soft_scale, size)
    operands = (query, key, value, cotangent, prev_key, prev_value, col, row, times)
    carry, out, dq, own_k, own_v, prev_gk, prev_gv = carried(near, summary, total, operands, sizes)

    owed = dot(prev_gk, key_weight, COLS) + dot(prev_gv, value_weight, COLS)
    owed = shifted(owed.astype(BF16), AXES, -1)

    layer_out, query_delta, grad_k, grad_v = pl.pallas_call(
        functools.partial(state_kernel, lin_scale, size),
        grid=(steps,),
        in_specs=[wide] * 4
        + [col_spec, pl.BlockSpec((2 * size, lanes), lambda i: (0, i))]
        + [wide] * 4,
        out_specs=[wide] * 4,
        out_shape=[shape(BF16)] * 4,
        cost_estimate=pl.CostEstimate(flops=10**9, bytes_accessed=10**7, transcendentals=0),
    )(query, key, value, cotangent, col, carry, out, dq, own_k, own_v)

    grad_norm = 1.0 / math.sqrt(row_count * devices)
    grads = reduce_grads(
        grad_norm,
        (tokens, prev_tokens, query_delta, grad_k, grad_v, prev_gk, prev_gv),
        sizes,
    )
    tokens_back = dot(query_delta, query_weight, COLS)
    tokens_back = tokens_back + dot(grad_k, key_weight, COLS) + dot(grad_v, value_weight, COLS)
    tokens_back = tokens_back + owed.astype(F32)
    return (layer_out, tokens_back.astype(BF16), *grads)


def bits_of(axis, size):
    return [(axis, k) for k in range(size.bit_length() - 1)]


def bit_of(bit):
    return (lax.axis_index(bit[0]) // 2 ** bit[1]) % 2


def partner_of(bit):
    place = {name: lax.axis_index(name) for name in AXES}
    place[bit[0]] = place[bit[0]] + (1 - 2 * bit_of(bit)) * 2 ** bit[1]
    return place


def greet(bits):
    barrier = pltpu.get_barrier_semaphore()
    for bit in bits:
        pl.semaphore_signal(barrier, inc=1, device_id=partner_of(bit), device_id_type=MESH)
    pl.semaphore_wait(barrier, len(bits))


def carry_kernel(bits, near, size, x, total, *refs):
    ins, col, row, count = refs[:6], refs[6], refs[7], refs[8]
    out, results = refs[9], refs[10:16]
    sent, came, sums, sums_came, carry, sem, sum_sem = refs[16:]
    steps, _, pair = col.shape
    lanes = pair * size

    def near_step(i, _):
        cut = pl.ds(pl.multiple_of(i * lanes, lanes), lanes)
        values = near(*(ref[:, cut] for ref in ins), col[i], row[i], count[...])
        for ref, value in zip(results, values):
            ref[:, cut] = value
        return 0

    greet(bits)
    stages = len(bits)
    width = x.shape[1]
    tf = x[:size, :].astype(F32)
    tb = x[size:, :].astype(F32)
    carry[...] = jnp.zeros_like(carry)
    log_all = total[...]
    log_before = jnp.zeros_like(log_all)
    log_after = jnp.zeros_like(log_all)
    for i, bit in enumerate(bits):
        mine = bit_of(bit)
        if i:
            sums[i] = log_all
            sent[i, :size, :] = tf.astype(BF16)
            sent[i, size:, :] = tb.astype(BF16)
        rows = slice(None) if i + 1 < stages else pl.ds(pl.multiple_of(mine * size, size), size)
        copies = [
            pltpu.make_async_remote_copy(
                src_ref=sent.at[i, rows] if i else x.at[rows], dst_ref=came.at[i, rows],
                send_sem=sem.at[0, i], recv_sem=sem.at[1, i],
                device_id=partner_of(bit), device_id_type=MESH,
            ),
            pltpu.make_async_remote_copy(
                src_ref=sums.at[i] if i else total, dst_ref=sums_came.at[i],
                send_sem=sum_sem.at[0, i], recv_sem=sum_sem.at[1, i],
                device_id=partner_of(bit), device_id_type=MESH,
            ),
        ]
        for copy in copies:
            copy.start()
        lax.fori_loop(steps * i // stages, steps * (i + 1) // stages, near_step, 0)
        for copy in copies:
            copy.wait()
        log_other = sums_came[i]
        if i + 1 == stages:
            rows = pl.ds(pl.multiple_of((1 - mine) * size, size), size)
            gap = jnp.where(jnp.full((1, width), mine) == 1, log_before[:1], log_after[:1])
            carry[rows, :] += jnp.exp(gap) * came[i, rows, :].astype(F32)
            break
        f_other = came[i, :size, :].astype(F32)
        b_other = came[i, size:, :].astype(F32)
        second = jnp.full((1, width), mine) == 1
        scale = jnp.exp(jnp.where(second, log_before, log_after)[:1])
        carry[:size, :] += jnp.where(second, scale, 0.0) * f_other
        carry[size:, :] += jnp.where(second, 0.0, scale) * b_other
        log_before = log_before + jnp.where(second, log_other, 0.0)
        log_after = log_after + jnp.where(second, 0.0, log_other)
        here, there = jnp.exp(log_all[:1]), jnp.exp(log_other[:1])
        one = jnp.ones_like(here)
        tf = jnp.where(second, one, there) * tf + jnp.where(second, here, one) * f_other
        tb = jnp.where(second, there, one) * tb + jnp.where(second, one, here) * b_other
        log_all = log_all + log_other
    out[...] = carry[...].astype(BF16)


def carried(near, summary, total, operands, sizes):
    bits = bits_of("span", sizes[1]) + bits_of("group", sizes[0])
    rows, width = summary.shape
    stages = len(bits)
    vmem = pl.BlockSpec(memory_space=pltpu.VMEM)
    return pl.pallas_call(
        functools.partial(carry_kernel, bits, near, rows // 2),
        in_specs=[vmem] * (2 + len(operands)),
        out_specs=[vmem] * 7,
        out_shape=[jax.ShapeDtypeStruct((rows, width), BF16)]
        + [jax.ShapeDtypeStruct(operands[0].shape, F32)] * 4
        + [jax.ShapeDtypeStruct(operands[0].shape, BF16)] * 2,
        scratch_shapes=[
            pltpu.VMEM((stages, rows, width), BF16),
            pltpu.VMEM((stages, rows, width), BF16),
            pltpu.VMEM((stages, 8, width), F32),
            pltpu.VMEM((stages, 8, width), F32),
            pltpu.VMEM((rows, width), F32),
            pltpu.SemaphoreType.DMA((2, stages)),
            pltpu.SemaphoreType.DMA((2, stages)),
        ],
        compiler_params=pltpu.CompilerParams(collective_id=0, has_side_effects=True),
        cost_estimate=pl.CostEstimate(flops=10**9, bytes_accessed=10**8, transcendentals=0),
    )(summary, total, *operands)


def reduce_kernel(orders, norm, tokens, prev, dq, dk, dv, pk, pv, *refs):
    count = len(orders)
    outs = refs[:count]
    made, held, acc, sem = refs[count:]
    parts = [made.at[p] for p in range(count)]
    deltas = ((dq, None), (dk, pk), (dv, pv))
    stages = len(orders[0])
    whole = outs[0].shape[0]
    greet(orders[0])

    def make(p, start):
        own, other = deltas[p]
        right = own[...] if other is None else jnp.concatenate([own[...], other[...]], axis=0)

        def one(c, _):
            cut = pl.ds(pl.multiple_of(start * 8 + c * 128, 128), 128)
            left = tokens[:, cut]
            if other is not None:
                left = jnp.concatenate([left, prev[:, cut]], axis=0)
            block = dot(left, right, ROWS) * norm
            made[p, pl.ds(start + c * 16, 16)] = block.reshape(16, 8, -1).astype(BF16)
            return 0

        lax.fori_loop(0, whole // 32, one, 0)

    low = [[0] for _ in orders]

    def halves(p, i):
        half = whole >> (i + 1)
        mine = bit_of(orders[p][i])
        keep = low[p][i] + mine * half
        give = low[p][i] + (1 - mine) * half
        return half, keep, give

    def copy(src, dst, p, i, slot):
        return pltpu.make_async_remote_copy(
            src_ref=src, dst_ref=dst, send_sem=sem.at[0, p, slot], recv_sem=sem.at[1, p, slot],
            device_id=partner_of(orders[p][i]), device_id_type=MESH,
        )

    def scatter(p, i):
        half, keep, give = halves(p, i)
        source = parts[p] if i == 0 else acc.at[p]
        place = whole - 2 * half
        return copy(source.at[pl.ds(give, half)], held.at[p, pl.ds(place, half)], p, i, i)

    def gather(p, i):
        half, keep, _ = halves(p, i)
        block = outs[p].at[pl.ds(keep, half)]
        return copy(block, block, p, i, stages + i)

    going = []
    for p in range(count):
        make(p, halves(p, 0)[2])
        going.append(scatter(p, 0))
        going[p].start()
    for p in range(count):
        make(p, halves(p, 0)[1])
    for i in range(stages):
        for p in range(count):
            going[p].wait()
            half, keep, _ = halves(p, i)
            source = parts[p] if i == 0 else acc.at[p]
            target = acc.at[p] if i + 1 < stages else outs[p]
            place = whole - 2 * half
            step = min(half, 8)

            def add(c, _):
                at = pl.ds(keep + c * step, step)
                target[at] = source[at] + held[p, pl.ds(place + c * step, step)]
                return 0

            lax.fori_loop(0, half // step, add, 0)
            low[p].append(keep)
            going[p] = scatter(p, i + 1) if i + 1 < stages else gather(p, i)
            going[p].start()
    for i in reversed(range(stages)):
        for p in range(count):
            going[p].wait()
            if i:
                going[p] = gather(p, i - 1)
                going[p].start()


def reduce_grads(norm, operands, sizes):
    group, span = bits_of("group", sizes[0]), bits_of("span", sizes[1])
    rest = group[1:] + span
    turns = [rest[k:3] + rest[:k] + rest[3:] for k in range(3)]
    orders = [group[:1] + turn for turn in turns]
    rows = width = operands[0].shape[1]
    deep = (rows // 8, 8, width)
    vmem = pl.BlockSpec(memory_space=pltpu.VMEM)
    stages = len(orders[0])
    outs = pl.pallas_call(
        functools.partial(reduce_kernel, orders, norm),
        in_specs=[vmem] * len(operands),
        out_specs=[vmem] * 3,
        out_shape=[jax.ShapeDtypeStruct(deep, BF16)] * 3,
        scratch_shapes=[
            pltpu.VMEM((3, *deep), BF16),
            pltpu.VMEM((3, *deep), BF16),
            pltpu.VMEM((3, *deep), BF16),
            pltpu.SemaphoreType.DMA((2, 3, 2 * stages)),
        ],
        compiler_params=pltpu.CompilerParams(
            collective_id=1, has_side_effects=True, vmem_limit_bytes=40 * 2**20
        ),
        cost_estimate=pl.CostEstimate(flops=10**9, bytes_accessed=10**8, transcendentals=0),
    )(*operands)
    return [out.reshape(rows, width) for out in outs]


def solution(mesh):
    return jax.shard_map(
        shards,
        mesh=mesh,
        in_specs=(
            P(AXES, None),
            P(),
            P(),
            P(),
            P(None, AXES),
            P(AXES, None),
            P(AXES, None),
        ),
        out_specs=(P(AXES, None), P(AXES, None), P(), P(), P()),
        check_vma=False,
    )
```

```python
import functools
import math

import jax
import jax.numpy as jnp
from jax import lax
from jax.experimental import pallas as pl
from jax.experimental.pallas import tpu as pltpu
from jax.sharding import PartitionSpec as P

AXES = ("group", "span")
F32 = jnp.float32
BF16 = jnp.bfloat16
ROWS = (((0,), (0,)), ((), ()))
MESH = pl.DeviceIdType.MESH
COLS = (((1,), (1,)), ((), ()))


def shifted(block, axis, distance):
    devices = range(lax.axis_size(axis))
    route = [(i - distance, i) for i in devices if i - distance in devices]
    return lax.ppermute(block, axis, route)


def dot(a, b, dims=(((1,), (0,)), ((), ()))):
    return lax.dot_general(a, b, dims, preferred_element_type=F32)


def summary_kernel(lin_scale, size, q, k, v, g, col, out):
    heads = q.shape[1] // size
    states, grads = [], []
    for j in range(heads):
        cut = slice(j * size, (j + 1) * size)
        run = col[0, :, j : j + 1]
        fading = jnp.exp(run[run.shape[0] - 1 :, :] - run)
        weighted = (v[:, cut].astype(F32) * fading).astype(BF16)
        scaled = (g[:, cut].astype(F32) * jnp.exp(run)).astype(BF16)
        states.append(dot(k[:, cut], weighted, ROWS))
        grads.append(lin_scale * dot(q[:, cut], scaled, ROWS))
    out[:size, :] = jnp.concatenate(states, axis=1).astype(BF16)
    out[size:, :] = jnp.concatenate(grads, axis=1).astype(BF16)


def near_pair(lin_scale, soft_scale, size, q, k, v, g, pk, pv, col, row, times):
    rows = q.shape[0]
    heads = q.shape[1] // size
    t = lax.broadcasted_iota(jnp.int32, (rows, rows), 0)
    s = lax.broadcasted_iota(jnp.int32, (rows, rows), 1)
    lower = t >= s
    outs, dqs, dkv, dvv = [], [], [], []
    for j in range(heads):
        cut = slice(j * size, (j + 1) * size)
        qh, gh = q[:, cut], g[:, cut]
        kh = jnp.concatenate([k[:, cut], pk[:, cut]], axis=0)
        vh = jnp.concatenate([v[:, cut], pv[:, cut]], axis=0)
        decay = jnp.where(
            lower, jnp.exp(jnp.minimum(col[:, j : j + 1] - row[j : j + 1, :], 0.0)), 0.0
        ) * lin_scale
        score = dot(qh, kh, COLS)
        grad = dot(gh, vh, COLS)
        logits = jnp.where(times > 0.0, score * soft_scale, -1e30)
        peak = jnp.max(logits, axis=1, keepdims=True)
        terms = jnp.exp(logits - peak) * times
        probs = terms / jnp.sum(terms, axis=1, keepdims=True)
        inner = jnp.sum(probs * grad, axis=1, keepdims=True)
        dlogit = probs * (grad - inner) * soft_scale
        mix = jnp.concatenate(
            [probs[:, :rows] + score[:, :rows] * decay, probs[:, rows:]], axis=1
        ).astype(BF16)
        dmix = jnp.concatenate(
            [dlogit[:, :rows] + grad[:, :rows] * decay, dlogit[:, rows:]], axis=1
        ).astype(BF16)
        outs.append(dot(mix, vh))
        dqs.append(dot(dmix, kh))
        dkv.append(dot(dmix, qh, ROWS))
        dvv.append(dot(mix, gh, ROWS))
    dk = jnp.concatenate(dkv, axis=1)
    dv = jnp.concatenate(dvv, axis=1)
    return (
        jnp.concatenate(outs, axis=1),
        jnp.concatenate(dqs, axis=1),
        dk[:rows],
        dv[:rows],
        dk[rows:].astype(BF16),
        dv[rows:].astype(BF16),
    )


def state_kernel(
    lin_scale, size, q, k, v, g, col, carry, out, dq, own_k, own_v,
    layer, delta, grad_k, grad_v,
):
    heads = q.shape[1] // size
    state, later = carry[:size, :], carry[size:, :]
    outs, dqs, dks, dvs = [], [], [], []
    for j in range(heads):
        cut = slice(j * size, (j + 1) * size)
        run = col[0, :, j : j + 1]
        growth = lin_scale * jnp.exp(run)
        fading = jnp.exp(run[run.shape[0] - 1 :, :] - run)
        st, lt = state[:, cut], later[:, cut]
        outs.append(growth * dot(q[:, cut], st))
        dqs.append(growth * dot(g[:, cut], st, COLS))
        dks.append(fading * dot(v[:, cut], lt, COLS))
        dvs.append(fading * dot(k[:, cut], lt))
    layer[...] = (out[...] + jnp.concatenate(outs, axis=1)).astype(BF16)
    delta[...] = (dq[...] + jnp.concatenate(dqs, axis=1)).astype(BF16)
    grad_k[...] = (own_k[...] + jnp.concatenate(dks, axis=1)).astype(BF16)
    grad_v[...] = (own_v[...] + jnp.concatenate(dvs, axis=1)).astype(BF16)


def attention_parts(row_count, feat_width, head_count):
    size = feat_width // head_count
    pair = 256 // size
    steps = head_count // pair
    lanes = pair * size
    wide = pl.BlockSpec((row_count, lanes), lambda i: (0, i))
    col = pl.BlockSpec((1, row_count, pair), lambda i: (i, 0, 0))
    row = pl.BlockSpec((1, pair, row_count), lambda i: (i, 0, 0))
    return size, pair, steps, lanes, wide, col, row


def project(inputs, weight):
    return dot(inputs, weight).astype(BF16)


def shards(tokens, query_weight, key_weight, value_weight, log_decay, neighbour_blocks, cotangent):
    row_count, feat_width = tokens.shape
    head_count = log_decay.shape[0]
    size, pair, steps, lanes, wide, col_spec, row_spec = attention_parts(
        row_count, feat_width, head_count
    )
    lin_scale = 1.0 / (size * math.sqrt(row_count))
    soft_scale = 1.0 / math.sqrt(size)
    sizes = tuple(lax.axis_size(name) for name in AXES)
    devices = sizes[0] * sizes[1]
    position = lax.axis_index(AXES)
    shape = lambda dtype: jax.ShapeDtypeStruct((row_count, feat_width), dtype)

    prev_tokens = shifted(tokens, AXES, 1)
    places = jnp.arange(row_count)
    upto = (places[:, None] <= places[None, :]).astype(F32)
    running = jnp.dot(log_decay, upto, precision=lax.Precision.HIGHEST)
    row = running.reshape(steps, pair, row_count)
    col = row.transpose(0, 2, 1)
    query = project(tokens, query_weight)
    key = project(tokens, key_weight)
    value = project(tokens, value_weight)

    summary = pl.pallas_call(
        functools.partial(summary_kernel, lin_scale, size),
        grid=(steps,),
        in_specs=[wide] * 4 + [col_spec],
        out_specs=pl.BlockSpec((2 * size, lanes), lambda i: (0, i)),
        out_shape=jax.ShapeDtypeStruct((2 * size, feat_width), BF16),
        cost_estimate=pl.CostEstimate(flops=10**8, bytes_accessed=10**6, transcendentals=0),
    )(query, key, value, cotangent, col)
    total = jnp.repeat(lax.all_gather(running[:, -1], AXES), size, axis=1)

    prev_key = project(prev_tokens, key_weight)
    prev_value = project(prev_tokens, value_weight)
    own_times = jnp.sum(neighbour_blocks == position).astype(F32)
    prev_times = jnp.sum(neighbour_blocks == position - 1).astype(F32)
    times = jnp.where(jnp.arange(2 * row_count) < row_count, own_times, prev_times)[None, :]
    near = functools.partial(near_pair, lin_scale, soft_scale, size)
    operands = (query, key, value, cotangent, prev_key, prev_value, col, row, times)
    carry, out, dq, own_k, own_v, prev_gk, prev_gv = carried(near, summary, total, operands, sizes)

    owed = dot(prev_gk, key_weight, COLS) + dot(prev_gv, value_weight, COLS)
    owed = shifted(owed.astype(BF16), AXES, -1)

    layer_out, query_delta, grad_k, grad_v = pl.pallas_call(
        functools.partial(state_kernel, lin_scale, size),
        grid=(steps,),
        in_specs=[wide] * 4
        + [col_spec, pl.BlockSpec((2 * size, lanes), lambda i: (0, i))]
        + [wide] * 4,
        out_specs=[wide] * 4,
        out_shape=[shape(BF16)] * 4,
        cost_estimate=pl.CostEstimate(flops=10**9, bytes_accessed=10**7, transcendentals=0),
    )(query, key, value, cotangent, col, carry, out, dq, own_k, own_v)

    grad_norm = 1.0 / math.sqrt(row_count * devices)
    grads = reduce_grads(
        grad_norm,
        (tokens, prev_tokens, query_delta, grad_k, grad_v, prev_gk, prev_gv),
        sizes,
    )
    tokens_back = dot(query_delta, query_weight, COLS)
    tokens_back = tokens_back + dot(grad_k, key_weight, COLS) + dot(grad_v, value_weight, COLS)
    tokens_back = tokens_back + owed.astype(F32)
    return (layer_out, tokens_back.astype(BF16), *grads)


def bits_of(axis, size):
    return [(axis, k) for k in range(size.bit_length() - 1)]


def bit_of(bit):
    return (lax.axis_index(bit[0]) // 2 ** bit[1]) % 2


def partner_of(bit):
    place = {name: lax.axis_index(name) for name in AXES}
    place[bit[0]] = place[bit[0]] + (1 - 2 * bit_of(bit)) * 2 ** bit[1]
    return place


def greet(bits):
    barrier = pltpu.get_barrier_semaphore()
    for bit in bits:
        pl.semaphore_signal(barrier, inc=1, device_id=partner_of(bit), device_id_type=MESH)
    pl.semaphore_wait(barrier, len(bits))


def spot_of(index, span):
    return (index // span, lax.rem(index, span))


def greet_all(count, me, span):
    barrier = pltpu.get_barrier_semaphore()

    def one(i, _):
        pl.semaphore_signal(
            barrier, inc=1, device_id=spot_of(lax.rem(me + i, count), span), device_id_type=MESH
        )
        return 0

    lax.fori_loop(1, count, one, 0)
    pl.semaphore_wait(barrier, count - 1)


def carry_kernel(sizes, near, size, x, totals, *refs):
    ins, col, row, count = refs[:6], refs[6], refs[7], refs[8]
    carry, results = refs[9], refs[10:16]
    came, made, decay, sem, back_sem = refs[16:]
    steps, _, pair = col.shape
    lanes = pair * size
    devices, span = sizes[0] * sizes[1], sizes[1]
    me = lax.axis_index("group") * span + lax.axis_index("span")
    tile, blocks = came.shape[1], back_sem.shape[1]
    width = came.shape[2]
    across = x.shape[0] // tile
    mine = lax.rem(me, blocks)
    base = me - mine

    def near_step(i, _):
        cut = pl.ds(pl.multiple_of(i * lanes, lanes), lanes)
        values = near(*(ref[:, cut] for ref in ins), col[i], row[i], count[...])
        for ref, value in zip(results, values):
            ref[:, cut] = value
        return 0

    def part(block):
        down = pl.ds(pl.multiple_of(lax.rem(block, across) * tile, tile), tile)
        along = pl.ds(pl.multiple_of(block // across * width, width), width)
        return down, along

    def outward(i):
        there = lax.rem(me + i, devices)
        return pltpu.make_async_remote_copy(
            src_ref=x.at[part(lax.rem(there, blocks))], dst_ref=came.at[me],
            send_sem=sem.at[0, there], recv_sem=sem.at[1, me],
            device_id=spot_of(there, span), device_id_type=MESH,
        )

    def inward(i):
        there = lax.rem(me + devices - i, devices)
        return pltpu.make_async_remote_copy(
            src_ref=x.at[part(mine)], dst_ref=came.at[there],
            send_sem=sem.at[0, there], recv_sem=sem.at[1, there],
            device_id=spot_of(there, span), device_id_type=MESH,
        )

    def outward_back(i):
        there = lax.rem(mine + i, blocks)
        return pltpu.make_async_remote_copy(
            src_ref=made.at[base + there], dst_ref=carry.at[part(mine)],
            send_sem=back_sem.at[0, there], recv_sem=back_sem.at[1, mine],
            device_id=spot_of(base + there, span), device_id_type=MESH,
        )

    def inward_back(i):
        there = lax.rem(mine + blocks - i, blocks)
        return pltpu.make_async_remote_copy(
            src_ref=made.at[base + there], dst_ref=carry.at[part(there)],
            send_sem=back_sem.at[0, there], recv_sem=back_sem.at[1, there],
            device_id=spot_of(base + there, span), device_id_type=MESH,
        )

    def each(stop, act):
        def one(i, _):
            act(i)
            return 0

        lax.fori_loop(1, stop, one, 0)

    greet_all(devices, me, span)
    each(devices, lambda i: outward(i).start())
    came[me] = x[part(mine)]
    decay[...] = jnp.exp(totals[:, part(mine)[1]])
    lax.fori_loop(0, steps // 2, near_step, 0)
    each(devices, lambda i: inward(i).wait_recv())
    back = (lax.rem(mine, across) * tile) // (x.shape[0] // 2)

    def scan(i, state):
        at = i + back * (devices - 1 - 2 * i)
        made[at] = state.astype(BF16)
        return decay[pl.ds(at, 1), :] * state + came[at].astype(F32)

    lax.fori_loop(0, devices, scan, jnp.zeros((tile, width), F32))
    each(blocks, lambda i: outward_back(i).start())
    carry[part(mine)] = made[me]
    lax.fori_loop(steps // 2, steps, near_step, 0)
    each(blocks, lambda i: inward_back(i).wait_recv())
    each(devices, lambda i: outward(i).wait_send())
    each(blocks, lambda i: outward_back(i).wait_send())


def carried(near, summary, totals, operands, sizes):
    rows, width = summary.shape
    devices = sizes[0] * sizes[1]
    tile = 16
    blocks = min(devices, rows // tile * (width // 128))
    part = width // (blocks // (rows // tile))
    vmem = pl.BlockSpec(memory_space=pltpu.VMEM)
    return pl.pallas_call(
        functools.partial(carry_kernel, sizes, near, rows // 2),
        in_specs=[vmem] * (2 + len(operands)),
        out_specs=[vmem] * 7,
        out_shape=[jax.ShapeDtypeStruct((rows, width), BF16)]
        + [jax.ShapeDtypeStruct(operands[0].shape, F32)] * 4
        + [jax.ShapeDtypeStruct(operands[0].shape, BF16)] * 2,
        scratch_shapes=[
            pltpu.VMEM((devices, tile, part), BF16),
            pltpu.VMEM((devices, tile, part), BF16),
            pltpu.VMEM((devices, part), F32),
            pltpu.SemaphoreType.DMA((2, devices)),
            pltpu.SemaphoreType.DMA((2, blocks)),
        ],
        compiler_params=pltpu.CompilerParams(
            collective_id=0, has_side_effects=True, vmem_limit_bytes=40 * 2**20
        ),
        cost_estimate=pl.CostEstimate(flops=10**9, bytes_accessed=10**8, transcendentals=0),
    )(summary, totals, *operands)


def reduce_kernel(orders, norm, tokens, prev, dq, dk, dv, pk, pv, *refs):
    count = len(orders)
    outs = refs[:count]
    made, held, acc, sem = refs[count:]
    parts = [made.at[p] for p in range(count)]
    deltas = ((dq, None), (dk, pk), (dv, pv))
    stages = len(orders[0])
    whole = outs[0].shape[0]
    greet(orders[0])

    def make(p, start):
        own, other = deltas[p]
        right = own[...] if other is None else jnp.concatenate([own[...], other[...]], axis=0)

        def one(c, _):
            cut = pl.ds(pl.multiple_of(start * 8 + c * 128, 128), 128)
            left = tokens[:, cut]
            if other is not None:
                left = jnp.concatenate([left, prev[:, cut]], axis=0)
            block = dot(left, right, ROWS) * norm
            made[p, pl.ds(start + c * 16, 16)] = block.reshape(16, 8, -1).astype(BF16)
            return 0

        lax.fori_loop(0, whole // 32, one, 0)

    low = [[0] for _ in orders]

    def halves(p, i):
        half = whole >> (i + 1)
        mine = bit_of(orders[p][i])
        keep = low[p][i] + mine * half
        give = low[p][i] + (1 - mine) * half
        return half, keep, give

    def copy(src, dst, p, i, slot):
        return pltpu.make_async_remote_copy(
            src_ref=src, dst_ref=dst, send_sem=sem.at[0, p, slot], recv_sem=sem.at[1, p, slot],
            device_id=partner_of(orders[p][i]), device_id_type=MESH,
        )

    def scatter(p, i):
        half, keep, give = halves(p, i)
        source = parts[p] if i == 0 else acc.at[p]
        place = whole - 2 * half
        return copy(source.at[pl.ds(give, half)], held.at[p, pl.ds(place, half)], p, i, i)

    def gather(p, i):
        half, keep, _ = halves(p, i)
        block = outs[p].at[pl.ds(keep, half)]
        return copy(block, block, p, i, stages + i)

    going = []
    for p in range(count):
        make(p, halves(p, 0)[2])
        going.append(scatter(p, 0))
        going[p].start()
    for p in range(count):
        make(p, halves(p, 0)[1])
    for i in range(stages):
        for p in range(count):
            going[p].wait()
            half, keep, _ = halves(p, i)
            source = parts[p] if i == 0 else acc.at[p]
            target = acc.at[p] if i + 1 < stages else outs[p]
            place = whole - 2 * half
            step = min(half, 8)

            def add(c, _):
                at = pl.ds(keep + c * step, step)
                target[at] = source[at] + held[p, pl.ds(place + c * step, step)]
                return 0

            lax.fori_loop(0, half // step, add, 0)
            low[p].append(keep)
            going[p] = scatter(p, i + 1) if i + 1 < stages else gather(p, i)
            going[p].start()
    for i in reversed(range(stages)):
        for p in range(count):
            going[p].wait()
            if i:
                going[p] = gather(p, i - 1)
                going[p].start()


def reduce_grads(norm, operands, sizes):
    group, span = bits_of("group", sizes[0]), bits_of("span", sizes[1])
    rest = group[1:] + span
    turns = [rest[k:3] + rest[:k] + rest[3:] for k in range(3)]
    orders = [group[:1] + turn for turn in turns]
    rows = width = operands[0].shape[1]
    deep = (rows // 8, 8, width)
    vmem = pl.BlockSpec(memory_space=pltpu.VMEM)
    stages = len(orders[0])
    outs = pl.pallas_call(
        functools.partial(reduce_kernel, orders, norm),
        in_specs=[vmem] * len(operands),
        out_specs=[vmem] * 3,
        out_shape=[jax.ShapeDtypeStruct(deep, BF16)] * 3,
        scratch_shapes=[
            pltpu.VMEM((3, *deep), BF16),
            pltpu.VMEM((3, *deep), BF16),
            pltpu.VMEM((3, *deep), BF16),
            pltpu.SemaphoreType.DMA((2, 3, 2 * stages)),
        ],
        compiler_params=pltpu.CompilerParams(
            collective_id=1, has_side_effects=True, vmem_limit_bytes=40 * 2**20
        ),
        cost_estimate=pl.CostEstimate(flops=10**9, bytes_accessed=10**8, transcendentals=0),
    )(*operands)
    return [out.reshape(rows, width) for out in outs]


def solution(mesh):
    return jax.shard_map(
        shards,
        mesh=mesh,
        in_specs=(
            P(AXES, None),
            P(),
            P(),
            P(),
            P(None, AXES),
            P(AXES, None),
            P(AXES, None),
        ),
        out_specs=(P(AXES, None), P(AXES, None), P(), P(), P()),
        check_vma=False,
    )
```

```python
import functools
import math

import jax
import jax.numpy as jnp
from jax import lax
from jax.experimental import pallas as pl
from jax.experimental.pallas import tpu as pltpu
from jax.sharding import PartitionSpec as P

AXES = ("group", "span")
F32 = jnp.float32
BF16 = jnp.bfloat16
ROWS = (((0,), (0,)), ((), ()))
MESH = pl.DeviceIdType.MESH
COLS = (((1,), (1,)), ((), ()))


def shifted(block, axis, distance):
    devices = range(lax.axis_size(axis))
    route = [(i - distance, i) for i in devices if i - distance in devices]
    return lax.ppermute(block, axis, route)


def dot(a, b, dims=(((1,), (0,)), ((), ()))):
    return lax.dot_general(a, b, dims, preferred_element_type=F32)


def summary_kernel(lin_scale, size, q, k, v, g, col, out):
    heads = q.shape[1] // size
    states, grads = [], []
    for j in range(heads):
        cut = slice(j * size, (j + 1) * size)
        run = col[0, :, j : j + 1]
        fading = jnp.exp(run[run.shape[0] - 1 :, :] - run)
        weighted = (v[:, cut].astype(F32) * fading).astype(BF16)
        scaled = (g[:, cut].astype(F32) * jnp.exp(run)).astype(BF16)
        states.append(dot(k[:, cut], weighted, ROWS))
        grads.append(lin_scale * dot(q[:, cut], scaled, ROWS))
    out[:size, :] = jnp.concatenate(states, axis=1).astype(BF16)
    out[size:, :] = jnp.concatenate(grads, axis=1).astype(BF16)


def near_pair(lin_scale, soft_scale, size, q, k, v, g, pk, pv, col, row, times):
    rows = q.shape[0]
    heads = q.shape[1] // size
    t = lax.broadcasted_iota(jnp.int32, (rows, rows), 0)
    s = lax.broadcasted_iota(jnp.int32, (rows, rows), 1)
    lower = t >= s
    outs, dqs, dkv, dvv = [], [], [], []
    for j in range(heads):
        cut = slice(j * size, (j + 1) * size)
        qh, gh = q[:, cut], g[:, cut]
        kh = jnp.concatenate([k[:, cut], pk[:, cut]], axis=0)
        vh = jnp.concatenate([v[:, cut], pv[:, cut]], axis=0)
        decay = jnp.where(
            lower, jnp.exp(jnp.minimum(col[:, j : j + 1] - row[j : j + 1, :], 0.0)), 0.0
        ) * lin_scale
        score = dot(qh, kh, COLS)
        grad = dot(gh, vh, COLS)
        logits = jnp.where(times > 0.0, score * soft_scale, -1e30)
        peak = jnp.max(logits, axis=1, keepdims=True)
        terms = jnp.exp(logits - peak) * times
        probs = terms / jnp.sum(terms, axis=1, keepdims=True)
        inner = jnp.sum(probs * grad, axis=1, keepdims=True)
        dlogit = probs * (grad - inner) * soft_scale
        mix = jnp.concatenate(
            [probs[:, :rows] + score[:, :rows] * decay, probs[:, rows:]], axis=1
        ).astype(BF16)
        dmix = jnp.concatenate(
            [dlogit[:, :rows] + grad[:, :rows] * decay, dlogit[:, rows:]], axis=1
        ).astype(BF16)
        outs.append(dot(mix, vh))
        dqs.append(dot(dmix, kh))
        dkv.append(dot(dmix, qh, ROWS))
        dvv.append(dot(mix, gh, ROWS))
    dk = jnp.concatenate(dkv, axis=1)
    dv = jnp.concatenate(dvv, axis=1)
    return (
        jnp.concatenate(outs, axis=1),
        jnp.concatenate(dqs, axis=1),
        dk[:rows],
        dv[:rows],
        dk[rows:].astype(BF16),
        dv[rows:].astype(BF16),
    )


def state_kernel(
    lin_scale, size, q, k, v, g, col, carry, out, dq, own_k, own_v,
    layer, delta, grad_k, grad_v,
):
    heads = q.shape[1] // size
    state, later = carry[:size, :], carry[size:, :]
    outs, dqs, dks, dvs = [], [], [], []
    for j in range(heads):
        cut = slice(j * size, (j + 1) * size)
        run = col[0, :, j : j + 1]
        growth = lin_scale * jnp.exp(run)
        fading = jnp.exp(run[run.shape[0] - 1 :, :] - run)
        st, lt = state[:, cut], later[:, cut]
        outs.append(growth * dot(q[:, cut], st))
        dqs.append(growth * dot(g[:, cut], st, COLS))
        dks.append(fading * dot(v[:, cut], lt, COLS))
        dvs.append(fading * dot(k[:, cut], lt))
    layer[...] = (out[...] + jnp.concatenate(outs, axis=1)).astype(BF16)
    delta[...] = (dq[...] + jnp.concatenate(dqs, axis=1)).astype(BF16)
    grad_k[...] = (own_k[...] + jnp.concatenate(dks, axis=1)).astype(BF16)
    grad_v[...] = (own_v[...] + jnp.concatenate(dvs, axis=1)).astype(BF16)


def attention_parts(row_count, feat_width, head_count):
    size = feat_width // head_count
    pair = 256 // size
    steps = head_count // pair
    lanes = pair * size
    wide = pl.BlockSpec((row_count, lanes), lambda i: (0, i))
    col = pl.BlockSpec((1, row_count, pair), lambda i: (i, 0, 0))
    row = pl.BlockSpec((1, pair, row_count), lambda i: (i, 0, 0))
    return size, pair, steps, lanes, wide, col, row


def project(inputs, weight):
    return dot(inputs, weight).astype(BF16)


def shards(tokens, query_weight, key_weight, value_weight, log_decay, neighbour_blocks, cotangent):
    row_count, feat_width = tokens.shape
    head_count = log_decay.shape[0]
    size, pair, steps, lanes, wide, col_spec, row_spec = attention_parts(
        row_count, feat_width, head_count
    )
    lin_scale = 1.0 / (size * math.sqrt(row_count))
    soft_scale = 1.0 / math.sqrt(size)
    sizes = tuple(lax.axis_size(name) for name in AXES)
    devices = sizes[0] * sizes[1]
    position = lax.axis_index(AXES)
    shape = lambda dtype: jax.ShapeDtypeStruct((row_count, feat_width), dtype)

    prev_tokens = shifted(tokens, AXES, 1)
    places = jnp.arange(row_count)
    upto = (places[:, None] <= places[None, :]).astype(F32)
    running = jnp.dot(log_decay, upto, precision=lax.Precision.HIGHEST)
    row = running.reshape(steps, pair, row_count)
    col = row.transpose(0, 2, 1)
    query = project(tokens, query_weight)
    key = project(tokens, key_weight)
    value = project(tokens, value_weight)

    summary = pl.pallas_call(
        functools.partial(summary_kernel, lin_scale, size),
        grid=(steps,),
        in_specs=[wide] * 4 + [col_spec],
        out_specs=pl.BlockSpec((2 * size, lanes), lambda i: (0, i)),
        out_shape=jax.ShapeDtypeStruct((2 * size, feat_width), BF16),
        cost_estimate=pl.CostEstimate(flops=10**8, bytes_accessed=10**6, transcendentals=0),
    )(query, key, value, cotangent, col)
    total = jnp.broadcast_to(jnp.repeat(running[:, -1], size)[None, :], (8, feat_width))

    prev_key = project(prev_tokens, key_weight)
    prev_value = project(prev_tokens, value_weight)
    own_times = jnp.sum(neighbour_blocks == position).astype(F32)
    prev_times = jnp.sum(neighbour_blocks == position - 1).astype(F32)
    times = jnp.where(jnp.arange(2 * row_count) < row_count, own_times, prev_times)[None, :]
    near = functools.partial(near_pair, lin_scale, soft_scale, size)
    operands = (query, key, value, cotangent, prev_key, prev_value, col, row, times)
    carry, out, dq, own_k, own_v, prev_gk, prev_gv = carried(near, summary, total, operands, sizes)

    owed = dot(prev_gk, key_weight, COLS) + dot(prev_gv, value_weight, COLS)
    owed = shifted(owed.astype(BF16), AXES, -1)

    layer_out, query_delta, grad_k, grad_v = pl.pallas_call(
        functools.partial(state_kernel, lin_scale, size),
        grid=(steps,),
        in_specs=[wide] * 4
        + [col_spec, pl.BlockSpec((2 * size, lanes), lambda i: (0, i))]
        + [wide] * 4,
        out_specs=[wide] * 4,
        out_shape=[shape(BF16)] * 4,
        cost_estimate=pl.CostEstimate(flops=10**9, bytes_accessed=10**7, transcendentals=0),
    )(query, key, value, cotangent, col, carry, out, dq, own_k, own_v)

    grad_norm = 1.0 / math.sqrt(row_count * devices)
    grads = reduce_grads(
        grad_norm,
        (tokens, prev_tokens, query_delta, grad_k, grad_v, prev_gk, prev_gv),
        sizes,
    )
    tokens_back = dot(query_delta, query_weight, COLS)
    tokens_back = tokens_back + dot(grad_k, key_weight, COLS) + dot(grad_v, value_weight, COLS)
    tokens_back = tokens_back + owed.astype(F32)
    return (layer_out, tokens_back.astype(BF16), *grads)


def bits_of(axis, size):
    return [(axis, k) for k in range(size.bit_length() - 1)]


def bit_of(bit):
    return (lax.axis_index(bit[0]) // 2 ** bit[1]) % 2


def partner_of(bit):
    place = {name: lax.axis_index(name) for name in AXES}
    place[bit[0]] = place[bit[0]] + (1 - 2 * bit_of(bit)) * 2 ** bit[1]
    return place


def greet(bits):
    barrier = pltpu.get_barrier_semaphore()
    for bit in bits:
        pl.semaphore_signal(barrier, inc=1, device_id=partner_of(bit), device_id_type=MESH)
    pl.semaphore_wait(barrier, len(bits))


def spot_of(index, span):
    return (index // span, lax.rem(index, span))


def greet_all(count, me, span):
    barrier = pltpu.get_barrier_semaphore()

    def one(i, _):
        pl.semaphore_signal(
            barrier, inc=1, device_id=spot_of(lax.rem(me + i, count), span), device_id_type=MESH
        )
        return 0

    lax.fori_loop(1, count, one, 0)
    pl.semaphore_wait(barrier, count - 1)


def carry_kernel(sizes, near, size, x, total, *refs):
    ins, col, row, count = refs[:6], refs[6], refs[7], refs[8]
    carry, results = refs[9], refs[10:16]
    came, made, decay, sem, sum_sem, back_sem = refs[16:]
    steps, _, pair = col.shape
    lanes = pair * size
    devices, span = sizes[0] * sizes[1], sizes[1]
    me = lax.axis_index("group") * span + lax.axis_index("span")
    tile, blocks = came.shape[1], back_sem.shape[1]
    width = came.shape[2]
    across = x.shape[0] // tile
    mine = lax.rem(me, blocks)
    base = me - mine

    def near_step(i, _):
        cut = pl.ds(pl.multiple_of(i * lanes, lanes), lanes)
        values = near(*(ref[:, cut] for ref in ins), col[i], row[i], count[...])
        for ref, value in zip(results, values):
            ref[:, cut] = value
        return 0

    def part(block):
        down = pl.ds(pl.multiple_of(lax.rem(block, across) * tile, tile), tile)
        along = pl.ds(pl.multiple_of(block // across * width, width), width)
        return down, along

    def outward(i):
        there = lax.rem(me + i, devices)
        return pltpu.make_async_remote_copy(
            src_ref=x.at[part(lax.rem(there, blocks))], dst_ref=came.at[me],
            send_sem=sem.at[0, there], recv_sem=sem.at[1, me],
            device_id=spot_of(there, span), device_id_type=MESH,
        )

    def inward(i):
        there = lax.rem(me + devices - i, devices)
        return pltpu.make_async_remote_copy(
            src_ref=x.at[part(mine)], dst_ref=came.at[there],
            send_sem=sem.at[0, there], recv_sem=sem.at[1, there],
            device_id=spot_of(there, span), device_id_type=MESH,
        )

    def sum_outward(i):
        there = lax.rem(me + i, devices)
        return pltpu.make_async_remote_copy(
            src_ref=total.at[:, part(lax.rem(there, blocks))[1]], dst_ref=decay.at[me],
            send_sem=sum_sem.at[0, there], recv_sem=sum_sem.at[1, me],
            device_id=spot_of(there, span), device_id_type=MESH,
        )

    def sum_inward(i):
        there = lax.rem(me + devices - i, devices)
        return pltpu.make_async_remote_copy(
            src_ref=total.at[:, part(mine)[1]], dst_ref=decay.at[there],
            send_sem=sum_sem.at[0, there], recv_sem=sum_sem.at[1, there],
            device_id=spot_of(there, span), device_id_type=MESH,
        )

    def outward_back(i):
        there = lax.rem(mine + i, blocks)
        return pltpu.make_async_remote_copy(
            src_ref=made.at[base + there], dst_ref=carry.at[part(mine)],
            send_sem=back_sem.at[0, there], recv_sem=back_sem.at[1, mine],
            device_id=spot_of(base + there, span), device_id_type=MESH,
        )

    def inward_back(i):
        there = lax.rem(mine + blocks - i, blocks)
        return pltpu.make_async_remote_copy(
            src_ref=made.at[base + there], dst_ref=carry.at[part(there)],
            send_sem=back_sem.at[0, there], recv_sem=back_sem.at[1, there],
            device_id=spot_of(base + there, span), device_id_type=MESH,
        )

    def each(stop, act):
        def one(i, _):
            act(i)
            return 0

        lax.fori_loop(1, stop, one, 0)

    greet_all(devices, me, span)
    each(devices, lambda i: sum_outward(i).start())
    each(devices, lambda i: outward(i).start())
    came[me] = x[part(mine)]
    decay[me] = total[:, part(mine)[1]]
    lax.fori_loop(0, steps // 2, near_step, 0)
    each(devices, lambda i: sum_inward(i).wait_recv())
    each(devices, lambda i: inward(i).wait_recv())
    back = (lax.rem(mine, across) * tile) // (x.shape[0] // 2)

    def scan(i, state):
        at = i + back * (devices - 1 - 2 * i)
        made[at] = state.astype(BF16)
        return jnp.exp(decay[at, :1, :]) * state + came[at].astype(F32)

    lax.fori_loop(0, devices, scan, jnp.zeros((tile, width), F32))
    each(blocks, lambda i: outward_back(i).start())
    carry[part(mine)] = made[me]
    lax.fori_loop(steps // 2, steps, near_step, 0)
    each(blocks, lambda i: inward_back(i).wait_recv())
    each(devices, lambda i: sum_outward(i).wait_send())
    each(devices, lambda i: outward(i).wait_send())
    each(blocks, lambda i: outward_back(i).wait_send())


def carried(near, summary, total, operands, sizes):
    rows, width = summary.shape
    devices = sizes[0] * sizes[1]
    tile = 16
    blocks = min(devices, rows // tile * (width // 128))
    part = width // (blocks // (rows // tile))
    vmem = pl.BlockSpec(memory_space=pltpu.VMEM)
    return pl.pallas_call(
        functools.partial(carry_kernel, sizes, near, rows // 2),
        in_specs=[vmem] * (2 + len(operands)),
        out_specs=[vmem] * 7,
        out_shape=[jax.ShapeDtypeStruct((rows, width), BF16)]
        + [jax.ShapeDtypeStruct(operands[0].shape, F32)] * 4
        + [jax.ShapeDtypeStruct(operands[0].shape, BF16)] * 2,
        scratch_shapes=[
            pltpu.VMEM((devices, tile, part), BF16),
            pltpu.VMEM((devices, tile, part), BF16),
            pltpu.VMEM((devices, 8, part), F32),
            pltpu.SemaphoreType.DMA((2, devices)),
            pltpu.SemaphoreType.DMA((2, devices)),
            pltpu.SemaphoreType.DMA((2, blocks)),
        ],
        compiler_params=pltpu.CompilerParams(
            collective_id=0, has_side_effects=True, vmem_limit_bytes=40 * 2**20
        ),
        cost_estimate=pl.CostEstimate(flops=10**9, bytes_accessed=10**8, transcendentals=0),
    )(summary, total, *operands)


def reduce_kernel(orders, norm, tokens, prev, dq, dk, dv, pk, pv, *refs):
    count = len(orders)
    outs = refs[:count]
    made, held, acc, sem = refs[count:]
    parts = [made.at[p] for p in range(count)]
    deltas = ((dq, None), (dk, pk), (dv, pv))
    stages = len(orders[0])
    whole = outs[0].shape[0]
    greet(orders[0])

    def make(p, start):
        own, other = deltas[p]
        right = own[...] if other is None else jnp.concatenate([own[...], other[...]], axis=0)

        def one(c, _):
            cut = pl.ds(pl.multiple_of(start * 8 + c * 128, 128), 128)
            left = tokens[:, cut]
            if other is not None:
                left = jnp.concatenate([left, prev[:, cut]], axis=0)
            block = dot(left, right, ROWS) * norm
            made[p, pl.ds(start + c * 16, 16)] = block.reshape(16, 8, -1).astype(BF16)
            return 0

        lax.fori_loop(0, whole // 32, one, 0)

    low = [[0] for _ in orders]

    def halves(p, i):
        half = whole >> (i + 1)
        mine = bit_of(orders[p][i])
        keep = low[p][i] + mine * half
        give = low[p][i] + (1 - mine) * half
        return half, keep, give

    def copy(src, dst, p, i, slot):
        return pltpu.make_async_remote_copy(
            src_ref=src, dst_ref=dst, send_sem=sem.at[0, p, slot], recv_sem=sem.at[1, p, slot],
            device_id=partner_of(orders[p][i]), device_id_type=MESH,
        )

    def scatter(p, i):
        half, keep, give = halves(p, i)
        source = parts[p] if i == 0 else acc.at[p]
        place = whole - 2 * half
        return copy(source.at[pl.ds(give, half)], held.at[p, pl.ds(place, half)], p, i, i)

    def gather(p, i):
        half, keep, _ = halves(p, i)
        block = outs[p].at[pl.ds(keep, half)]
        return copy(block, block, p, i, stages + i)

    going = []
    for p in range(count):
        make(p, halves(p, 0)[2])
        going.append(scatter(p, 0))
        going[p].start()
    for p in range(count):
        make(p, halves(p, 0)[1])
    for i in range(stages):
        for p in range(count):
            going[p].wait()
            half, keep, _ = halves(p, i)
            source = parts[p] if i == 0 else acc.at[p]
            target = acc.at[p] if i + 1 < stages else outs[p]
            place = whole - 2 * half
            step = min(half, 8)

            def add(c, _):
                at = pl.ds(keep + c * step, step)
                target[at] = source[at] + held[p, pl.ds(place + c * step, step)]
                return 0

            lax.fori_loop(0, half // step, add, 0)
            low[p].append(keep)
            going[p] = scatter(p, i + 1) if i + 1 < stages else gather(p, i)
            going[p].start()
    for i in reversed(range(stages)):
        for p in range(count):
            going[p].wait()
            if i:
                going[p] = gather(p, i - 1)
                going[p].start()


def reduce_grads(norm, operands, sizes):
    group, span = bits_of("group", sizes[0]), bits_of("span", sizes[1])
    rest = group[1:] + span
    turns = [rest[k:3] + rest[:k] + rest[3:] for k in range(3)]
    orders = [group[:1] + turn for turn in turns]
    rows = width = operands[0].shape[1]
    deep = (rows // 8, 8, width)
    vmem = pl.BlockSpec(memory_space=pltpu.VMEM)
    stages = len(orders[0])
    outs = pl.pallas_call(
        functools.partial(reduce_kernel, orders, norm),
        in_specs=[vmem] * len(operands),
        out_specs=[vmem] * 3,
        out_shape=[jax.ShapeDtypeStruct(deep, BF16)] * 3,
        scratch_shapes=[
            pltpu.VMEM((3, *deep), BF16),
            pltpu.VMEM((3, *deep), BF16),
            pltpu.VMEM((3, *deep), BF16),
            pltpu.SemaphoreType.DMA((2, 3, 2 * stages)),
        ],
        compiler_params=pltpu.CompilerParams(
            collective_id=1, has_side_effects=True, vmem_limit_bytes=40 * 2**20
        ),
        cost_estimate=pl.CostEstimate(flops=10**9, bytes_accessed=10**8, transcendentals=0),
    )(*operands)
    return [out.reshape(rows, width) for out in outs]


def solution(mesh):
    return jax.shard_map(
        shards,
        mesh=mesh,
        in_specs=(
            P(AXES, None),
            P(),
            P(),
            P(),
            P(None, AXES),
            P(AXES, None),
            P(AXES, None),
        ),
        out_specs=(P(AXES, None), P(AXES, None), P(), P(), P()),
        check_vma=False,
    )
```

```python
import functools
import math

import jax
import jax.numpy as jnp
from jax import lax
from jax.experimental import pallas as pl
from jax.experimental.pallas import tpu as pltpu
from jax.sharding import PartitionSpec as P

AXES = ("group", "span")
F32 = jnp.float32
BF16 = jnp.bfloat16
ROWS = (((0,), (0,)), ((), ()))
COLS = (((1,), (1,)), ((), ()))
MESH = pl.DeviceIdType.MESH
LANES = 128


def dot(a, b, dims=(((1,), (0,)), ((), ())), precision=None):
    return lax.dot_general(a, b, dims, precision=precision, preferred_element_type=F32)


def summary_of(lin_scale, size, q, k, v, g, col):
    heads = q.shape[1] // size
    states, grads = [], []
    for j in range(heads):
        cut = slice(j * size, (j + 1) * size)
        run = col[:, j : j + 1]
        fading = jnp.exp(run[run.shape[0] - 1 :, :] - run)
        weighted = (v[:, cut].astype(F32) * fading).astype(BF16)
        scaled = (g[:, cut].astype(F32) * jnp.exp(run)).astype(BF16)
        states.append(dot(k[:, cut], weighted, ROWS))
        grads.append(lin_scale * dot(q[:, cut], scaled, ROWS))
    return jnp.concatenate(
        [jnp.concatenate(states, axis=1), jnp.concatenate(grads, axis=1)], axis=0
    ).astype(BF16)


def near_pair(lin_scale, soft_scale, size, q, k, v, g, pk, pv, col, row, times):
    rows = q.shape[0]
    heads = q.shape[1] // size
    t = lax.broadcasted_iota(jnp.int32, (rows, rows), 0)
    s = lax.broadcasted_iota(jnp.int32, (rows, rows), 1)
    lower = t >= s
    outs, dqs, dkv, dvv = [], [], [], []
    for j in range(heads):
        cut = slice(j * size, (j + 1) * size)
        qh, gh = q[:, cut], g[:, cut]
        kh = jnp.concatenate([k[:, cut], pk[:, cut]], axis=0)
        vh = jnp.concatenate([v[:, cut], pv[:, cut]], axis=0)
        decay = jnp.where(
            lower, jnp.exp(jnp.minimum(col[:, j : j + 1] - row[j : j + 1, :], 0.0)), 0.0
        ) * lin_scale
        score = dot(qh, kh, COLS)
        grad = dot(gh, vh, COLS)
        logits = jnp.where(times > 0.0, score * soft_scale, -1e30)
        peak = jnp.max(logits, axis=1, keepdims=True)
        terms = jnp.exp(logits - peak) * times
        probs = terms / jnp.sum(terms, axis=1, keepdims=True)
        inner = jnp.sum(probs * grad, axis=1, keepdims=True)
        dlogit = probs * (grad - inner) * soft_scale
        mix = jnp.concatenate(
            [probs[:, :rows] + score[:, :rows] * decay, probs[:, rows:]], axis=1
        ).astype(BF16)
        dmix = jnp.concatenate(
            [dlogit[:, :rows] + grad[:, :rows] * decay, dlogit[:, rows:]], axis=1
        ).astype(BF16)
        outs.append(dot(mix, vh))
        dqs.append(dot(dmix, kh))
        dkv.append(dot(dmix, qh, ROWS))
        dvv.append(dot(mix, gh, ROWS))
    dk = jnp.concatenate(dkv, axis=1)
    dv = jnp.concatenate(dvv, axis=1)
    return (
        jnp.concatenate(outs, axis=1),
        jnp.concatenate(dqs, axis=1),
        dk[:rows],
        dv[:rows],
        jnp.concatenate([dk[rows:], dv[rows:]], axis=1).astype(BF16),
    )


def state_terms(lin_scale, size, q, k, v, g, col, state, later):
    heads = q.shape[1] // size
    outs, dqs, dks, dvs = [], [], [], []
    for j in range(heads):
        cut = slice(j * size, (j + 1) * size)
        run = col[:, j : j + 1]
        growth = lin_scale * jnp.exp(run)
        fading = jnp.exp(run[run.shape[0] - 1 :, :] - run)
        st, lt = state[:, cut], later[:, cut]
        outs.append(growth * dot(q[:, cut], st))
        dqs.append(growth * dot(g[:, cut], st, COLS))
        dks.append(fading * dot(v[:, cut], lt, COLS))
        dvs.append(fading * dot(k[:, cut], lt))
    return [jnp.concatenate(terms, axis=1) for terms in (outs, dqs, dks, dvs)]


def span_of(start, step, length):
    return pl.ds(pl.multiple_of(start * step, step), length)


def layer_kernel(
    sizes, size, norm,
    tokens, g, times, rates, wq, wk, wv,
    layer, back, grads,
    w, q, k, v, prev, local, total, col, row,
    came, decay, made, carry, out, dq, own_k, own_v, owe, due, delta, packed,
    spread, gathered, part, parts_in,
    w_sem, prev_sem, carry_sem, owe_sem, token_sem, delta_sem, part_sem, arrive, sent,
):
    rows, width = tokens.shape
    steps, _, pair = col.shape
    lanes = pair * size
    devices, span = sizes[0] * sizes[1], sizes[1]
    group_at, span_at = lax.axis_index("group"), lax.axis_index("span")
    me = group_at * span + span_at
    lin_scale = 1.0 / (size * math.sqrt(rows))
    soft_scale = 1.0 / math.sqrt(size)
    high = lax.Precision.HIGHEST

    def spot(index):
        return (index // span, lax.rem(index, span))

    def remote(src, dst, send, recv, where):
        return pltpu.make_async_remote_copy(
            src_ref=src, dst_ref=dst, send_sem=send, recv_sem=recv,
            device_id=where, device_id_type=MESH,
        )

    def each(start, stop, act):
        def one(i, _):
            act(i)
            return 0

        lax.fori_loop(start, stop, one, 0)

    weights = [
        pltpu.make_async_copy(src, w.at[m], w_sem.at[m]) for m, src in enumerate((wq, wk, wv))
    ]
    for copy in weights:
        copy.start()
    barrier = pltpu.get_barrier_semaphore()
    each(
        1, devices,
        lambda i: pl.semaphore_signal(
            barrier, inc=1, device_id=spot(lax.rem(me + i, devices)), device_id_type=MESH
        ),
    )
    down = lax.broadcasted_iota(jnp.int32, (rows, rows), 0)
    along = lax.broadcasted_iota(jnp.int32, (rows, rows), 1)
    rate = rates[...]
    by_row = dot(rate, (down <= along).astype(F32), precision=high)
    by_col = dot((down >= along).astype(F32), rate, COLS, precision=high)
    for i in range(steps):
        col[i] = by_col[:, i * pair : (i + 1) * pair]
        row[i] = by_row[i * pair : (i + 1) * pair, :]
    head = lax.broadcasted_iota(jnp.int32, (steps * pair, width), 0)
    lane = lax.broadcasted_iota(jnp.int32, (steps * pair, width), 1)
    ours = jnp.logical_and(lane >= head * size, lane < (head + 1) * size).astype(F32)
    last = jnp.broadcast_to(by_col[rows - 1 :, :], (8, steps * pair))
    total[...] = dot(last, ours, precision=high)
    pl.semaphore_wait(barrier, devices - 1)

    after = lax.rem(me + 1, devices)
    before = lax.rem(me + devices - 1, devices)
    tokens_on = remote(tokens, prev, prev_sem.at[0], prev_sem.at[1], spot(after))
    tokens_on.start()

    for copy in weights:
        copy.wait()

    def project(i):
        cut = span_of(i, lanes, lanes)
        left = tokens[...]
        q[:, cut] = dot(left, w[0, :, cut]).astype(BF16)
        k[:, cut] = dot(left, w[1, :, cut]).astype(BF16)
        v[:, cut] = dot(left, w[2, :, cut]).astype(BF16)
        local[:, cut] = summary_of(
            lin_scale, size, q[:, cut], k[:, cut], v[:, cut], g[:, cut], col[i]
        )

    each(0, steps, project)

    tile, wide = came.shape[1], came.shape[2]
    across = local.shape[0] // tile
    blocks = across * (width // wide)
    mine = lax.rem(me, blocks)
    base = me - mine

    def part_of(block):
        return span_of(lax.rem(block, across), tile, tile), span_of(block // across, wide, wide)

    one_row = pl.ds(0, 1)

    def send_states(i):
        there = lax.rem(me + i, devices)
        at = part_of(lax.rem(there, blocks))
        remote(
            total.at[one_row, at[1]], decay.at[me, one_row], carry_sem.at[0, 0],
            carry_sem.at[1, 0], spot(there),
        ).start()
        remote(
            local.at[at], came.at[me], carry_sem.at[0, 1], carry_sem.at[1, 1], spot(there)
        ).start()

    each(1, devices, send_states)
    others = pl.ds(0, devices - 1)
    all_sums = remote(
        decay.at[others, one_row], decay.at[others, one_row],
        carry_sem.at[0, 0], carry_sem.at[1, 0], spot(after),
    )
    all_states = remote(
        came.at[others], came.at[others], carry_sem.at[0, 1], carry_sem.at[1, 1], spot(after)
    )
    came[me] = local[part_of(mine)]
    decay[me] = total[:, part_of(mine)[1]]

    depth_at, x_at = span_at // 2, lax.rem(span_at, 2)
    depth = span // 2
    plane = 2 * sizes[0]
    here = group_at * 2 + x_at

    def plane_spot(c):
        return (c // 2, depth_at * 2 + lax.rem(c, 2))

    gathered[span_of(here, rows, rows), :] = tokens[...]

    def send_tokens(i):
        remote(
            tokens, gathered.at[span_of(here, rows, rows)], token_sem.at[0], token_sem.at[1],
            plane_spot(lax.rem(here + i, plane)),
        ).start()

    each(1, plane, send_tokens)
    others_here = pl.ds(0, (plane - 1) * rows)
    all_tokens = remote(
        gathered.at[others_here], gathered.at[others_here], token_sem.at[0], token_sem.at[1],
        spot(after),
    )

    tokens_on.wait()

    def owe_copy(i):
        return remote(owe.at[i], due.at[i], owe_sem.at[0, i], owe_sem.at[1, i], spot(before))

    def near(i):
        cut = span_of(i, lanes, lanes)
        pk = dot(prev[...], w[1, :, cut]).astype(BF16)
        pv = dot(prev[...], w[2, :, cut]).astype(BF16)
        values = near_pair(
            lin_scale, soft_scale, size, q[:, cut], k[:, cut], v[:, cut], g[:, cut], pk, pv,
            col[i], row[i], times[...],
        )
        for ref, value in zip((out, dq, own_k, own_v), values):
            ref[:, cut] = value
        owe[i] = values[4]
        owe_copy(i).start()

    each(0, steps // 2, near)

    all_sums.wait_recv()
    all_states.wait_recv()
    back_way = (lax.rem(mine, across) * tile) // size

    def scan(i, state):
        at = i + back_way * (devices - 1 - 2 * i)
        made[at] = state.astype(BF16)
        return jnp.exp(decay[at, :1, :]) * state + came[at].astype(F32)

    lax.fori_loop(0, devices, scan, jnp.zeros((tile, wide), F32))

    def send_carry(i):
        there = base + lax.rem(mine + i, blocks)
        remote(
            made.at[there], carry.at[part_of(mine)], carry_sem.at[0, 2], carry_sem.at[1, 2],
            spot(there),
        ).start()

    each(1, blocks, send_carry)
    other_blocks = pl.ds(0, blocks - 1)
    all_carry = remote(
        came.at[other_blocks], came.at[other_blocks], carry_sem.at[0, 2], carry_sem.at[1, 2],
        spot(after),
    )
    carry[part_of(mine)] = made[me]
    each(steps // 2, steps, near)
    all_carry.wait_recv()

    def delta_copy(c):
        return remote(
            packed.at[c], spread.at[span_of(here, rows, rows)], delta_sem.at[0],
            delta_sem.at[1], plane_spot(c),
        )

    def finish(n):
        i = lax.rem(n + here // 2, steps)
        cut = span_of(i, lanes, lanes)
        owe_copy(i).wait_recv()
        terms = state_terms(
            lin_scale, size, q[:, cut], k[:, cut], v[:, cut], g[:, cut], col[i],
            carry[:size, cut], carry[size:, cut],
        )
        layer[:, cut] = (out[:, cut] + terms[0]).astype(BF16)
        owed = due[i].astype(F32)
        deltas = [
            (dq[:, cut] + terms[1]).astype(BF16),
            (own_k[:, cut] + terms[2] + owed[:, :lanes]).astype(BF16),
            (own_v[:, cut] + terms[3] + owed[:, lanes:]).astype(BF16),
        ]
        for m in range(3):
            delta[m, :, cut] = deltas[m]
        for u in range(lanes // LANES):
            c = i * (lanes // LANES) + u
            for m in range(3):
                packed[c, :, m * LANES : (m + 1) * LANES] = deltas[m][:, u * LANES : (u + 1) * LANES]

            @pl.when(c != here)
            def _():
                delta_copy(c).start()

    each(0, steps, finish)
    spread[span_of(here, rows, rows), :] = packed[here]

    def token_back(i):
        cut = span_of(i, lanes, lanes)
        back[:, cut] = (
            dot(delta[0], w[0, cut, :], COLS)
            + dot(delta[1], w[1, cut, :], COLS)
            + dot(delta[2], w[2, cut, :], COLS)
        ).astype(BF16)

    each(0, width // lanes, token_back)

    all_tokens.wait_recv()
    all_deltas = remote(
        spread.at[others_here], spread.at[others_here], delta_sem.at[0], delta_sem.at[1],
        spot(after),
    )
    all_deltas.wait_recv()
    tall = width // depth
    in_block = max(1, lanes // tall)

    def depth_spot(d):
        return (group_at, d * 2 + x_at)

    def multiply(n):
        b = lax.rem(depth_at // in_block + n, width // lanes)
        cut = span_of(b, lanes, lanes)
        part[cut, :] = dot(gathered[:, cut], spread[...], ROWS).astype(BF16)
        for u in range(in_block):
            d = b * in_block + u

            @pl.when(d != depth_at)
            def _():
                remote(
                    part.at[span_of(d, tall, tall)], parts_in.at[depth_at], part_sem.at[0],
                    part_sem.at[1], depth_spot(d),
                ).start()

    each(1, width // lanes + 1, multiply)
    other_parts = pl.ds(0, depth - 1)
    all_parts = remote(
        parts_in.at[other_parts], parts_in.at[other_parts], part_sem.at[0], part_sem.at[1],
        spot(after),
    )
    all_parts.wait_recv()
    parts_in[depth_at] = part[span_of(depth_at, tall, tall), :]
    for m in range(3):
        cut = slice(m * LANES, (m + 1) * LANES)
        summed = lax.fori_loop(
            0, depth, lambda d, so_far: so_far + parts_in[d, :, cut].astype(F32),
            jnp.zeros((tall, LANES), F32),
        )
        grads[m, span_of(depth_at, tall, tall), span_of(here, LANES, LANES)] = (
            summed * norm
        ).astype(BF16)

    core_at, y_at = lax.rem(group_at, 2), group_at // 2
    half = tall // 2
    x_step, y_step, core_step = 1 - 2 * x_at, 4 * (1 - 2 * y_at), 2 * (1 - 2 * core_at)
    c_x, c_y = here + x_step, here + y_step
    c_xy = here + x_step + y_step
    x_spot = (group_at, span_at + x_step)
    y_spot = (group_at + 2 * (1 - 2 * y_at), span_at)
    core_spot = (group_at + 1 - 2 * core_at, span_at)
    first = ((x_spot, c_x), (y_spot, c_y))
    second = ((y_spot, (c_y, c_xy)), (x_spot, (c_x, c_xy)))

    def block(d, c, h):
        return grads.at[:, span_of(d * 2 + h, half, half), span_of(c, LANES, LANES)]

    def pass_on(d, c, h, leg, where):
        remote(block(d, c, h), block(d, c, h), sent.at[h, leg], arrive.at[h, d, c], where).start()

    def landed(d, c, h):
        remote(
            block(d, c, h), block(d, c, h), sent.at[h, 0], arrive.at[h, d, c], spot(after)
        ).wait_recv()

    def along_depth(i):
        d = lax.rem(depth_at + i, depth)
        for h in range(2):
            pass_on(depth_at, here, h, 0, depth_spot(d))

    each(1, depth, along_depth)

    def last_leg(d):
        for h in range(2):
            for c in second[h][1]:
                landed(d, c, h)
                pass_on(d, c, h, 3, core_spot)

    def gather(i):
        d = lax.rem(depth_at + i, depth)

        @pl.when(i > 0)
        def _():
            for h in range(2):
                landed(d, here, h)

        for h in range(2):
            pass_on(d, here, h, 1, first[h][0])
            pass_on(d, here, h, 2, second[h][0])
            pass_on(d, here, h, 3, core_spot)
        for h in range(2):
            landed(d, first[h][1], h)
            pass_on(d, first[h][1], h, 2, second[h][0])
            pass_on(d, first[h][1], h, 3, core_spot)

        @pl.when(i > 0)
        def _():
            last_leg(lax.rem(depth_at + i - 1, depth))

    each(0, depth, gather)
    last_leg(lax.rem(depth_at + depth - 1, depth))

    def from_core(i):
        d = lax.rem(depth_at + i, depth)
        for h in range(2):
            for c in (here, c_x, c_y, c_xy):
                landed(d, c + core_step, h)

    each(0, depth, from_core)

    tokens_on_rest = (all_sums, all_states, all_carry, all_tokens, all_deltas, all_parts)
    for copy in tokens_on_rest:
        copy.wait_send()
    each(0, steps, lambda i: owe_copy(i).wait_send())
    for h in range(2):
        for leg, (tall_sent, wide_sent) in enumerate(
            (((depth - 1) * half, 1), (depth * half, 1), (depth * half, 2), (depth * half, 4))
        ):
            ref = grads.at[:, pl.ds(0, tall_sent), pl.ds(0, wide_sent * LANES)]
            remote(ref, ref, sent.at[h, leg], arrive.at[h, 0, 0], spot(after)).wait_send()


def shards(tokens, query_weight, key_weight, value_weight, log_decay, neighbour_blocks, cotangent):
    rows, width = tokens.shape
    heads = log_decay.shape[0]
    size = width // heads
    pair = 256 // size
    steps = heads // pair
    lanes = pair * size
    sizes = tuple(lax.axis_size(name) for name in AXES)
    devices = sizes[0] * sizes[1]
    position = lax.axis_index(AXES)
    tile = 16
    blocks = min(devices, 2 * size // tile * (width // LANES))
    part = width // (blocks // (2 * size // tile))
    plane, depth = 2 * sizes[0], sizes[1] // 2

    own_times = jnp.sum(neighbour_blocks == position).astype(F32)
    prev_times = jnp.sum(neighbour_blocks == position - 1).astype(F32)
    times = jnp.where(jnp.arange(2 * rows) < rows, own_times, prev_times)[None, :]
    norm = 1.0 / math.sqrt(rows * devices)

    vmem = pl.BlockSpec(memory_space=pltpu.VMEM)
    hbm = pl.BlockSpec(memory_space=pl.ANY)
    semaphores = pltpu.SemaphoreType.DMA
    layer_out, tokens_grad, grads = pl.pallas_call(
        functools.partial(layer_kernel, sizes, size, norm),
        in_specs=[vmem] * 4 + [hbm] * 3,
        out_specs=[vmem] * 3,
        out_shape=[jax.ShapeDtypeStruct((rows, width), BF16)] * 2
        + [jax.ShapeDtypeStruct((3, width, width), BF16)],
        scratch_shapes=[
            pltpu.VMEM((3, width, width), BF16),
            pltpu.VMEM((rows, width), BF16),
            pltpu.VMEM((rows, width), BF16),
            pltpu.VMEM((rows, width), BF16),
            pltpu.VMEM((rows, width), BF16),
            pltpu.VMEM((2 * size, width), BF16),
            pltpu.VMEM((8, width), F32),
            pltpu.VMEM((steps, rows, pair), F32),
            pltpu.VMEM((steps, pair, rows), F32),
            pltpu.VMEM((devices, tile, part), BF16),
            pltpu.VMEM((devices, 8, part), F32),
            pltpu.VMEM((devices, tile, part), BF16),
            pltpu.VMEM((2 * size, width), BF16),
            pltpu.VMEM((rows, width), F32),
            pltpu.VMEM((rows, width), F32),
            pltpu.VMEM((rows, width), F32),
            pltpu.VMEM((rows, width), F32),
            pltpu.VMEM((steps, rows, 2 * lanes), BF16),
            pltpu.VMEM((steps, rows, 2 * lanes), BF16),
            pltpu.VMEM((3, rows, width), BF16),
            pltpu.VMEM((plane, rows, 3 * LANES), BF16),
            pltpu.VMEM((plane * rows, 3 * LANES), BF16),
            pltpu.VMEM((plane * rows, width), BF16),
            pltpu.VMEM((width, 3 * LANES), BF16),
            pltpu.VMEM((depth, width // depth, 3 * LANES), BF16),
            semaphores((3,)),
            semaphores((2,)),
            semaphores((2, 3)),
            semaphores((2, steps)),
            semaphores((2,)),
            semaphores((2,)),
            semaphores((2,)),
            semaphores((2, depth, plane)),
            semaphores((2, 4)),
        ],
        compiler_params=pltpu.CompilerParams(
            collective_id=0, has_side_effects=True, vmem_limit_bytes=50 * 2**20
        ),
        cost_estimate=pl.CostEstimate(flops=10**9, bytes_accessed=10**8, transcendentals=0),
    )(tokens, cotangent, times, log_decay, query_weight, key_weight, value_weight)
    return (layer_out, tokens_grad, grads[0], grads[1], grads[2])


def solution(mesh):
    return jax.shard_map(
        shards,
        mesh=mesh,
        in_specs=(
            P(AXES, None),
            P(),
            P(),
            P(),
            P(None, AXES),
            P(AXES, None),
            P(AXES, None),
        ),
        out_specs=(P(AXES, None), P(AXES, None), P(), P(), P()),
        check_vma=False,
    )
```

```python
import functools
import math

import jax
import jax.numpy as jnp
from jax import lax
from jax.experimental import pallas as pl
from jax.experimental.pallas import tpu as pltpu
from jax.sharding import PartitionSpec as P

AXES = ("group", "span")
F32 = jnp.float32
BF16 = jnp.bfloat16
ROWS = (((0,), (0,)), ((), ()))
COLS = (((1,), (1,)), ((), ()))
MESH = pl.DeviceIdType.MESH
LANES = 128


def dot(a, b, dims=(((1,), (0,)), ((), ())), precision=None):
    return lax.dot_general(a, b, dims, precision=precision, preferred_element_type=F32)


def summary_of(lin_scale, size, q, k, v, g, col):
    heads = q.shape[1] // size
    states, grads = [], []
    for j in range(heads):
        cut = slice(j * size, (j + 1) * size)
        run = col[:, j : j + 1]
        fading = jnp.exp(run[run.shape[0] - 1 :, :] - run)
        weighted = (v[:, cut].astype(F32) * fading).astype(BF16)
        scaled = (g[:, cut].astype(F32) * jnp.exp(run)).astype(BF16)
        states.append(dot(k[:, cut], weighted, ROWS))
        grads.append(lin_scale * dot(q[:, cut], scaled, ROWS))
    return jnp.concatenate(
        [jnp.concatenate(states, axis=1), jnp.concatenate(grads, axis=1)], axis=0
    ).astype(BF16)


def near_pair(lin_scale, soft_scale, size, q, k, v, g, pk, pv, col, row, times):
    rows = q.shape[0]
    heads = q.shape[1] // size
    t = lax.broadcasted_iota(jnp.int32, (rows, rows), 0)
    s = lax.broadcasted_iota(jnp.int32, (rows, rows), 1)
    lower = t >= s
    outs, dqs, dkv, dvv = [], [], [], []
    for j in range(heads):
        cut = slice(j * size, (j + 1) * size)
        qh, gh = q[:, cut], g[:, cut]
        kh = jnp.concatenate([k[:, cut], pk[:, cut]], axis=0)
        vh = jnp.concatenate([v[:, cut], pv[:, cut]], axis=0)
        decay = jnp.where(
            lower, jnp.exp(jnp.minimum(col[:, j : j + 1] - row[j : j + 1, :], 0.0)), 0.0
        ) * lin_scale
        score = dot(qh, kh, COLS)
        grad = dot(gh, vh, COLS)
        logits = jnp.where(times > 0.0, score * soft_scale, -1e30)
        peak = jnp.max(logits, axis=1, keepdims=True)
        terms = jnp.exp(logits - peak) * times
        probs = terms / jnp.sum(terms, axis=1, keepdims=True)
        inner = jnp.sum(probs * grad, axis=1, keepdims=True)
        dlogit = probs * (grad - inner) * soft_scale
        mix = jnp.concatenate(
            [probs[:, :rows] + score[:, :rows] * decay, probs[:, rows:]], axis=1
        ).astype(BF16)
        dmix = jnp.concatenate(
            [dlogit[:, :rows] + grad[:, :rows] * decay, dlogit[:, rows:]], axis=1
        ).astype(BF16)
        outs.append(dot(mix, vh))
        dqs.append(dot(dmix, kh))
        dkv.append(dot(dmix, qh, ROWS))
        dvv.append(dot(mix, gh, ROWS))
    dk = jnp.concatenate(dkv, axis=1)
    dv = jnp.concatenate(dvv, axis=1)
    return (
        jnp.concatenate(outs, axis=1),
        jnp.concatenate(dqs, axis=1),
        dk[:rows],
        dv[:rows],
        jnp.concatenate([dk[rows:], dv[rows:]], axis=1).astype(BF16),
    )


def state_terms(lin_scale, size, q, k, v, g, col, state, later):
    heads = q.shape[1] // size
    outs, dqs, dks, dvs = [], [], [], []
    for j in range(heads):
        cut = slice(j * size, (j + 1) * size)
        run = col[:, j : j + 1]
        growth = lin_scale * jnp.exp(run)
        fading = jnp.exp(run[run.shape[0] - 1 :, :] - run)
        st, lt = state[:, cut], later[:, cut]
        outs.append(growth * dot(q[:, cut], st))
        dqs.append(growth * dot(g[:, cut], st, COLS))
        dks.append(fading * dot(v[:, cut], lt, COLS))
        dvs.append(fading * dot(k[:, cut], lt))
    return [jnp.concatenate(terms, axis=1) for terms in (outs, dqs, dks, dvs)]


def span_of(start, step, length):
    return pl.ds(pl.multiple_of(start * step, step), length)


def layer_kernel(
    sizes, size, norm,
    tokens, g, listed, rates, wq, wk, wv,
    layer, back, grads,
    w, times, q, k, v, prev, local, total, col, row,
    came, decay, made, carry, out, dq, own_k, own_v, owe, due, delta, packed,
    spread, gathered, part, parts_in,
    w_sem, prev_sem, carry_sem, owe_sem, token_sem, delta_sem, part_sem, arrive, sent,
):
    rows, width = tokens.shape
    steps, _, pair = col.shape
    lanes = pair * size
    devices, span = sizes[0] * sizes[1], sizes[1]
    group_at, span_at = lax.axis_index("group"), lax.axis_index("span")
    me = group_at * span + span_at
    depth_at, x_at = span_at // 2, lax.rem(span_at, 2)
    depth = span // 2
    plane = 2 * sizes[0]
    here = group_at * 2 + x_at
    core_at, y_at = lax.rem(group_at, 2), group_at // 2
    x_step, y_step, core_step = 1 - 2 * x_at, 4 * (1 - 2 * y_at), 2 * (1 - 2 * core_at)
    c_x, c_y = here + x_step, here + y_step
    c_xy = here + x_step + y_step
    x_spot = (group_at, span_at + x_step)
    y_spot = (group_at + 2 * (1 - 2 * y_at), span_at)
    core_spot = (group_at + 1 - 2 * core_at, span_at)
    lin_scale = 1.0 / (size * math.sqrt(rows))
    soft_scale = 1.0 / math.sqrt(size)
    high = lax.Precision.HIGHEST

    def spot(index):
        return (index // span, lax.rem(index, span))

    def remote(src, dst, send, recv, where):
        return pltpu.make_async_remote_copy(
            src_ref=src, dst_ref=dst, send_sem=send, recv_sem=recv,
            device_id=where, device_id_type=MESH,
        )

    def each(start, stop, act):
        def one(i, _):
            act(i)
            return 0

        lax.fori_loop(start, stop, one, 0)

    weights = [
        pltpu.make_async_copy(src, w.at[m], w_sem.at[m]) for m, src in enumerate((wq, wk, wv))
    ]
    for copy in weights:
        copy.start()
    barrier = pltpu.get_barrier_semaphore()
    each(
        1, devices,
        lambda i: pl.semaphore_signal(
            barrier, inc=1, device_id=spot(lax.rem(me + i, devices)), device_id_type=MESH
        ),
    )
    down = lax.broadcasted_iota(jnp.int32, (rows, rows), 0)
    along = lax.broadcasted_iota(jnp.int32, (rows, rows), 1)
    rate = rates[...]
    by_row = dot(rate, (down <= along).astype(F32), precision=high)
    by_col = dot((down >= along).astype(F32), rate, COLS, precision=high)
    for i in range(steps):
        col[i] = by_col[:, i * pair : (i + 1) * pair]
        row[i] = by_row[i * pair : (i + 1) * pair, :]
    head = lax.broadcasted_iota(jnp.int32, (steps * pair, width), 0)
    lane = lax.broadcasted_iota(jnp.int32, (steps * pair, width), 1)
    ours = jnp.logical_and(lane >= head * size, lane < (head + 1) * size).astype(F32)
    last = jnp.broadcast_to(by_col[rows - 1 :, :], (8, steps * pair))
    total[...] = dot(last, ours, precision=high)
    listed_own = jnp.sum((listed[...] == me).astype(F32), axis=1, keepdims=True)
    listed_prev = jnp.sum((listed[...] == me - 1).astype(F32), axis=1, keepdims=True)
    key_at = lax.broadcasted_iota(jnp.int32, (1, 2 * rows), 1)
    times[...] = jnp.where(key_at < rows, listed_own, listed_prev)
    pl.semaphore_wait(barrier, devices - 1)

    after = lax.rem(me + 1, devices)
    before = lax.rem(me + devices - 1, devices)
    tokens_on = remote(tokens, prev, prev_sem.at[0], prev_sem.at[1], spot(after))
    tokens_on.start()

    def token_copy(c, n, where):
        at = gathered.at[span_of(c, rows, rows)]
        return remote(tokens if c is here else at, at, token_sem.at[0, n], token_sem.at[1, c], where)

    token_copies = [
        token_copy(here, 0, y_spot), token_copy(here, 1, core_spot), token_copy(here, 2, x_spot),
        token_copy(c_y, 3, core_spot), token_copy(c_x, 4, y_spot), token_copy(c_x, 5, core_spot),
        token_copy(c_xy, 6, core_spot),
    ]
    others_here = pl.ds(0, (plane - 1) * rows)
    token_copies[0].start()
    token_copies[1].start()

    for copy in weights:
        copy.wait()

    def project(i):
        cut = span_of(i, lanes, lanes)
        left = tokens[...]
        q[:, cut] = dot(left, w[0, :, cut]).astype(BF16)
        k[:, cut] = dot(left, w[1, :, cut]).astype(BF16)
        v[:, cut] = dot(left, w[2, :, cut]).astype(BF16)
        local[:, cut] = summary_of(
            lin_scale, size, q[:, cut], k[:, cut], v[:, cut], g[:, cut], col[i]
        )

    each(0, steps, project)

    tile, wide = came.shape[1], came.shape[2]
    across = local.shape[0] // tile
    blocks = across * (width // wide)
    mine = lax.rem(me, blocks)
    base = me - mine

    def part_of(block):
        return span_of(lax.rem(block, across), tile, tile), span_of(block // across, wide, wide)

    one_row = pl.ds(0, 1)

    def send_states(i):
        there = lax.rem(me + i, devices)
        at = part_of(lax.rem(there, blocks))
        remote(
            total.at[one_row, at[1]], decay.at[me, one_row], carry_sem.at[0, 0],
            carry_sem.at[1, 0], spot(there),
        ).start()
        remote(
            local.at[at], came.at[me], carry_sem.at[0, 1], carry_sem.at[1, 1], spot(there)
        ).start()

    each(1, devices, send_states)
    others = pl.ds(0, devices - 1)
    all_sums = remote(
        decay.at[others, one_row], decay.at[others, one_row],
        carry_sem.at[0, 0], carry_sem.at[1, 0], spot(after),
    )
    all_states = remote(
        came.at[others], came.at[others], carry_sem.at[0, 1], carry_sem.at[1, 1], spot(after)
    )
    came[me] = local[part_of(mine)]
    decay[me] = total[:, part_of(mine)[1]]


    def plane_spot(c):
        return (c // 2, depth_at * 2 + lax.rem(c, 2))

    token_copies[2].start()
    gathered[span_of(here, rows, rows), :] = tokens[...]

    tokens_on.wait()

    def owe_copy(i):
        return remote(owe.at[i], due.at[i], owe_sem.at[0, i], owe_sem.at[1, i], spot(before))

    def near(i):
        cut = span_of(i, lanes, lanes)
        pk = dot(prev[...], w[1, :, cut]).astype(BF16)
        pv = dot(prev[...], w[2, :, cut]).astype(BF16)
        values = near_pair(
            lin_scale, soft_scale, size, q[:, cut], k[:, cut], v[:, cut], g[:, cut], pk, pv,
            col[i], row[i], times[...],
        )
        for ref, value in zip((out, dq, own_k, own_v), values):
            ref[:, cut] = value
        owe[i] = values[4]
        owe_copy(i).start()

    each(0, steps // 2, near)

    all_sums.wait_recv()
    all_states.wait_recv()
    back_way = (lax.rem(mine, across) * tile) // size

    def scan(i, state):
        at = i + back_way * (devices - 1 - 2 * i)
        made[at] = state.astype(BF16)
        return jnp.exp(decay[at, :1, :]) * state + came[at].astype(F32)

    lax.fori_loop(0, devices, scan, jnp.zeros((tile, wide), F32))

    def send_carry(i):
        there = base + lax.rem(mine + i, blocks)
        remote(
            made.at[there], carry.at[part_of(mine)], carry_sem.at[0, 2], carry_sem.at[1, 2],
            spot(there),
        ).start()

    each(1, blocks, send_carry)

    def tokens_landed(c):
        token_copy(c, 0, y_spot).wait_recv()

    tokens_landed(c_y)
    token_copies[3].start()
    tokens_landed(c_x)
    token_copies[4].start()
    token_copies[5].start()
    other_blocks = pl.ds(0, blocks - 1)
    all_carry = remote(
        came.at[other_blocks], came.at[other_blocks], carry_sem.at[0, 2], carry_sem.at[1, 2],
        spot(after),
    )
    carry[part_of(mine)] = made[me]
    each(steps // 2, steps, near)
    tokens_landed(c_xy)
    token_copies[6].start()
    all_carry.wait_recv()

    def delta_copy(c):
        return remote(
            packed.at[c], spread.at[span_of(here, rows, rows)], delta_sem.at[0],
            delta_sem.at[1], plane_spot(c),
        )

    def finish(n):
        i = lax.rem(n + here // 2, steps)
        cut = span_of(i, lanes, lanes)
        owe_copy(i).wait_recv()
        terms = state_terms(
            lin_scale, size, q[:, cut], k[:, cut], v[:, cut], g[:, cut], col[i],
            carry[:size, cut], carry[size:, cut],
        )
        layer[:, cut] = (out[:, cut] + terms[0]).astype(BF16)
        owed = due[i].astype(F32)
        deltas = [
            (dq[:, cut] + terms[1]).astype(BF16),
            (own_k[:, cut] + terms[2] + owed[:, :lanes]).astype(BF16),
            (own_v[:, cut] + terms[3] + owed[:, lanes:]).astype(BF16),
        ]
        for m in range(3):
            delta[m, :, cut] = deltas[m]
        for u in range(lanes // LANES):
            c = i * (lanes // LANES) + u
            for m in range(3):
                packed[c, :, m * LANES : (m + 1) * LANES] = deltas[m][:, u * LANES : (u + 1) * LANES]

            @pl.when(c != here)
            def _():
                delta_copy(c).start()

    each(0, steps, finish)
    spread[span_of(here, rows, rows), :] = packed[here]

    def token_back(i):
        cut = span_of(i, lanes, lanes)
        back[:, cut] = (
            dot(delta[0], w[0, cut, :], COLS)
            + dot(delta[1], w[1, cut, :], COLS)
            + dot(delta[2], w[2, cut, :], COLS)
        ).astype(BF16)

    each(0, width // lanes, token_back)

    for c in (here, c_x, c_y, c_xy):
        tokens_landed(c + core_step)
    all_deltas = remote(
        spread.at[others_here], spread.at[others_here], delta_sem.at[0], delta_sem.at[1],
        spot(after),
    )
    all_deltas.wait_recv()
    tall = width // depth
    in_block = max(1, lanes // tall)

    def depth_spot(d):
        return (group_at, d * 2 + x_at)

    def multiply(n):
        b = lax.rem(depth_at // in_block + n, width // lanes)
        cut = span_of(b, lanes, lanes)
        part[cut, :] = dot(gathered[:, cut], spread[...], ROWS).astype(BF16)
        for u in range(in_block):
            d = b * in_block + u

            @pl.when(d != depth_at)
            def _():
                remote(
                    part.at[span_of(d, tall, tall)], parts_in.at[depth_at], part_sem.at[0],
                    part_sem.at[1], depth_spot(d),
                ).start()

    each(1, width // lanes + 1, multiply)
    other_parts = pl.ds(0, depth - 1)
    all_parts = remote(
        parts_in.at[other_parts], parts_in.at[other_parts], part_sem.at[0], part_sem.at[1],
        spot(after),
    )
    all_parts.wait_recv()
    parts_in[depth_at] = part[span_of(depth_at, tall, tall), :]
    for m in range(3):
        cut = slice(m * LANES, (m + 1) * LANES)
        summed = lax.fori_loop(
            0, depth, lambda d, so_far: so_far + parts_in[d, :, cut].astype(F32),
            jnp.zeros((tall, LANES), F32),
        )
        grads[m, span_of(depth_at, tall, tall), span_of(here, LANES, LANES)] = (
            summed * norm
        ).astype(BF16)

    half = tall // 2
    first = ((x_spot, c_x), (y_spot, c_y))
    second = ((y_spot, (c_y, c_xy)), (x_spot, (c_x, c_xy)))

    def block(d, c, h):
        return grads.at[:, span_of(d * 2 + h, half, half), span_of(c, LANES, LANES)]

    def pass_on(d, c, h, leg, where):
        remote(block(d, c, h), block(d, c, h), sent.at[h, leg], arrive.at[h, d, c], where).start()

    def landed(d, c, h):
        remote(
            block(d, c, h), block(d, c, h), sent.at[h, 0], arrive.at[h, d, c], spot(after)
        ).wait_recv()

    def along_depth(i):
        d = lax.rem(depth_at + i, depth)
        for h in range(2):
            pass_on(depth_at, here, h, 0, depth_spot(d))

    each(1, depth, along_depth)

    def last_leg(d):
        for h in range(2):
            for c in second[h][1]:
                landed(d, c, h)
                pass_on(d, c, h, 3, core_spot)

    def gather(i):
        d = lax.rem(depth_at + i, depth)

        @pl.when(i > 0)
        def _():
            for h in range(2):
                landed(d, here, h)

        for h in range(2):
            pass_on(d, here, h, 1, first[h][0])
            pass_on(d, here, h, 2, second[h][0])
            pass_on(d, here, h, 3, core_spot)
        for h in range(2):
            landed(d, first[h][1], h)
            pass_on(d, first[h][1], h, 2, second[h][0])
            pass_on(d, first[h][1], h, 3, core_spot)

        @pl.when(i > 0)
        def _():
            last_leg(lax.rem(depth_at + i - 1, depth))

    each(0, depth, gather)
    last_leg(lax.rem(depth_at + depth - 1, depth))

    def from_core(i):
        d = lax.rem(depth_at + i, depth)
        for h in range(2):
            for c in (here, c_x, c_y, c_xy):
                landed(d, c + core_step, h)

    each(0, depth, from_core)

    tokens_on_rest = (all_sums, all_states, all_carry, all_deltas, all_parts, *token_copies)
    for copy in tokens_on_rest:
        copy.wait_send()
    each(0, steps, lambda i: owe_copy(i).wait_send())
    for h in range(2):
        for leg, (tall_sent, wide_sent) in enumerate(
            (((depth - 1) * half, 1), (depth * half, 1), (depth * half, 2), (depth * half, 4))
        ):
            ref = grads.at[:, pl.ds(0, tall_sent), pl.ds(0, wide_sent * LANES)]
            remote(ref, ref, sent.at[h, leg], arrive.at[h, 0, 0], spot(after)).wait_send()


def shards(tokens, query_weight, key_weight, value_weight, log_decay, neighbour_blocks, cotangent):
    rows, width = tokens.shape
    heads = log_decay.shape[0]
    size = width // heads
    pair = 256 // size
    steps = heads // pair
    lanes = pair * size
    sizes = tuple(lax.axis_size(name) for name in AXES)
    devices = sizes[0] * sizes[1]
    tile = 16
    blocks = min(devices, 2 * size // tile * (width // LANES))
    part = width // (blocks // (2 * size // tile))
    plane, depth = 2 * sizes[0], sizes[1] // 2

    norm = 1.0 / math.sqrt(rows * devices)

    vmem = pl.BlockSpec(memory_space=pltpu.VMEM)
    hbm = pl.BlockSpec(memory_space=pl.ANY)
    semaphores = pltpu.SemaphoreType.DMA
    layer_out, tokens_grad, grads = pl.pallas_call(
        functools.partial(layer_kernel, sizes, size, norm),
        in_specs=[vmem] * 4 + [hbm] * 3,
        out_specs=[vmem] * 3,
        out_shape=[jax.ShapeDtypeStruct((rows, width), BF16)] * 2
        + [jax.ShapeDtypeStruct((3, width, width), BF16)],
        scratch_shapes=[
            pltpu.VMEM((3, width, width), BF16),
            pltpu.VMEM((1, 2 * rows), F32),
            pltpu.VMEM((rows, width), BF16),
            pltpu.VMEM((rows, width), BF16),
            pltpu.VMEM((rows, width), BF16),
            pltpu.VMEM((rows, width), BF16),
            pltpu.VMEM((2 * size, width), BF16),
            pltpu.VMEM((8, width), F32),
            pltpu.VMEM((steps, rows, pair), F32),
            pltpu.VMEM((steps, pair, rows), F32),
            pltpu.VMEM((devices, tile, part), BF16),
            pltpu.VMEM((devices, 8, part), F32),
            pltpu.VMEM((devices, tile, part), BF16),
            pltpu.VMEM((2 * size, width), BF16),
            pltpu.VMEM((rows, width), F32),
            pltpu.VMEM((rows, width), F32),
            pltpu.VMEM((rows, width), F32),
            pltpu.VMEM((rows, width), F32),
            pltpu.VMEM((steps, rows, 2 * lanes), BF16),
            pltpu.VMEM((steps, rows, 2 * lanes), BF16),
            pltpu.VMEM((3, rows, width), BF16),
            pltpu.VMEM((plane, rows, 3 * LANES), BF16),
            pltpu.VMEM((plane * rows, 3 * LANES), BF16),
            pltpu.VMEM((plane * rows, width), BF16),
            pltpu.VMEM((width, 3 * LANES), BF16),
            pltpu.VMEM((depth, width // depth, 3 * LANES), BF16),
            semaphores((3,)),
            semaphores((2,)),
            semaphores((2, 3)),
            semaphores((2, steps)),
            semaphores((2, plane)),
            semaphores((2,)),
            semaphores((2,)),
            semaphores((2, depth, plane)),
            semaphores((2, 4)),
        ],
        compiler_params=pltpu.CompilerParams(
            collective_id=0, has_side_effects=True, vmem_limit_bytes=60 * 2**20
        ),
        cost_estimate=pl.CostEstimate(flops=10**9, bytes_accessed=10**8, transcendentals=0),
    )(tokens, cotangent, neighbour_blocks, log_decay, query_weight, key_weight, value_weight)
    return (layer_out, tokens_grad, grads[0], grads[1], grads[2])


def solution(mesh):
    return jax.shard_map(
        shards,
        mesh=mesh,
        in_specs=(
            P(AXES, None),
            P(),
            P(),
            P(),
            P(None, AXES),
            P(AXES, None),
            P(AXES, None),
        ),
        out_specs=(P(AXES, None), P(AXES, None), P(), P(), P()),
        check_vma=False,
    )
```

```python
import functools
import math

import jax
import jax.numpy as jnp
from jax import lax
from jax.experimental import pallas as pl
from jax.experimental.pallas import tpu as pltpu
from jax.sharding import PartitionSpec as P

AXES = ("group", "span")
F32 = jnp.float32
BF16 = jnp.bfloat16
ROWS = (((0,), (0,)), ((), ()))
COLS = (((1,), (1,)), ((), ()))
MESH = pl.DeviceIdType.MESH
LANES = 128


def dot(a, b, dims=(((1,), (0,)), ((), ())), precision=None):
    return lax.dot_general(a, b, dims, precision=precision, preferred_element_type=F32)


def summary_of(lin_scale, size, q, k, v, g, col):
    heads = q.shape[1] // size
    states, grads = [], []
    for j in range(heads):
        cut = slice(j * size, (j + 1) * size)
        run = col[:, j : j + 1]
        fading = jnp.exp(run[run.shape[0] - 1 :, :] - run)
        weighted = (v[:, cut].astype(F32) * fading).astype(BF16)
        scaled = (g[:, cut].astype(F32) * jnp.exp(run)).astype(BF16)
        states.append(dot(k[:, cut], weighted, ROWS))
        grads.append(lin_scale * dot(q[:, cut], scaled, ROWS))
    return jnp.concatenate(
        [jnp.concatenate(states, axis=1), jnp.concatenate(grads, axis=1)], axis=0
    ).astype(BF16)


def near_pair(lin_scale, soft_scale, size, q, k, v, g, pk, pv, col, row, times):
    rows = q.shape[0]
    heads = q.shape[1] // size
    t = lax.broadcasted_iota(jnp.int32, (rows, rows), 0)
    s = lax.broadcasted_iota(jnp.int32, (rows, rows), 1)
    lower = t >= s
    outs, dqs, dkv, dvv = [], [], [], []
    for j in range(heads):
        cut = slice(j * size, (j + 1) * size)
        qh, gh = q[:, cut], g[:, cut]
        kh = jnp.concatenate([k[:, cut], pk[:, cut]], axis=0)
        vh = jnp.concatenate([v[:, cut], pv[:, cut]], axis=0)
        decay = jnp.where(
            lower, jnp.exp(jnp.minimum(col[:, j : j + 1] - row[j : j + 1, :], 0.0)), 0.0
        ) * lin_scale
        score = dot(qh, kh, COLS)
        grad = dot(gh, vh, COLS)
        logits = jnp.where(times > 0.0, score * soft_scale, -1e30)
        peak = jnp.max(logits, axis=1, keepdims=True)
        terms = jnp.exp(logits - peak) * times
        probs = terms / jnp.sum(terms, axis=1, keepdims=True)
        inner = jnp.sum(probs * grad, axis=1, keepdims=True)
        dlogit = probs * (grad - inner) * soft_scale
        mix = jnp.concatenate(
            [probs[:, :rows] + score[:, :rows] * decay, probs[:, rows:]], axis=1
        ).astype(BF16)
        dmix = jnp.concatenate(
            [dlogit[:, :rows] + grad[:, :rows] * decay, dlogit[:, rows:]], axis=1
        ).astype(BF16)
        outs.append(dot(mix, vh))
        dqs.append(dot(dmix, kh))
        dkv.append(dot(dmix, qh, ROWS))
        dvv.append(dot(mix, gh, ROWS))
    dk = jnp.concatenate(dkv, axis=1)
    dv = jnp.concatenate(dvv, axis=1)
    return (
        jnp.concatenate(outs, axis=1),
        jnp.concatenate(dqs, axis=1),
        dk[:rows],
        dv[:rows],
        jnp.concatenate([dk[rows:], dv[rows:]], axis=1).astype(BF16),
    )


def state_terms(lin_scale, size, q, k, v, g, col, state, later):
    heads = q.shape[1] // size
    outs, dqs, dks, dvs = [], [], [], []
    for j in range(heads):
        cut = slice(j * size, (j + 1) * size)
        run = col[:, j : j + 1]
        growth = lin_scale * jnp.exp(run)
        fading = jnp.exp(run[run.shape[0] - 1 :, :] - run)
        st, lt = state[:, cut], later[:, cut]
        outs.append(growth * dot(q[:, cut], st))
        dqs.append(growth * dot(g[:, cut], st, COLS))
        dks.append(fading * dot(v[:, cut], lt, COLS))
        dvs.append(fading * dot(k[:, cut], lt))
    return [jnp.concatenate(terms, axis=1) for terms in (outs, dqs, dks, dvs)]


def span_of(start, step, length):
    return pl.ds(pl.multiple_of(start * step, step), length)


def layer_kernel(
    sizes, size, norm,
    tokens, g, listed, rates, wq, wk, wv,
    layer, back, grad_q, grad_k, grad_v,
    w, times, q, k, v, prev, local, total, col, row,
    came, decay, made, carry, out, dq, own_k, own_v, owe, due, delta, packed,
    spread, gathered, part, parts_in,
    w_sem, prev_sem, carry_sem, owe_sem, token_sem, delta_sem, part_sem, arrive, sent, hop_sem,
):
    rows, width = tokens.shape
    steps, _, pair = col.shape
    lanes = pair * size
    devices, span = sizes[0] * sizes[1], sizes[1]
    group_at, span_at = lax.axis_index("group"), lax.axis_index("span")
    me = group_at * span + span_at
    depth_at, x_at = span_at // 2, lax.rem(span_at, 2)
    depth = span // 2
    plane = 2 * sizes[0]
    here = group_at * 2 + x_at
    core_at, y_at = lax.rem(group_at, 2), group_at // 2
    x_step, y_step, core_step = 1 - 2 * x_at, 4 * (1 - 2 * y_at), 2 * (1 - 2 * core_at)
    c_x, c_y = here + x_step, here + y_step
    c_xy = here + x_step + y_step
    x_spot = (group_at, span_at + x_step)
    y_spot = (group_at + 2 * (1 - 2 * y_at), span_at)
    core_spot = (group_at + 1 - 2 * core_at, span_at)
    lin_scale = 1.0 / (size * math.sqrt(rows))
    soft_scale = 1.0 / math.sqrt(size)
    high = lax.Precision.HIGHEST

    def spot(index):
        return (index // span, lax.rem(index, span))

    def remote(src, dst, send, recv, where):
        return pltpu.make_async_remote_copy(
            src_ref=src, dst_ref=dst, send_sem=send, recv_sem=recv,
            device_id=where, device_id_type=MESH,
        )

    def each(start, stop, act):
        def one(i, _):
            act(i)
            return 0

        lax.fori_loop(start, stop, one, 0)

    weights = [
        pltpu.make_async_copy(src, w.at[m], w_sem.at[m]) for m, src in enumerate((wq, wk, wv))
    ]
    for copy in weights:
        copy.start()
    barrier = pltpu.get_barrier_semaphore()
    each(
        1, devices,
        lambda i: pl.semaphore_signal(
            barrier, inc=1, device_id=spot(lax.rem(me + i, devices)), device_id_type=MESH
        ),
    )
    down = lax.broadcasted_iota(jnp.int32, (rows, rows), 0)
    along = lax.broadcasted_iota(jnp.int32, (rows, rows), 1)
    rate = rates[...]
    by_row = dot(rate, (down <= along).astype(F32), precision=high)
    by_col = dot((down >= along).astype(F32), rate, COLS, precision=high)
    for i in range(steps):
        col[i] = by_col[:, i * pair : (i + 1) * pair]
        row[i] = by_row[i * pair : (i + 1) * pair, :]
    head = lax.broadcasted_iota(jnp.int32, (steps * pair, width), 0)
    lane = lax.broadcasted_iota(jnp.int32, (steps * pair, width), 1)
    ours = jnp.logical_and(lane >= head * size, lane < (head + 1) * size).astype(F32)
    last = jnp.broadcast_to(by_col[rows - 1 :, :], (8, steps * pair))
    total[...] = dot(last, ours, precision=high)
    listed_own = jnp.sum((listed[...] == me).astype(F32), axis=1, keepdims=True)
    listed_prev = jnp.sum((listed[...] == me - 1).astype(F32), axis=1, keepdims=True)
    key_at = lax.broadcasted_iota(jnp.int32, (1, 2 * rows), 1)
    times[...] = jnp.where(key_at < rows, listed_own, listed_prev)
    pl.semaphore_wait(barrier, devices - 1)

    after = lax.rem(me + 1, devices)
    before = lax.rem(me + devices - 1, devices)
    tokens_on = remote(tokens, prev, prev_sem.at[0], prev_sem.at[1], spot(after))
    tokens_on.start()

    def token_copy(c, n, where):
        at = gathered.at[span_of(c, rows, rows)]
        return remote(tokens if c is here else at, at, token_sem.at[0, n], token_sem.at[1, c], where)

    token_copies = [
        token_copy(here, 0, y_spot), token_copy(here, 1, core_spot), token_copy(here, 2, x_spot),
        token_copy(c_y, 3, core_spot), token_copy(c_x, 4, y_spot), token_copy(c_x, 5, core_spot),
        token_copy(c_xy, 6, core_spot),
    ]
    others_here = pl.ds(0, (plane - 1) * rows)
    token_copies[0].start()
    token_copies[1].start()

    for copy in weights:
        copy.wait()

    def project(i):
        cut = span_of(i, lanes, lanes)
        left = tokens[...]
        q[:, cut] = dot(left, w[0, :, cut]).astype(BF16)
        k[:, cut] = dot(left, w[1, :, cut]).astype(BF16)
        v[:, cut] = dot(left, w[2, :, cut]).astype(BF16)
        local[:, cut] = summary_of(
            lin_scale, size, q[:, cut], k[:, cut], v[:, cut], g[:, cut], col[i]
        )

    each(0, steps, project)

    tile, wide = came.shape[1], came.shape[2]
    across = local.shape[0] // tile
    blocks = across * (width // wide)
    mine = lax.rem(me, blocks)
    base = me - mine

    def part_of(block):
        return span_of(lax.rem(block, across), tile, tile), span_of(block // across, wide, wide)

    one_row = pl.ds(0, 1)

    def send_states(i):
        there = lax.rem(me + i, devices)
        at = part_of(lax.rem(there, blocks))
        remote(
            total.at[one_row, at[1]], decay.at[me, one_row], carry_sem.at[0, 0],
            carry_sem.at[1, 0], spot(there),
        ).start()
        remote(
            local.at[at], came.at[me], carry_sem.at[0, 1], carry_sem.at[1, 1], spot(there)
        ).start()

    each(1, devices, send_states)
    others = pl.ds(0, devices - 1)
    all_sums = remote(
        decay.at[others, one_row], decay.at[others, one_row],
        carry_sem.at[0, 0], carry_sem.at[1, 0], spot(after),
    )
    all_states = remote(
        came.at[others], came.at[others], carry_sem.at[0, 1], carry_sem.at[1, 1], spot(after)
    )
    came[me] = local[part_of(mine)]
    decay[me] = total[:, part_of(mine)[1]]


    def plane_spot(c):
        return (c // 2, depth_at * 2 + lax.rem(c, 2))

    token_copies[2].start()
    gathered[span_of(here, rows, rows), :] = tokens[...]

    tokens_on.wait()

    def owe_copy(i):
        return remote(owe.at[i], due.at[i], owe_sem.at[0, i], owe_sem.at[1, i], spot(before))

    def near(i):
        cut = span_of(i, lanes, lanes)
        pk = dot(prev[...], w[1, :, cut]).astype(BF16)
        pv = dot(prev[...], w[2, :, cut]).astype(BF16)
        values = near_pair(
            lin_scale, soft_scale, size, q[:, cut], k[:, cut], v[:, cut], g[:, cut], pk, pv,
            col[i], row[i], times[...],
        )
        for ref, value in zip((out, dq, own_k, own_v), values):
            ref[:, cut] = value
        owe[i] = values[4]
        owe_copy(i).start()

    each(0, steps // 2, near)

    all_sums.wait_recv()
    all_states.wait_recv()
    back_way = (lax.rem(mine, across) * tile) // size

    def scan(i, state):
        at = i + back_way * (devices - 1 - 2 * i)
        made[at] = state.astype(BF16)
        return jnp.exp(decay[at, :1, :]) * state + came[at].astype(F32)

    lax.fori_loop(0, devices, scan, jnp.zeros((tile, wide), F32))

    def send_carry(i):
        there = base + lax.rem(mine + i, blocks)
        remote(
            made.at[there], carry.at[part_of(mine)], carry_sem.at[0, 2], carry_sem.at[1, 2],
            spot(there),
        ).start()

    each(1, blocks, send_carry)

    def tokens_landed(c):
        token_copy(c, 0, y_spot).wait_recv()

    tokens_landed(c_y)
    token_copies[3].start()
    tokens_landed(c_x)
    token_copies[4].start()
    token_copies[5].start()
    other_blocks = pl.ds(0, blocks - 1)
    all_carry = remote(
        came.at[other_blocks], came.at[other_blocks], carry_sem.at[0, 2], carry_sem.at[1, 2],
        spot(after),
    )
    carry[part_of(mine)] = made[me]
    each(steps // 2, steps, near)
    tokens_landed(c_xy)
    token_copies[6].start()
    all_carry.wait_recv()

    def delta_copy(c):
        return remote(
            packed.at[c], spread.at[span_of(here, rows, rows)], delta_sem.at[0],
            delta_sem.at[1], plane_spot(c),
        )

    def finish(n):
        i = lax.rem(n + here // 2, steps)
        cut = span_of(i, lanes, lanes)
        owe_copy(i).wait_recv()
        terms = state_terms(
            lin_scale, size, q[:, cut], k[:, cut], v[:, cut], g[:, cut], col[i],
            carry[:size, cut], carry[size:, cut],
        )
        layer[:, cut] = (out[:, cut] + terms[0]).astype(BF16)
        owed = due[i].astype(F32)
        deltas = [
            (dq[:, cut] + terms[1]).astype(BF16),
            (own_k[:, cut] + terms[2] + owed[:, :lanes]).astype(BF16),
            (own_v[:, cut] + terms[3] + owed[:, lanes:]).astype(BF16),
        ]
        for m in range(3):
            delta[m, :, cut] = deltas[m]
        for u in range(lanes // LANES):
            c = i * (lanes // LANES) + u
            for m in range(3):
                packed[c, :, m * LANES : (m + 1) * LANES] = deltas[m][:, u * LANES : (u + 1) * LANES]

            @pl.when(c != here)
            def _():
                delta_copy(c).start()

    each(0, steps, finish)
    spread[span_of(here, rows, rows), :] = packed[here]

    def token_back(i):
        cut = span_of(i, lanes, lanes)
        back[:, cut] = (
            dot(delta[0], w[0, cut, :], COLS)
            + dot(delta[1], w[1, cut, :], COLS)
            + dot(delta[2], w[2, cut, :], COLS)
        ).astype(BF16)

    each(0, width // lanes // 2, token_back)

    for c in (here, c_x, c_y, c_xy):
        tokens_landed(c + core_step)
    all_deltas = remote(
        spread.at[others_here], spread.at[others_here], delta_sem.at[0], delta_sem.at[1],
        spot(after),
    )
    all_deltas.wait_recv()
    tall = width // depth
    in_block = max(1, lanes // tall)
    grads = (grad_q, grad_k, grad_v)
    other_parts = pl.ds(0, depth - 1)

    def depth_spot(d):
        return (group_at, d * 2 + x_at)

    def part_copy(m, d):
        return remote(
            part.at[m, span_of(d, tall, tall)], parts_in.at[m, depth_at], part_sem.at[0, m],
            part_sem.at[1, m], depth_spot(d),
        )

    def multiply(n):
        b = lax.rem(depth_at // in_block + n, width // lanes)
        cut = span_of(b, lanes, lanes)
        product = dot(gathered[:, cut], spread[...], ROWS).astype(BF16)
        for m in range(3):
            part[m, cut, :] = product[:, m * LANES : (m + 1) * LANES]
        for u in range(in_block):
            d = b * in_block + u

            @pl.when(d != depth_at)
            def _():
                part_copy(0, d).start()

    each(1, width // lanes + 1, multiply)
    each(width // lanes // 2, width // lanes, token_back)

    half = tall // 2
    ways = ((x_spot, c_x), (y_spot, c_y))
    pieces = ((0, 0, tall, 0), (1, 0, tall, 1), (2, 0, half, 0), (2, half, half, 1))

    def block(d, c, p):
        m, start, count, _ = pieces[p]
        down = pl.ds(pl.multiple_of(d * tall + start, 16), count)
        return grads[m].at[down, span_of(c, LANES, LANES)]

    def block_copy(d, c, p, leg, where):
        return remote(block(d, c, p), block(d, c, p), sent.at[p, leg], arrive.at[p, d, c], where)

    def hop_copy(d, p, way):
        to = depth_at + 1 - 2 * way
        return remote(
            block(d, here, p), block(d, here, p), hop_sem.at[p, way, d], arrive.at[p, d, here],
            depth_spot(to),
        )

    def landed(d, c, p):
        block_copy(d, c, p, 0, spot(after)).wait_recv()

    def hop(d, p, way, act):
        to = depth_at + 1 - 2 * way

        @pl.when(jnp.logical_and(to >= 0, to < depth))
        def _():
            act(hop_copy(d, p, way))

    def around(i, act):
        for way in range(2):
            d = depth_at - i * (1 - 2 * way)
            valid = jnp.logical_and(jnp.logical_and(d >= 0, d < depth), i >= way)

            @pl.when(valid)
            def _():
                act(d, way)

    def to_ways(d, p):
        one = pieces[p][3]
        block_copy(d, here, p, 0, ways[one][0]).start()
        block_copy(d, here, p, 1, ways[1 - one][0]).start()
        block_copy(d, here, p, 2, core_spot).start()

    def step(p, i):
        def act(d, way):
            landed(d, here, p)
            hop(d, p, way, lambda copy: copy.start())
            to_ways(d, p)

        around(i, act)

    def first_leg(p, i):
        one = pieces[p][3]

        def act(d, way):
            c = ways[one][1]
            landed(d, c, p)
            block_copy(d, c, p, 1, ways[1 - one][0]).start()
            block_copy(d, c, p, 2, core_spot).start()

        around(i, act)

    def second_leg(p, i):
        def act(d, way):
            for c in (ways[1 - pieces[p][3]][1], c_xy):
                landed(d, c, p)
                block_copy(d, c, p, 2, core_spot).start()

        around(i, act)

    all_parts = [
        remote(
            parts_in.at[m, other_parts], parts_in.at[m, other_parts], part_sem.at[0, m],
            part_sem.at[1, m], spot(after),
        )
        for m in range(3)
    ]

    def sum_parts(m):
        all_parts[m].wait_recv()
        if m < 2:
            each(1, depth, lambda i: part_copy(m + 1, lax.rem(depth_at + i, depth)).start())
        own = span_of(depth_at, tall, tall)
        parts_in[m, depth_at] = part[m, own, :]
        summed = lax.fori_loop(
            0, depth, lambda d, so_far: so_far + parts_in[m, d].astype(F32),
            jnp.zeros((tall, LANES), F32),
        )
        grads[m][own, span_of(here, LANES, LANES)] = (summed * norm).astype(BF16)
        for p, piece in enumerate(pieces):
            if piece[0] == m:
                for way in range(2):
                    hop(depth_at, p, way, lambda copy: copy.start())
                to_ways(depth_at, p)

    sum_parts(0)
    first_leg(0, 0)
    step(0, 1)
    sum_parts(1)
    first_leg(0, 1)
    second_leg(0, 0)
    step(0, 2)
    first_leg(1, 0)
    step(1, 1)
    sum_parts(2)

    def onward(n):
        for p, ahead in enumerate((2, 1, 0, 0)):
            i = n + ahead
            step(p, i)
            first_leg(p, i - 1)
            second_leg(p, i - 2)

    each(1, depth + 2, onward)

    def from_core(d):
        for p in range(len(pieces)):
            for c in (here, c_x, c_y, c_xy):
                landed(d, c + core_step, p)

    each(0, depth, from_core)

    tokens_on_rest = (all_sums, all_states, all_carry, all_deltas, *all_parts, *token_copies)
    for copy in tokens_on_rest:
        copy.wait_send()
    each(0, steps, lambda i: owe_copy(i).wait_send())
    for p, (m, _, count, _) in enumerate(pieces):
        for leg, columns in enumerate((1, 2, 4)):
            ref = grads[m].at[pl.ds(0, depth * count), pl.ds(0, columns * LANES)]
            remote(ref, ref, sent.at[p, leg], arrive.at[p, 0, 0], spot(after)).wait_send()

    def hops_left(i):
        def act(d, way):
            for p in range(len(pieces)):
                hop(d, p, way, lambda copy: copy.wait_send())

        around(i, act)

    each(1, depth, hops_left)
    for p in range(len(pieces)):
        for way in range(2):
            hop(depth_at, p, way, lambda copy: copy.wait_send())


def shards(tokens, query_weight, key_weight, value_weight, log_decay, neighbour_blocks, cotangent):
    rows, width = tokens.shape
    heads = log_decay.shape[0]
    size = width // heads
    pair = 256 // size
    steps = heads // pair
    lanes = pair * size
    sizes = tuple(lax.axis_size(name) for name in AXES)
    devices = sizes[0] * sizes[1]
    tile = 16
    blocks = min(devices, 2 * size // tile * (width // LANES))
    part = width // (blocks // (2 * size // tile))
    plane, depth = 2 * sizes[0], sizes[1] // 2

    norm = 1.0 / math.sqrt(rows * devices)

    vmem = pl.BlockSpec(memory_space=pltpu.VMEM)
    hbm = pl.BlockSpec(memory_space=pl.ANY)
    semaphores = pltpu.SemaphoreType.DMA
    return pl.pallas_call(
        functools.partial(layer_kernel, sizes, size, norm),
        in_specs=[vmem] * 4 + [hbm] * 3,
        out_specs=[vmem] * 5,
        out_shape=[jax.ShapeDtypeStruct((rows, width), BF16)] * 2
        + [jax.ShapeDtypeStruct((width, width), BF16)] * 3,
        scratch_shapes=[
            pltpu.VMEM((3, width, width), BF16),
            pltpu.VMEM((1, 2 * rows), F32),
            pltpu.VMEM((rows, width), BF16),
            pltpu.VMEM((rows, width), BF16),
            pltpu.VMEM((rows, width), BF16),
            pltpu.VMEM((rows, width), BF16),
            pltpu.VMEM((2 * size, width), BF16),
            pltpu.VMEM((8, width), F32),
            pltpu.VMEM((steps, rows, pair), F32),
            pltpu.VMEM((steps, pair, rows), F32),
            pltpu.VMEM((devices, tile, part), BF16),
            pltpu.VMEM((devices, 8, part), F32),
            pltpu.VMEM((devices, tile, part), BF16),
            pltpu.VMEM((2 * size, width), BF16),
            pltpu.VMEM((rows, width), F32),
            pltpu.VMEM((rows, width), F32),
            pltpu.VMEM((rows, width), F32),
            pltpu.VMEM((rows, width), F32),
            pltpu.VMEM((steps, rows, 2 * lanes), BF16),
            pltpu.VMEM((steps, rows, 2 * lanes), BF16),
            pltpu.VMEM((3, rows, width), BF16),
            pltpu.VMEM((plane, rows, 3 * LANES), BF16),
            pltpu.VMEM((plane * rows, 3 * LANES), BF16),
            pltpu.VMEM((plane * rows, width), BF16),
            pltpu.VMEM((3, width, LANES), BF16),
            pltpu.VMEM((3, depth, width // depth, LANES), BF16),
            semaphores((3,)),
            semaphores((2,)),
            semaphores((2, 3)),
            semaphores((2, steps)),
            semaphores((2, plane)),
            semaphores((2,)),
            semaphores((2, 3)),
            semaphores((4, depth, plane)),
            semaphores((4, 3)),
            semaphores((4, 2, depth)),
        ],
        compiler_params=pltpu.CompilerParams(
            collective_id=0, has_side_effects=True, vmem_limit_bytes=60 * 2**20
        ),
        cost_estimate=pl.CostEstimate(flops=10**9, bytes_accessed=10**8, transcendentals=0),
    )(tokens, cotangent, neighbour_blocks, log_decay, query_weight, key_weight, value_weight)


def solution(mesh):
    return jax.shard_map(
        shards,
        mesh=mesh,
        in_specs=(
            P(AXES, None),
            P(),
            P(),
            P(),
            P(None, AXES),
            P(AXES, None),
            P(AXES, None),
        ),
        out_specs=(P(AXES, None), P(AXES, None), P(), P(), P()),
        check_vma=False,
    )
```

```python
import functools
import math

import jax
import jax.numpy as jnp
from jax import lax
from jax.experimental import pallas as pl
from jax.experimental.pallas import tpu as pltpu
from jax.sharding import PartitionSpec as P

AXES = ("group", "span")
F32 = jnp.float32
BF16 = jnp.bfloat16
ROWS = (((0,), (0,)), ((), ()))
COLS = (((1,), (1,)), ((), ()))
MESH = pl.DeviceIdType.MESH
LANES = 128


def dot(a, b, dims=(((1,), (0,)), ((), ())), precision=None):
    return lax.dot_general(a, b, dims, precision=precision, preferred_element_type=F32)


def summary_of(lin_scale, size, q, k, v, g, col):
    heads = q.shape[1] // size
    states, grads = [], []
    for j in range(heads):
        cut = slice(j * size, (j + 1) * size)
        run = col[:, j : j + 1]
        fading = jnp.exp(run[run.shape[0] - 1 :, :] - run)
        weighted = (v[:, cut].astype(F32) * fading).astype(BF16)
        scaled = (g[:, cut].astype(F32) * jnp.exp(run)).astype(BF16)
        states.append(dot(k[:, cut], weighted, ROWS))
        grads.append(lin_scale * dot(q[:, cut], scaled, ROWS))
    return jnp.concatenate(
        [jnp.concatenate(states, axis=1), jnp.concatenate(grads, axis=1)], axis=0
    ).astype(BF16)


def near_pair(lin_scale, soft_scale, size, q, k, v, g, pk, pv, col, row, times):
    rows = q.shape[0]
    heads = q.shape[1] // size
    t = lax.broadcasted_iota(jnp.int32, (rows, rows), 0)
    s = lax.broadcasted_iota(jnp.int32, (rows, rows), 1)
    lower = t >= s
    outs, dqs, dkv, dvv = [], [], [], []
    for j in range(heads):
        cut = slice(j * size, (j + 1) * size)
        qh, gh = q[:, cut], g[:, cut]
        kh = jnp.concatenate([k[:, cut], pk[:, cut]], axis=0)
        vh = jnp.concatenate([v[:, cut], pv[:, cut]], axis=0)
        decay = jnp.where(
            lower, jnp.exp(jnp.minimum(col[:, j : j + 1] - row[j : j + 1, :], 0.0)), 0.0
        ) * lin_scale
        score = dot(qh, kh, COLS)
        grad = dot(gh, vh, COLS)
        logits = jnp.where(times > 0.0, score * soft_scale, -1e30)
        peak = jnp.max(logits, axis=1, keepdims=True)
        terms = jnp.exp(logits - peak) * times
        probs = terms / jnp.sum(terms, axis=1, keepdims=True)
        inner = jnp.sum(probs * grad, axis=1, keepdims=True)
        dlogit = probs * (grad - inner) * soft_scale
        mix = jnp.concatenate(
            [probs[:, :rows] + score[:, :rows] * decay, probs[:, rows:]], axis=1
        ).astype(BF16)
        dmix = jnp.concatenate(
            [dlogit[:, :rows] + grad[:, :rows] * decay, dlogit[:, rows:]], axis=1
        ).astype(BF16)
        outs.append(dot(mix, vh))
        dqs.append(dot(dmix, kh))
        dkv.append(dot(dmix, qh, ROWS))
        dvv.append(dot(mix, gh, ROWS))
    dk = jnp.concatenate(dkv, axis=1)
    dv = jnp.concatenate(dvv, axis=1)
    return (
        jnp.concatenate(outs, axis=1),
        jnp.concatenate(dqs, axis=1),
        dk[:rows],
        dv[:rows],
        jnp.concatenate([dk[rows:], dv[rows:]], axis=1).astype(BF16),
    )


def state_terms(lin_scale, size, q, k, v, g, col, state, later):
    heads = q.shape[1] // size
    outs, dqs, dks, dvs = [], [], [], []
    for j in range(heads):
        cut = slice(j * size, (j + 1) * size)
        run = col[:, j : j + 1]
        growth = lin_scale * jnp.exp(run)
        fading = jnp.exp(run[run.shape[0] - 1 :, :] - run)
        st, lt = state[:, cut], later[:, cut]
        outs.append(growth * dot(q[:, cut], st))
        dqs.append(growth * dot(g[:, cut], st, COLS))
        dks.append(fading * dot(v[:, cut], lt, COLS))
        dvs.append(fading * dot(k[:, cut], lt))
    return [jnp.concatenate(terms, axis=1) for terms in (outs, dqs, dks, dvs)]


def span_of(start, step, length):
    return pl.ds(pl.multiple_of(start * step, step), length)


def layer_kernel(
    sizes, size, norm,
    tokens, g, listed, rates, wq, wk, wv,
    layer, back, grad_q, grad_k, grad_v,
    w, times, q, k, v, prev, local, total, col, row,
    came, decay, made, carry, out, dq, own_k, own_v, owe, due, delta, packed,
    spread, gathered, part, parts_in,
    w_sem, prev_sem, carry_sem, owe_sem, token_sem, delta_sem, part_sem, arrive, sent, hop_sem,
):
    rows, width = tokens.shape
    steps, _, pair = col.shape
    lanes = pair * size
    devices, span = sizes[0] * sizes[1], sizes[1]
    group_at, span_at = lax.axis_index("group"), lax.axis_index("span")
    me = group_at * span + span_at
    depth_at, x_at = span_at // 2, lax.rem(span_at, 2)
    depth = span // 2
    plane = 2 * sizes[0]
    here = group_at * 2 + x_at
    core_at, y_at = lax.rem(group_at, 2), group_at // 2
    x_step, y_step, core_step = 1 - 2 * x_at, 4 * (1 - 2 * y_at), 2 * (1 - 2 * core_at)
    c_x, c_y = here + x_step, here + y_step
    c_xy = here + x_step + y_step
    x_spot = (group_at, span_at + x_step)
    y_spot = (group_at + 2 * (1 - 2 * y_at), span_at)
    core_spot = (group_at + 1 - 2 * core_at, span_at)
    lin_scale = 1.0 / (size * math.sqrt(rows))
    soft_scale = 1.0 / math.sqrt(size)
    high = lax.Precision.HIGHEST

    def spot(index):
        return (index // span, lax.rem(index, span))

    def remote(src, dst, send, recv, where):
        return pltpu.make_async_remote_copy(
            src_ref=src, dst_ref=dst, send_sem=send, recv_sem=recv,
            device_id=where, device_id_type=MESH,
        )

    def each(start, stop, act):
        def one(i, _):
            act(i)
            return 0

        lax.fori_loop(start, stop, one, 0)

    weights = [
        pltpu.make_async_copy(src, w.at[m], w_sem.at[m]) for m, src in enumerate((wq, wk, wv))
    ]
    for copy in weights:
        copy.start()
    barrier = pltpu.get_barrier_semaphore()
    each(
        1, devices,
        lambda i: pl.semaphore_signal(
            barrier, inc=1, device_id=spot(lax.rem(me + i, devices)), device_id_type=MESH
        ),
    )
    down = lax.broadcasted_iota(jnp.int32, (rows, rows), 0)
    along = lax.broadcasted_iota(jnp.int32, (rows, rows), 1)
    rate = rates[...]
    by_row = dot(rate, (down <= along).astype(F32), precision=high)
    by_col = dot((down >= along).astype(F32), rate, COLS, precision=high)
    for i in range(steps):
        col[i] = by_col[:, i * pair : (i + 1) * pair]
        row[i] = by_row[i * pair : (i + 1) * pair, :]
    head = lax.broadcasted_iota(jnp.int32, (steps * pair, width), 0)
    lane = lax.broadcasted_iota(jnp.int32, (steps * pair, width), 1)
    ours = jnp.logical_and(lane >= head * size, lane < (head + 1) * size).astype(F32)
    last = jnp.broadcast_to(by_col[rows - 1 :, :], (8, steps * pair))
    total[...] = dot(last, ours, precision=high)
    listed_own = jnp.sum((listed[...] == me).astype(F32), axis=1, keepdims=True)
    listed_prev = jnp.sum((listed[...] == me - 1).astype(F32), axis=1, keepdims=True)
    key_at = lax.broadcasted_iota(jnp.int32, (1, 2 * rows), 1)
    times[...] = jnp.where(key_at < rows, listed_own, listed_prev)
    pl.semaphore_wait(barrier, devices - 1)

    after = lax.rem(me + 1, devices)
    before = lax.rem(me + devices - 1, devices)
    tokens_on = remote(tokens, prev, prev_sem.at[0], prev_sem.at[1], spot(after))
    tokens_on.start()

    def token_copy(c, n, where):
        at = gathered.at[span_of(c, rows, rows)]
        return remote(tokens if c is here else at, at, token_sem.at[0, n], token_sem.at[1, c], where)

    token_copies = [
        token_copy(here, 0, y_spot), token_copy(here, 1, core_spot), token_copy(here, 2, x_spot),
        token_copy(c_y, 3, core_spot), token_copy(c_x, 4, y_spot), token_copy(c_x, 5, core_spot),
        token_copy(c_xy, 6, core_spot),
    ]
    others_here = pl.ds(0, (plane - 1) * rows)
    token_copies[0].start()
    token_copies[1].start()

    for copy in weights:
        copy.wait()

    def project(i):
        cut = span_of(i, lanes, lanes)
        left = tokens[...]
        q[:, cut] = dot(left, w[0, :, cut]).astype(BF16)
        k[:, cut] = dot(left, w[1, :, cut]).astype(BF16)
        v[:, cut] = dot(left, w[2, :, cut]).astype(BF16)
        local[:, cut] = summary_of(
            lin_scale, size, q[:, cut], k[:, cut], v[:, cut], g[:, cut], col[i]
        )

    each(0, steps // 2, project)
    token_copies[2].start()
    each(steps // 2, steps, project)

    tile, wide = came.shape[1], came.shape[2]
    across = local.shape[0] // tile
    blocks = across * (width // wide)
    mine = lax.rem(me, blocks)
    base = me - mine

    def part_of(block):
        return span_of(lax.rem(block, across), tile, tile), span_of(block // across, wide, wide)

    one_row = pl.ds(0, 1)

    def send_states(i):
        there = lax.rem(me + i, devices)
        at = part_of(lax.rem(there, blocks))
        remote(
            total.at[one_row, at[1]], decay.at[me, one_row], carry_sem.at[0, 0],
            carry_sem.at[1, 0], spot(there),
        ).start()
        remote(
            local.at[at], came.at[me], carry_sem.at[0, 1], carry_sem.at[1, 1], spot(there)
        ).start()

    each(1, devices, send_states)
    others = pl.ds(0, devices - 1)
    all_sums = remote(
        decay.at[others, one_row], decay.at[others, one_row],
        carry_sem.at[0, 0], carry_sem.at[1, 0], spot(after),
    )
    all_states = remote(
        came.at[others], came.at[others], carry_sem.at[0, 1], carry_sem.at[1, 1], spot(after)
    )
    came[me] = local[part_of(mine)]
    decay[me] = total[:, part_of(mine)[1]]


    def plane_spot(c):
        return (c // 2, depth_at * 2 + lax.rem(c, 2))

    gathered[span_of(here, rows, rows), :] = tokens[...]

    tokens_on.wait()

    def owe_copy(i):
        return remote(owe.at[i], due.at[i], owe_sem.at[0, i], owe_sem.at[1, i], spot(before))

    def near(i):
        cut = span_of(i, lanes, lanes)
        pk = dot(prev[...], w[1, :, cut]).astype(BF16)
        pv = dot(prev[...], w[2, :, cut]).astype(BF16)
        values = near_pair(
            lin_scale, soft_scale, size, q[:, cut], k[:, cut], v[:, cut], g[:, cut], pk, pv,
            col[i], row[i], times[...],
        )
        for ref, value in zip((out, dq, own_k, own_v), values):
            ref[:, cut] = value
        owe[i] = values[4]
        owe_copy(i).start()

    each(0, steps // 2, near)

    all_sums.wait_recv()
    all_states.wait_recv()
    back_way = (lax.rem(mine, across) * tile) // size

    def scan(i, state):
        at = i + back_way * (devices - 1 - 2 * i)
        made[at] = state.astype(BF16)
        return jnp.exp(decay[at, :1, :]) * state + came[at].astype(F32)

    lax.fori_loop(0, devices, scan, jnp.zeros((tile, wide), F32))

    def send_carry(i):
        there = base + lax.rem(mine + i, blocks)
        remote(
            made.at[there], carry.at[part_of(mine)], carry_sem.at[0, 2], carry_sem.at[1, 2],
            spot(there),
        ).start()

    each(1, blocks, send_carry)

    def tokens_landed(c):
        token_copy(c, 0, y_spot).wait_recv()

    tokens_landed(c_y)
    token_copies[3].start()
    other_blocks = pl.ds(0, blocks - 1)
    all_carry = remote(
        came.at[other_blocks], came.at[other_blocks], carry_sem.at[0, 2], carry_sem.at[1, 2],
        spot(after),
    )
    carry[part_of(mine)] = made[me]
    each(steps // 2, steps - 1, near)
    tokens_landed(c_x)
    token_copies[4].start()
    token_copies[5].start()
    each(steps - 1, steps, near)
    all_carry.wait_recv()

    def delta_copy(c):
        return remote(
            packed.at[c], spread.at[span_of(here, rows, rows)], delta_sem.at[0],
            delta_sem.at[1], plane_spot(c),
        )

    def finish(i):
        cut = span_of(i, lanes, lanes)
        owe_copy(i).wait_recv()
        terms = state_terms(
            lin_scale, size, q[:, cut], k[:, cut], v[:, cut], g[:, cut], col[i],
            carry[:size, cut], carry[size:, cut],
        )
        layer[:, cut] = (out[:, cut] + terms[0]).astype(BF16)
        owed = due[i].astype(F32)
        deltas = [
            (dq[:, cut] + terms[1]).astype(BF16),
            (own_k[:, cut] + terms[2] + owed[:, :lanes]).astype(BF16),
            (own_v[:, cut] + terms[3] + owed[:, lanes:]).astype(BF16),
        ]
        for m in range(3):
            delta[m, :, cut] = deltas[m]
        for u in range(lanes // LANES):
            c = i * (lanes // LANES) + u
            for m in range(3):
                packed[c, :, m * LANES : (m + 1) * LANES] = deltas[m][:, u * LANES : (u + 1) * LANES]

            @pl.when(c != here)
            def _():
                delta_copy(c).start()

    each(0, steps, finish)
    spread[span_of(here, rows, rows), :] = packed[here]
    tokens_landed(c_xy)
    token_copies[6].start()

    def token_back(i):
        cut = span_of(i, lanes, lanes)
        back[:, cut] = (
            dot(delta[0], w[0, cut, :], COLS)
            + dot(delta[1], w[1, cut, :], COLS)
            + dot(delta[2], w[2, cut, :], COLS)
        ).astype(BF16)

    each(0, width // lanes // 2, token_back)

    for c in (here, c_x, c_y, c_xy):
        tokens_landed(c + core_step)
    all_deltas = remote(
        spread.at[others_here], spread.at[others_here], delta_sem.at[0], delta_sem.at[1],
        spot(after),
    )
    all_deltas.wait_recv()
    tall = width // depth
    in_block = max(1, lanes // tall)
    grads = (grad_q, grad_k, grad_v)
    other_parts = pl.ds(0, depth - 1)

    def depth_spot(d):
        return (group_at, d * 2 + x_at)

    def part_copy(m, d):
        return remote(
            part.at[m, span_of(d, tall, tall)], parts_in.at[m, depth_at], part_sem.at[0, m],
            part_sem.at[1, m], depth_spot(d),
        )

    def multiply(n):
        b = lax.rem(depth_at // in_block + n, width // lanes)
        cut = span_of(b, lanes, lanes)
        product = dot(gathered[:, cut], spread[...], ROWS).astype(BF16)
        for m in range(3):
            part[m, cut, :] = product[:, m * LANES : (m + 1) * LANES]
        for u in range(in_block):
            d = b * in_block + u

            @pl.when(d != depth_at)
            def _():
                part_copy(0, d).start()

    each(1, width // lanes + 1, multiply)
    each(width // lanes // 2, width // lanes, token_back)

    half = tall // 2
    ways = ((x_spot, c_x), (y_spot, c_y))
    pieces = ((0, 0, tall, 0), (1, 0, tall, 1), (2, 0, half, 0), (2, half, half, 1))

    def block(d, c, p):
        m, start, count, _ = pieces[p]
        down = pl.ds(pl.multiple_of(d * tall + start, 16), count)
        return grads[m].at[down, span_of(c, LANES, LANES)]

    def block_copy(d, c, p, leg, where):
        return remote(block(d, c, p), block(d, c, p), sent.at[p, leg], arrive.at[p, d, c], where)

    def hop_copy(d, p, way):
        to = depth_at + 1 - 2 * way
        return remote(
            block(d, here, p), block(d, here, p), hop_sem.at[p, way, d], arrive.at[p, d, here],
            depth_spot(to),
        )

    def landed(d, c, p):
        block_copy(d, c, p, 0, spot(after)).wait_recv()

    def hop(d, p, way, act):
        to = depth_at + 1 - 2 * way

        @pl.when(jnp.logical_and(to >= 0, to < depth))
        def _():
            act(hop_copy(d, p, way))

    def around(i, act):
        for way in range(2):
            d = depth_at - i * (1 - 2 * way)
            valid = jnp.logical_and(jnp.logical_and(d >= 0, d < depth), i >= way)

            @pl.when(valid)
            def _():
                act(d, way)

    def to_ways(d, p):
        one = pieces[p][3]
        block_copy(d, here, p, 0, ways[one][0]).start()
        block_copy(d, here, p, 1, ways[1 - one][0]).start()
        block_copy(d, here, p, 2, core_spot).start()

    def step(p, i):
        def act(d, way):
            landed(d, here, p)
            hop(d, p, way, lambda copy: copy.start())
            to_ways(d, p)

        around(i, act)

    def first_leg(p, i):
        one = pieces[p][3]

        def act(d, way):
            c = ways[one][1]
            landed(d, c, p)
            block_copy(d, c, p, 1, ways[1 - one][0]).start()
            block_copy(d, c, p, 2, core_spot).start()

        around(i, act)

    def second_leg(p, i):
        def act(d, way):
            for c in (ways[1 - pieces[p][3]][1], c_xy):
                landed(d, c, p)
                block_copy(d, c, p, 2, core_spot).start()

        around(i, act)

    all_parts = [
        remote(
            parts_in.at[m, other_parts], parts_in.at[m, other_parts], part_sem.at[0, m],
            part_sem.at[1, m], spot(after),
        )
        for m in range(3)
    ]

    def sum_parts(m):
        all_parts[m].wait_recv()
        if m < 2:
            each(1, depth, lambda i: part_copy(m + 1, lax.rem(depth_at + i, depth)).start())
        own = span_of(depth_at, tall, tall)
        parts_in[m, depth_at] = part[m, own, :]
        summed = lax.fori_loop(
            0, depth, lambda d, so_far: so_far + parts_in[m, d].astype(F32),
            jnp.zeros((tall, LANES), F32),
        )
        grads[m][own, span_of(here, LANES, LANES)] = (summed * norm).astype(BF16)
        for p, piece in enumerate(pieces):
            if piece[0] == m:
                for way in range(2):
                    hop(depth_at, p, way, lambda copy: copy.start())
                to_ways(depth_at, p)

    sum_parts(0)
    first_leg(0, 0)
    step(0, 1)
    sum_parts(1)
    first_leg(0, 1)
    second_leg(0, 0)
    step(0, 2)
    first_leg(1, 0)
    step(1, 1)
    sum_parts(2)

    def onward(n):
        for p, ahead in enumerate((2, 1, 0, 0)):
            i = n + ahead
            step(p, i)
            first_leg(p, i - 1)
            second_leg(p, i - 2)

    each(1, depth + 2, onward)

    def from_core(d):
        for p in range(len(pieces)):
            for c in (here, c_x, c_y, c_xy):
                landed(d, c + core_step, p)

    each(0, depth, from_core)

    tokens_on_rest = (all_sums, all_states, all_carry, all_deltas, *all_parts, *token_copies)
    for copy in tokens_on_rest:
        copy.wait_send()
    each(0, steps, lambda i: owe_copy(i).wait_send())
    for p, (m, _, count, _) in enumerate(pieces):
        for leg, columns in enumerate((1, 2, 4)):
            ref = grads[m].at[pl.ds(0, depth * count), pl.ds(0, columns * LANES)]
            remote(ref, ref, sent.at[p, leg], arrive.at[p, 0, 0], spot(after)).wait_send()

    def hops_left(i):
        def act(d, way):
            for p in range(len(pieces)):
                hop(d, p, way, lambda copy: copy.wait_send())

        around(i, act)

    each(1, depth, hops_left)
    for p in range(len(pieces)):
        for way in range(2):
            hop(depth_at, p, way, lambda copy: copy.wait_send())


def leave_kernel(*refs):
    count = len(refs) // 2
    sem = refs[-1]
    copies = [pltpu.make_async_copy(refs[i], refs[count + i], sem.at[i]) for i in range(count)]
    for copy in copies:
        copy.start()
    for copy in copies:
        copy.wait()


def shards(tokens, query_weight, key_weight, value_weight, log_decay, neighbour_blocks, cotangent):
    rows, width = tokens.shape
    heads = log_decay.shape[0]
    size = width // heads
    pair = 256 // size
    steps = heads // pair
    lanes = pair * size
    sizes = tuple(lax.axis_size(name) for name in AXES)
    devices = sizes[0] * sizes[1]
    tile = 16
    blocks = min(devices, 2 * size // tile * (width // LANES))
    part = width // (blocks // (2 * size // tile))
    plane, depth = 2 * sizes[0], sizes[1] // 2

    norm = 1.0 / math.sqrt(rows * devices)

    vmem = pl.BlockSpec(memory_space=pltpu.VMEM)
    hbm = pl.BlockSpec(memory_space=pltpu.HBM)
    semaphores = pltpu.SemaphoreType.DMA
    results = pl.pallas_call(
        functools.partial(layer_kernel, sizes, size, norm),
        in_specs=[vmem] * 4 + [hbm] * 3,
        out_specs=[vmem] * 5,
        out_shape=[pltpu.VMEM((rows, width), BF16)] * 2 + [pltpu.VMEM((width, width), BF16)] * 3,
        scratch_shapes=[
            pltpu.VMEM((3, width, width), BF16),
            pltpu.VMEM((1, 2 * rows), F32),
            pltpu.VMEM((rows, width), BF16),
            pltpu.VMEM((rows, width), BF16),
            pltpu.VMEM((rows, width), BF16),
            pltpu.VMEM((rows, width), BF16),
            pltpu.VMEM((2 * size, width), BF16),
            pltpu.VMEM((8, width), F32),
            pltpu.VMEM((steps, rows, pair), F32),
            pltpu.VMEM((steps, pair, rows), F32),
            pltpu.VMEM((devices, tile, part), BF16),
            pltpu.VMEM((devices, 8, part), F32),
            pltpu.VMEM((devices, tile, part), BF16),
            pltpu.VMEM((2 * size, width), BF16),
            pltpu.VMEM((rows, width), F32),
            pltpu.VMEM((rows, width), F32),
            pltpu.VMEM((rows, width), F32),
            pltpu.VMEM((rows, width), F32),
            pltpu.VMEM((steps, rows, 2 * lanes), BF16),
            pltpu.VMEM((steps, rows, 2 * lanes), BF16),
            pltpu.VMEM((3, rows, width), BF16),
            pltpu.VMEM((plane, rows, 3 * LANES), BF16),
            pltpu.VMEM((plane * rows, 3 * LANES), BF16),
            pltpu.VMEM((plane * rows, width), BF16),
            pltpu.VMEM((3, width, LANES), BF16),
            pltpu.VMEM((3, depth, width // depth, LANES), BF16),
            semaphores((3,)),
            semaphores((2,)),
            semaphores((2, 3)),
            semaphores((2, steps)),
            semaphores((2, plane)),
            semaphores((2,)),
            semaphores((2, 3)),
            semaphores((4, depth, plane)),
            semaphores((4, 3)),
            semaphores((4, 2, depth)),
        ],
        compiler_params=pltpu.CompilerParams(
            collective_id=0, has_side_effects=True, vmem_limit_bytes=57 * 2**20
        ),
        cost_estimate=pl.CostEstimate(flops=10**9, bytes_accessed=10**8, transcendentals=0),
    )(
        tokens, cotangent, neighbour_blocks, log_decay,
        *(pltpu.with_memory_space_constraint(x, pltpu.HBM) for x in (query_weight, key_weight, value_weight)),
    )
    return pl.pallas_call(
        leave_kernel,
        in_specs=[vmem] * len(results),
        out_specs=[hbm] * len(results),
        out_shape=[jax.ShapeDtypeStruct(x.shape, x.dtype) for x in results],
        scratch_shapes=[semaphores((len(results),))],
        compiler_params=pltpu.CompilerParams(vmem_limit_bytes=2**20),
        cost_estimate=pl.CostEstimate(flops=0, bytes_accessed=10**7, transcendentals=0),
    )(*(pltpu.with_memory_space_constraint(x, pltpu.VMEM) for x in results))


def solution(mesh):
    return jax.shard_map(
        shards,
        mesh=mesh,
        in_specs=(
            P(AXES, None),
            P(),
            P(),
            P(),
            P(None, AXES),
            P(AXES, None),
            P(AXES, None),
        ),
        out_specs=(P(AXES, None), P(AXES, None), P(), P(), P()),
        check_vma=False,
    )
```

```python
import functools
import math

import jax
import jax.numpy as jnp
from jax import lax
from jax.experimental import pallas as pl
from jax.experimental.pallas import tpu as pltpu
from jax.sharding import PartitionSpec as P

AXES = ("group", "span")
F32 = jnp.float32
BF16 = jnp.bfloat16
ROWS = (((0,), (0,)), ((), ()))
COLS = (((1,), (1,)), ((), ()))
MESH = pl.DeviceIdType.MESH
LANES = 128


def dot(a, b, dims=(((1,), (0,)), ((), ())), precision=None):
    return lax.dot_general(a, b, dims, precision=precision, preferred_element_type=F32)


def summary_of(lin_scale, size, q, k, v, g, col):
    heads = q.shape[1] // size
    states, grads = [], []
    for j in range(heads):
        cut = slice(j * size, (j + 1) * size)
        run = col[:, j : j + 1]
        fading = jnp.exp(run[run.shape[0] - 1 :, :] - run)
        weighted = (v[:, cut].astype(F32) * fading).astype(BF16)
        scaled = (g[:, cut].astype(F32) * jnp.exp(run)).astype(BF16)
        states.append(dot(k[:, cut], weighted, ROWS))
        grads.append(lin_scale * dot(q[:, cut], scaled, ROWS))
    return jnp.concatenate(
        [jnp.concatenate(states, axis=1), jnp.concatenate(grads, axis=1)], axis=0
    ).astype(BF16)


def near_pair(lin_scale, soft_scale, size, q, k, v, g, pk, pv, col, row, times):
    rows = q.shape[0]
    heads = q.shape[1] // size
    t = lax.broadcasted_iota(jnp.int32, (rows, rows), 0)
    s = lax.broadcasted_iota(jnp.int32, (rows, rows), 1)
    lower = t >= s
    outs, dqs, dkv, dvv = [], [], [], []
    for j in range(heads):
        cut = slice(j * size, (j + 1) * size)
        qh, gh = q[:, cut], g[:, cut]
        kh = jnp.concatenate([k[:, cut], pk[:, cut]], axis=0)
        vh = jnp.concatenate([v[:, cut], pv[:, cut]], axis=0)
        decay = jnp.where(
            lower, jnp.exp(jnp.minimum(col[:, j : j + 1] - row[j : j + 1, :], 0.0)), 0.0
        ) * lin_scale
        score = dot(qh, kh, COLS)
        grad = dot(gh, vh, COLS)
        logits = jnp.where(times > 0.0, score * soft_scale, -1e30)
        peak = jnp.max(logits, axis=1, keepdims=True)
        terms = jnp.exp(logits - peak) * times
        probs = terms / jnp.sum(terms, axis=1, keepdims=True)
        inner = jnp.sum(probs * grad, axis=1, keepdims=True)
        dlogit = probs * (grad - inner) * soft_scale
        mix = jnp.concatenate(
            [probs[:, :rows] + score[:, :rows] * decay, probs[:, rows:]], axis=1
        ).astype(BF16)
        dmix = jnp.concatenate(
            [dlogit[:, :rows] + grad[:, :rows] * decay, dlogit[:, rows:]], axis=1
        ).astype(BF16)
        outs.append(dot(mix, vh))
        dqs.append(dot(dmix, kh))
        dkv.append(dot(dmix, qh, ROWS))
        dvv.append(dot(mix, gh, ROWS))
    dk = jnp.concatenate(dkv, axis=1)
    dv = jnp.concatenate(dvv, axis=1)
    return (
        jnp.concatenate(outs, axis=1),
        jnp.concatenate(dqs, axis=1),
        dk[:rows],
        dv[:rows],
        jnp.concatenate([dk[rows:], dv[rows:]], axis=1).astype(BF16),
    )


def state_terms(lin_scale, size, q, k, v, g, col, state, later):
    heads = q.shape[1] // size
    outs, dqs, dks, dvs = [], [], [], []
    for j in range(heads):
        cut = slice(j * size, (j + 1) * size)
        run = col[:, j : j + 1]
        growth = lin_scale * jnp.exp(run)
        fading = jnp.exp(run[run.shape[0] - 1 :, :] - run)
        st, lt = state[:, cut], later[:, cut]
        outs.append(growth * dot(q[:, cut], st))
        dqs.append(growth * dot(g[:, cut], st, COLS))
        dks.append(fading * dot(v[:, cut], lt, COLS))
        dvs.append(fading * dot(k[:, cut], lt))
    return [jnp.concatenate(terms, axis=1) for terms in (outs, dqs, dks, dvs)]


def span_of(start, step, length):
    return pl.ds(pl.multiple_of(start * step, step), length)


def layer_kernel(
    sizes, size, norm,
    tokens, g, listed, rates, wq, wk, wv,
    layer, back, grads,
    w, times, q, k, v, prev, local, total, col, row,
    came, decay, made, carry, out, dq, own_k, own_v, owe, due, delta, packed,
    spread, gathered, part, parts_in,
    w_sem, prev_sem, carry_sem, owe_sem, token_sem, delta_sem, part_sem, arrive, sent, hop_sem,
):
    rows, width = tokens.shape
    steps, _, pair = col.shape
    lanes = pair * size
    devices, span = sizes[0] * sizes[1], sizes[1]
    group_at, span_at = lax.axis_index("group"), lax.axis_index("span")
    me = group_at * span + span_at
    depth_at, x_at = span_at // 2, lax.rem(span_at, 2)
    depth = span // 2
    plane = 2 * sizes[0]
    here = group_at * 2 + x_at
    core_at, y_at = lax.rem(group_at, 2), group_at // 2
    x_step, y_step, core_step = 1 - 2 * x_at, 4 * (1 - 2 * y_at), 2 * (1 - 2 * core_at)
    c_x, c_y = here + x_step, here + y_step
    c_xy = here + x_step + y_step
    x_spot = (group_at, span_at + x_step)
    y_spot = (group_at + 2 * (1 - 2 * y_at), span_at)
    core_spot = (group_at + 1 - 2 * core_at, span_at)
    lin_scale = 1.0 / (size * math.sqrt(rows))
    soft_scale = 1.0 / math.sqrt(size)
    high = lax.Precision.HIGHEST

    def spot(index):
        return (index // span, lax.rem(index, span))

    def remote(src, dst, send, recv, where):
        return pltpu.make_async_remote_copy(
            src_ref=src, dst_ref=dst, send_sem=send, recv_sem=recv,
            device_id=where, device_id_type=MESH,
        )

    def each(start, stop, act):
        def one(i, _):
            act(i)
            return 0

        lax.fori_loop(start, stop, one, 0)

    weights = [
        pltpu.make_async_copy(src, w.at[m], w_sem.at[m]) for m, src in enumerate((wq, wk, wv))
    ]
    for copy in weights:
        copy.start()
    barrier = pltpu.get_barrier_semaphore()
    each(
        1, devices,
        lambda i: pl.semaphore_signal(
            barrier, inc=1, device_id=spot(lax.rem(me + i, devices)), device_id_type=MESH
        ),
    )
    down = lax.broadcasted_iota(jnp.int32, (rows, rows), 0)
    along = lax.broadcasted_iota(jnp.int32, (rows, rows), 1)
    rate = rates[...]
    by_row = dot(rate, (down <= along).astype(F32), precision=high)
    by_col = dot((down >= along).astype(F32), rate, COLS, precision=high)
    for i in range(steps):
        col[i] = by_col[:, i * pair : (i + 1) * pair]
        row[i] = by_row[i * pair : (i + 1) * pair, :]
    head = lax.broadcasted_iota(jnp.int32, (steps * pair, width), 0)
    lane = lax.broadcasted_iota(jnp.int32, (steps * pair, width), 1)
    ours = jnp.logical_and(lane >= head * size, lane < (head + 1) * size).astype(F32)
    last = jnp.broadcast_to(by_col[rows - 1 :, :], (8, steps * pair))
    total[...] = dot(last, ours, precision=high)
    listed_own = jnp.sum((listed[...] == me).astype(F32), axis=1, keepdims=True)
    listed_prev = jnp.sum((listed[...] == me - 1).astype(F32), axis=1, keepdims=True)
    key_at = lax.broadcasted_iota(jnp.int32, (1, 2 * rows), 1)
    times[...] = jnp.where(key_at < rows, listed_own, listed_prev)
    pl.semaphore_wait(barrier, devices - 1)

    after = lax.rem(me + 1, devices)
    before = lax.rem(me + devices - 1, devices)
    tokens_on = remote(tokens, prev, prev_sem.at[0], prev_sem.at[1], spot(after))
    tokens_on.start()

    def token_copy(c, n, where):
        at = gathered.at[span_of(c, rows, rows)]
        return remote(tokens if c is here else at, at, token_sem.at[0, n], token_sem.at[1, c], where)

    token_copies = [
        token_copy(here, 0, y_spot), token_copy(here, 1, core_spot), token_copy(here, 2, x_spot),
        token_copy(c_y, 3, core_spot), token_copy(c_x, 4, y_spot), token_copy(c_x, 5, core_spot),
        token_copy(c_xy, 6, core_spot),
    ]
    others_here = pl.ds(0, (plane - 1) * rows)
    token_copies[0].start()
    token_copies[1].start()

    for copy in weights:
        copy.wait()

    def project(i):
        cut = span_of(i, lanes, lanes)
        left = tokens[...]
        q[:, cut] = dot(left, w[0, :, cut]).astype(BF16)
        k[:, cut] = dot(left, w[1, :, cut]).astype(BF16)
        v[:, cut] = dot(left, w[2, :, cut]).astype(BF16)
        local[:, cut] = summary_of(
            lin_scale, size, q[:, cut], k[:, cut], v[:, cut], g[:, cut], col[i]
        )

    each(0, steps // 2, project)
    token_copies[2].start()
    each(steps // 2, steps, project)

    tile, wide = came.shape[1], came.shape[2]
    across = local.shape[0] // tile
    blocks = across * (width // wide)
    mine = lax.rem(me, blocks)
    base = me - mine

    def part_of(block):
        return span_of(lax.rem(block, across), tile, tile), span_of(block // across, wide, wide)

    one_row = pl.ds(0, 1)

    def send_states(i):
        there = lax.rem(me + i, devices)
        at = part_of(lax.rem(there, blocks))
        remote(
            total.at[one_row, at[1]], decay.at[me, one_row], carry_sem.at[0, 0],
            carry_sem.at[1, 0], spot(there),
        ).start()
        remote(
            local.at[at], came.at[me], carry_sem.at[0, 1], carry_sem.at[1, 1], spot(there)
        ).start()

    each(1, devices, send_states)
    others = pl.ds(0, devices - 1)
    all_sums = remote(
        decay.at[others, one_row], decay.at[others, one_row],
        carry_sem.at[0, 0], carry_sem.at[1, 0], spot(after),
    )
    all_states = remote(
        came.at[others], came.at[others], carry_sem.at[0, 1], carry_sem.at[1, 1], spot(after)
    )
    came[me] = local[part_of(mine)]
    decay[me] = total[:, part_of(mine)[1]]


    def plane_spot(c):
        return (c // 2, depth_at * 2 + lax.rem(c, 2))

    gathered[span_of(here, rows, rows), :] = tokens[...]

    tokens_on.wait()

    def owe_copy(i):
        return remote(owe.at[i], due.at[i], owe_sem.at[0, i], owe_sem.at[1, i], spot(before))

    def near(i):
        cut = span_of(i, lanes, lanes)
        pk = dot(prev[...], w[1, :, cut]).astype(BF16)
        pv = dot(prev[...], w[2, :, cut]).astype(BF16)
        values = near_pair(
            lin_scale, soft_scale, size, q[:, cut], k[:, cut], v[:, cut], g[:, cut], pk, pv,
            col[i], row[i], times[...],
        )
        for ref, value in zip((out, dq, own_k, own_v), values):
            ref[:, cut] = value
        owe[i] = values[4]
        owe_copy(i).start()

    each(0, steps // 2, near)

    all_sums.wait_recv()
    all_states.wait_recv()
    back_way = (lax.rem(mine, across) * tile) // size

    def scan(i, state):
        at = i + back_way * (devices - 1 - 2 * i)
        made[at] = state.astype(BF16)
        return jnp.exp(decay[at, :1, :]) * state + came[at].astype(F32)

    lax.fori_loop(0, devices, scan, jnp.zeros((tile, wide), F32))

    def send_carry(i):
        there = base + lax.rem(mine + i, blocks)
        remote(
            made.at[there], carry.at[part_of(mine)], carry_sem.at[0, 2], carry_sem.at[1, 2],
            spot(there),
        ).start()

    each(1, blocks, send_carry)

    def tokens_landed(c):
        token_copy(c, 0, y_spot).wait_recv()

    tokens_landed(c_y)
    token_copies[3].start()
    other_blocks = pl.ds(0, blocks - 1)
    all_carry = remote(
        came.at[other_blocks], came.at[other_blocks], carry_sem.at[0, 2], carry_sem.at[1, 2],
        spot(after),
    )
    carry[part_of(mine)] = made[me]
    each(steps // 2, steps - 1, near)
    tokens_landed(c_x)
    token_copies[4].start()
    token_copies[5].start()
    each(steps - 1, steps, near)
    all_carry.wait_recv()

    def delta_copy(c):
        return remote(
            packed.at[c], spread.at[span_of(here, rows, rows)], delta_sem.at[0],
            delta_sem.at[1], plane_spot(c),
        )

    def finish(i):
        cut = span_of(i, lanes, lanes)
        owe_copy(i).wait_recv()
        terms = state_terms(
            lin_scale, size, q[:, cut], k[:, cut], v[:, cut], g[:, cut], col[i],
            carry[:size, cut], carry[size:, cut],
        )
        layer[:, cut] = (out[:, cut] + terms[0]).astype(BF16)
        owed = due[i].astype(F32)
        deltas = [
            (dq[:, cut] + terms[1]).astype(BF16),
            (own_k[:, cut] + terms[2] + owed[:, :lanes]).astype(BF16),
            (own_v[:, cut] + terms[3] + owed[:, lanes:]).astype(BF16),
        ]
        for m in range(3):
            delta[m, :, cut] = deltas[m]
        for u in range(lanes // LANES):
            c = i * (lanes // LANES) + u
            for m in range(3):
                packed[c, :, m * LANES : (m + 1) * LANES] = deltas[m][:, u * LANES : (u + 1) * LANES]

            @pl.when(c != here)
            def _():
                delta_copy(c).start()

    each(0, steps, finish)
    spread[span_of(here, rows, rows), :] = packed[here]
    tokens_landed(c_xy)
    token_copies[6].start()

    def token_back(i):
        cut = span_of(i, lanes, lanes)
        back[:, cut] = (
            dot(delta[0], w[0, cut, :], COLS)
            + dot(delta[1], w[1, cut, :], COLS)
            + dot(delta[2], w[2, cut, :], COLS)
        ).astype(BF16)

    each(0, width // lanes // 2, token_back)

    for c in (here, c_x, c_y, c_xy):
        tokens_landed(c + core_step)
    all_deltas = remote(
        spread.at[others_here], spread.at[others_here], delta_sem.at[0], delta_sem.at[1],
        spot(after),
    )
    all_deltas.wait_recv()
    tall = width // depth
    in_block = max(1, lanes // tall)
    half = tall // 2
    pieces = 6
    other_parts = pl.ds(0, depth - 1)

    def depth_spot(d):
        return (group_at, d * 2 + x_at)

    def piece_rows(p, d):
        return span_of(2 * d + lax.rem(p, 2), half, half)

    def part_copy(p, d):
        return remote(
            part.at[p // 2, piece_rows(p, d)], parts_in.at[p, depth_at], part_sem.at[0, p],
            part_sem.at[1, p], depth_spot(d),
        )

    def multiply(n):
        b = lax.rem(depth_at // in_block + n, width // lanes)
        cut = span_of(b, lanes, lanes)
        product = dot(gathered[:, cut], spread[...], ROWS).astype(BF16)
        for m in range(3):
            part[m, cut, :] = product[:, m * LANES : (m + 1) * LANES]
        for u in range(in_block):
            d = b * in_block + u

            @pl.when(d != depth_at)
            def _():
                part_copy(0, d).start()
                part_copy(1, d).start()

    each(1, width // lanes + 1, multiply)
    each(width // lanes // 2, width // lanes, token_back)

    def way_spot(which):
        return (group_at + which * 2 * (1 - 2 * y_at), span_at + (1 - which) * x_step)

    def way_columns(which):
        return here + which * y_step + (1 - which) * x_step

    def block(d, c, p):
        return grads.at[p // 2, piece_rows(p, d), span_of(c, LANES, LANES)]

    def block_copy(d, c, p, leg, where):
        return remote(block(d, c, p), block(d, c, p), sent.at[p, leg], arrive.at[p, d, c], where)

    def hop_copy(d, p, way):
        to = depth_at + 1 - 2 * way
        return remote(
            block(d, here, p), block(d, here, p), hop_sem.at[p, way, d], arrive.at[p, d, here],
            depth_spot(to),
        )

    def landed(d, c, p):
        block_copy(d, c, p, 0, spot(after)).wait_recv()

    def hop(d, p, way, act):
        to = depth_at + 1 - 2 * way

        @pl.when(jnp.logical_and(to >= 0, to < depth))
        def _():
            act(hop_copy(d, p, way))

    def around(i, act):
        for way in range(2):
            d = depth_at - i * (1 - 2 * way)
            valid = jnp.logical_and(jnp.logical_and(d >= 0, d < depth), i >= way)

            @pl.when(valid)
            def _():
                act(d, way)

    def to_ways(d, p):
        one = lax.rem(p, 2)
        block_copy(d, here, p, 0, way_spot(one)).start()
        block_copy(d, here, p, 1, way_spot(1 - one)).start()
        block_copy(d, here, p, 2, core_spot).start()

    def step(p, i):
        def act(d, way):
            landed(d, here, p)
            hop(d, p, way, lambda copy: copy.start())
            to_ways(d, p)

        around(i, act)

    def first_leg(p, i):
        one = lax.rem(p, 2)

        def act(d, way):
            c = way_columns(one)
            landed(d, c, p)
            block_copy(d, c, p, 1, way_spot(1 - one)).start()
            block_copy(d, c, p, 2, core_spot).start()

        around(i, act)

    def second_leg(p, i):
        def act(d, way):
            for c in (way_columns(1 - lax.rem(p, 2)), c_xy):
                landed(d, c, p)
                block_copy(d, c, p, 2, core_spot).start()

        around(i, act)

    def all_parts(p):
        return remote(
            parts_in.at[p, other_parts], parts_in.at[p, other_parts], part_sem.at[0, p],
            part_sem.at[1, p], spot(after),
        )

    def tick(p, i):
        step(p, i)
        first_leg(p, i - 1)
        second_leg(p, i - 2)

    def sum_piece(p):
        all_parts(p).wait_recv()

        @pl.when(p + 2 < pieces)
        def _():
            each(1, depth, lambda i: part_copy(p + 2, lax.rem(depth_at + i, depth)).start())

        own = piece_rows(p, depth_at)
        parts_in[p, depth_at] = part[p // 2, own, :]
        summed = lax.fori_loop(
            0, depth, lambda d, so_far: so_far + parts_in[p, d].astype(F32),
            jnp.zeros((half, LANES), F32),
        )
        grads[p // 2, own, span_of(here, LANES, LANES)] = (summed * norm).astype(BF16)
        for way in range(2):
            hop(depth_at, p, way, lambda copy: copy.start())
        to_ways(depth_at, p)
        each(0, p, lambda r: tick(r, p - r))

    each(0, pieces, sum_piece)
    each(1, depth + 2, lambda n: each(0, pieces, lambda p: tick(p, n + pieces - 1 - p)))

    def from_core(d):
        def one(p):
            for c in (here, c_x, c_y, c_xy):
                landed(d, c + core_step, p)

        each(0, pieces, one)

    each(0, depth, from_core)

    tokens_on_rest = (all_sums, all_states, all_carry, all_deltas, *token_copies)
    for copy in tokens_on_rest:
        copy.wait_send()
    each(0, steps, lambda i: owe_copy(i).wait_send())

    def pieces_left(p):
        all_parts(p).wait_send()
        for leg, columns in enumerate((1, 2, 4)):
            ref = grads.at[0, pl.ds(0, depth * half), pl.ds(0, columns * LANES)]
            remote(ref, ref, sent.at[p, leg], arrive.at[p, 0, 0], spot(after)).wait_send()

        def hops_left(i):
            def act(d, way):
                hop(d, p, way, lambda copy: copy.wait_send())

            around(i, act)

        each(1, depth, hops_left)
        for way in range(2):
            hop(depth_at, p, way, lambda copy: copy.wait_send())

    each(0, pieces, pieces_left)


def leave_kernel(layer, back, grads, *refs):
    outs, sem = refs[:-1], refs[-1]
    sources = (layer, back, *(grads.at[m] for m in range(3)))
    copies = [
        pltpu.make_async_copy(source, out, sem.at[i])
        for i, (source, out) in enumerate(zip(sources, outs))
    ]
    for copy in copies:
        copy.start()
    for copy in copies:
        copy.wait()


def shards(tokens, query_weight, key_weight, value_weight, log_decay, neighbour_blocks, cotangent):
    rows, width = tokens.shape
    heads = log_decay.shape[0]
    size = width // heads
    pair = 256 // size
    steps = heads // pair
    lanes = pair * size
    sizes = tuple(lax.axis_size(name) for name in AXES)
    devices = sizes[0] * sizes[1]
    tile = 16
    blocks = min(devices, 2 * size // tile * (width // LANES))
    part = width // (blocks // (2 * size // tile))
    plane, depth = 2 * sizes[0], sizes[1] // 2

    norm = 1.0 / math.sqrt(rows * devices)

    vmem = pl.BlockSpec(memory_space=pltpu.VMEM)
    hbm = pl.BlockSpec(memory_space=pltpu.HBM)
    semaphores = pltpu.SemaphoreType.DMA
    results = pl.pallas_call(
        functools.partial(layer_kernel, sizes, size, norm),
        in_specs=[vmem] * 4 + [hbm] * 3,
        out_specs=[vmem] * 3,
        out_shape=[pltpu.VMEM((rows, width), BF16)] * 2 + [pltpu.VMEM((3, width, width), BF16)],
        scratch_shapes=[
            pltpu.VMEM((3, width, width), BF16),
            pltpu.VMEM((1, 2 * rows), F32),
            pltpu.VMEM((rows, width), BF16),
            pltpu.VMEM((rows, width), BF16),
            pltpu.VMEM((rows, width), BF16),
            pltpu.VMEM((rows, width), BF16),
            pltpu.VMEM((2 * size, width), BF16),
            pltpu.VMEM((8, width), F32),
            pltpu.VMEM((steps, rows, pair), F32),
            pltpu.VMEM((steps, pair, rows), F32),
            pltpu.VMEM((devices, tile, part), BF16),
            pltpu.VMEM((devices, 8, part), F32),
            pltpu.VMEM((devices, tile, part), BF16),
            pltpu.VMEM((2 * size, width), BF16),
            pltpu.VMEM((rows, width), F32),
            pltpu.VMEM((rows, width), F32),
            pltpu.VMEM((rows, width), F32),
            pltpu.VMEM((rows, width), F32),
            pltpu.VMEM((steps, rows, 2 * lanes), BF16),
            pltpu.VMEM((steps, rows, 2 * lanes), BF16),
            pltpu.VMEM((3, rows, width), BF16),
            pltpu.VMEM((plane, rows, 3 * LANES), BF16),
            pltpu.VMEM((plane * rows, 3 * LANES), BF16),
            pltpu.VMEM((plane * rows, width), BF16),
            pltpu.VMEM((3, width, LANES), BF16),
            pltpu.VMEM((6, depth, width // depth // 2, LANES), BF16),
            semaphores((3,)),
            semaphores((2,)),
            semaphores((2, 3)),
            semaphores((2, steps)),
            semaphores((2, plane)),
            semaphores((2,)),
            semaphores((2, 6)),
            semaphores((6, depth, plane)),
            semaphores((6, 3)),
            semaphores((6, 2, depth)),
        ],
        compiler_params=pltpu.CompilerParams(
            collective_id=0, has_side_effects=True, vmem_limit_bytes=57 * 2**20
        ),
        cost_estimate=pl.CostEstimate(flops=10**9, bytes_accessed=10**8, transcendentals=0),
    )(
        tokens, cotangent, neighbour_blocks, log_decay,
        *(pltpu.with_memory_space_constraint(x, pltpu.HBM) for x in (query_weight, key_weight, value_weight)),
    )
    return pl.pallas_call(
        leave_kernel,
        in_specs=[vmem] * len(results),
        out_specs=[hbm] * 5,
        out_shape=[jax.ShapeDtypeStruct((rows, width), BF16)] * 2
        + [jax.ShapeDtypeStruct((width, width), BF16)] * 3,
        scratch_shapes=[semaphores((5,))],
        compiler_params=pltpu.CompilerParams(vmem_limit_bytes=2**20),
        cost_estimate=pl.CostEstimate(flops=0, bytes_accessed=10**7, transcendentals=0),
    )(*(pltpu.with_memory_space_constraint(x, pltpu.VMEM) for x in results))


def solution(mesh):
    return jax.shard_map(
        shards,
        mesh=mesh,
        in_specs=(
            P(AXES, None),
            P(),
            P(),
            P(),
            P(None, AXES),
            P(AXES, None),
            P(AXES, None),
        ),
        out_specs=(P(AXES, None), P(AXES, None), P(), P(), P()),
        check_vma=False,
    )
```

```python
import functools
import math

import jax
import jax.numpy as jnp
from jax import lax
from jax.experimental import pallas as pl
from jax.experimental.pallas import tpu as pltpu
from jax.sharding import PartitionSpec as P

AXES = ("group", "span")
F32 = jnp.float32
BF16 = jnp.bfloat16
ROWS = (((0,), (0,)), ((), ()))
COLS = (((1,), (1,)), ((), ()))
MESH = pl.DeviceIdType.MESH
LANES = 128


def dot(a, b, dims=(((1,), (0,)), ((), ())), precision=None):
    return lax.dot_general(a, b, dims, precision=precision, preferred_element_type=F32)


def summary_of(lin_scale, size, q, k, v, g, col):
    heads = q.shape[1] // size
    states, grads = [], []
    for j in range(heads):
        cut = slice(j * size, (j + 1) * size)
        run = col[:, j : j + 1]
        fading = jnp.exp(run[run.shape[0] - 1 :, :] - run)
        weighted = (v[:, cut].astype(F32) * fading).astype(BF16)
        scaled = (g[:, cut].astype(F32) * jnp.exp(run)).astype(BF16)
        states.append(dot(k[:, cut], weighted, ROWS))
        grads.append(lin_scale * dot(q[:, cut], scaled, ROWS))
    return jnp.concatenate(
        [jnp.concatenate(states, axis=1), jnp.concatenate(grads, axis=1)], axis=0
    ).astype(BF16)


def near_pair(lin_scale, soft_scale, size, q, k, v, g, pk, pv, col, row, times):
    rows = q.shape[0]
    heads = q.shape[1] // size
    t = lax.broadcasted_iota(jnp.int32, (rows, rows), 0)
    s = lax.broadcasted_iota(jnp.int32, (rows, rows), 1)
    lower = t >= s
    outs, dqs, dkv, dvv = [], [], [], []
    for j in range(heads):
        cut = slice(j * size, (j + 1) * size)
        qh, gh = q[:, cut], g[:, cut]
        kh = jnp.concatenate([k[:, cut], pk[:, cut]], axis=0)
        vh = jnp.concatenate([v[:, cut], pv[:, cut]], axis=0)
        decay = jnp.where(
            lower, jnp.exp(jnp.minimum(col[:, j : j + 1] - row[j : j + 1, :], 0.0)), 0.0
        ) * lin_scale
        score = dot(qh, kh, COLS)
        grad = dot(gh, vh, COLS)
        logits = jnp.where(times > 0.0, score * soft_scale, -1e30)
        peak = jnp.max(logits, axis=1, keepdims=True)
        terms = jnp.exp(logits - peak) * times
        probs = terms / jnp.sum(terms, axis=1, keepdims=True)
        inner = jnp.sum(probs * grad, axis=1, keepdims=True)
        dlogit = probs * (grad - inner) * soft_scale
        mix = jnp.concatenate(
            [probs[:, :rows] + score[:, :rows] * decay, probs[:, rows:]], axis=1
        ).astype(BF16)
        dmix = jnp.concatenate(
            [dlogit[:, :rows] + grad[:, :rows] * decay, dlogit[:, rows:]], axis=1
        ).astype(BF16)
        outs.append(dot(mix, vh))
        dqs.append(dot(dmix, kh))
        dkv.append(dot(dmix, qh, ROWS))
        dvv.append(dot(mix, gh, ROWS))
    dk = jnp.concatenate(dkv, axis=1)
    dv = jnp.concatenate(dvv, axis=1)
    return (
        jnp.concatenate(outs, axis=1),
        jnp.concatenate(dqs, axis=1),
        dk[:rows],
        dv[:rows],
        jnp.concatenate([dk[rows:], dv[rows:]], axis=1).astype(BF16),
    )


def query_terms(lin_scale, size, q, g, col, state):
    heads = q.shape[1] // size
    outs, dqs = [], []
    for j in range(heads):
        cut = slice(j * size, (j + 1) * size)
        growth = lin_scale * jnp.exp(col[:, j : j + 1])
        st = state[:, cut]
        outs.append(growth * dot(q[:, cut], st))
        dqs.append(growth * dot(g[:, cut], st, COLS))
    return jnp.concatenate(outs, axis=1), jnp.concatenate(dqs, axis=1)


def key_value_terms(size, k, v, col, later):
    heads = k.shape[1] // size
    dks, dvs = [], []
    for j in range(heads):
        cut = slice(j * size, (j + 1) * size)
        run = col[:, j : j + 1]
        fading = jnp.exp(run[run.shape[0] - 1 :, :] - run)
        lt = later[:, cut]
        dks.append(fading * dot(v[:, cut], lt, COLS))
        dvs.append(fading * dot(k[:, cut], lt))
    return jnp.concatenate(dks, axis=1), jnp.concatenate(dvs, axis=1)


def span_of(start, step, length):
    return pl.ds(pl.multiple_of(start * step, step), length)


def layer_kernel(
    sizes, size, norm,
    tokens, g, listed, rates, wq, wk, wv,
    layer, back, grad_q, grad_k, grad_v,
    w, times, q, k, v, prev, local, total, col, row,
    came, decay, made, carry, out, dq, own_k, own_v, owe, due, delta,
    packed_q, packed_kv, spread_q, spread_kv, gathered, part, parts_in,
    w_sem, prev_sem, carry_sem, owe_sem, token_sem, delta_sem, part_sem, arrive, sent, hop_sem,
):
    rows, width = tokens.shape
    steps, _, pair = col.shape
    lanes = pair * size
    devices, span = sizes[0] * sizes[1], sizes[1]
    group_at, span_at = lax.axis_index("group"), lax.axis_index("span")
    me = group_at * span + span_at
    depth_at, x_at = span_at // 2, lax.rem(span_at, 2)
    depth = span // 2
    plane = 2 * sizes[0]
    here = group_at * 2 + x_at
    core_at, y_at = lax.rem(group_at, 2), group_at // 2
    x_step, y_step, core_step = 1 - 2 * x_at, 4 * (1 - 2 * y_at), 2 * (1 - 2 * core_at)
    c_x, c_y = here + x_step, here + y_step
    c_xy = here + x_step + y_step
    x_spot = (group_at, span_at + x_step)
    y_spot = (group_at + 2 * (1 - 2 * y_at), span_at)
    core_spot = (group_at + 1 - 2 * core_at, span_at)
    lin_scale = 1.0 / (size * math.sqrt(rows))
    soft_scale = 1.0 / math.sqrt(size)
    high = lax.Precision.HIGHEST

    def spot(index):
        return (index // span, lax.rem(index, span))

    def remote(src, dst, send, recv, where):
        return pltpu.make_async_remote_copy(
            src_ref=src, dst_ref=dst, send_sem=send, recv_sem=recv,
            device_id=where, device_id_type=MESH,
        )

    def each(start, stop, act):
        def one(i, _):
            act(i)
            return 0

        lax.fori_loop(start, stop, one, 0)

    weights = [
        pltpu.make_async_copy(src, w.at[m], w_sem.at[m]) for m, src in enumerate((wq, wk, wv))
    ]
    for copy in weights:
        copy.start()
    barrier = pltpu.get_barrier_semaphore()
    each(
        1, devices,
        lambda i: pl.semaphore_signal(
            barrier, inc=1, device_id=spot(lax.rem(me + i, devices)), device_id_type=MESH
        ),
    )
    down = lax.broadcasted_iota(jnp.int32, (rows, rows), 0)
    along = lax.broadcasted_iota(jnp.int32, (rows, rows), 1)
    rate = rates[...]
    by_row = dot(rate, (down <= along).astype(F32), precision=high)
    by_col = dot((down >= along).astype(F32), rate, COLS, precision=high)
    for i in range(steps):
        col[i] = by_col[:, i * pair : (i + 1) * pair]
        row[i] = by_row[i * pair : (i + 1) * pair, :]
    head = lax.broadcasted_iota(jnp.int32, (steps * pair, width), 0)
    lane = lax.broadcasted_iota(jnp.int32, (steps * pair, width), 1)
    ours = jnp.logical_and(lane >= head * size, lane < (head + 1) * size).astype(F32)
    last = jnp.broadcast_to(by_col[rows - 1 :, :], (8, steps * pair))
    total[...] = dot(last, ours, precision=high)
    listed_own = jnp.sum((listed[...] == me).astype(F32), axis=1, keepdims=True)
    listed_prev = jnp.sum((listed[...] == me - 1).astype(F32), axis=1, keepdims=True)
    key_at = lax.broadcasted_iota(jnp.int32, (1, 2 * rows), 1)
    times[...] = jnp.where(key_at < rows, listed_own, listed_prev)
    pl.semaphore_wait(barrier, devices - 1)

    after = lax.rem(me + 1, devices)
    before = lax.rem(me + devices - 1, devices)
    tokens_on = remote(tokens, prev, prev_sem.at[0], prev_sem.at[1], spot(after))
    tokens_on.start()

    def token_copy(c, n, where):
        at = gathered.at[span_of(c, rows, rows)]
        return remote(tokens if c is here else at, at, token_sem.at[0, n], token_sem.at[1, c], where)

    token_copies = [
        token_copy(here, 0, y_spot), token_copy(here, 1, core_spot), token_copy(here, 2, x_spot),
        token_copy(c_y, 3, core_spot), token_copy(c_x, 4, y_spot), token_copy(c_x, 5, core_spot),
        token_copy(c_xy, 6, core_spot),
    ]
    others_here = pl.ds(0, (plane - 1) * rows)
    token_copies[0].start()
    token_copies[1].start()

    for copy in weights:
        copy.wait()

    def project(i):
        cut = span_of(i, lanes, lanes)
        left = tokens[...]
        q[:, cut] = dot(left, w[0, :, cut]).astype(BF16)
        k[:, cut] = dot(left, w[1, :, cut]).astype(BF16)
        v[:, cut] = dot(left, w[2, :, cut]).astype(BF16)
        local[:, cut] = summary_of(
            lin_scale, size, q[:, cut], k[:, cut], v[:, cut], g[:, cut], col[i]
        )

    each(0, steps // 2, project)
    token_copies[2].start()
    each(steps // 2, steps, project)

    tile, wide = came.shape[1], came.shape[2]
    across = local.shape[0] // tile
    blocks = across * (width // wide)
    mine = lax.rem(me, blocks)
    base = me - mine

    def part_of(block):
        return span_of(lax.rem(block, across), tile, tile), span_of(block // across, wide, wide)

    one_row = pl.ds(0, 1)

    def send_states(i):
        there = lax.rem(me + i, devices)
        at = part_of(lax.rem(there, blocks))
        remote(
            total.at[one_row, at[1]], decay.at[me, one_row], carry_sem.at[0, 0],
            carry_sem.at[1, 0], spot(there),
        ).start()
        remote(
            local.at[at], came.at[me], carry_sem.at[0, 1], carry_sem.at[1, 1], spot(there)
        ).start()

    each(1, devices, send_states)
    others = pl.ds(0, devices - 1)
    all_sums = remote(
        decay.at[others, one_row], decay.at[others, one_row],
        carry_sem.at[0, 0], carry_sem.at[1, 0], spot(after),
    )
    all_states = remote(
        came.at[others], came.at[others], carry_sem.at[0, 1], carry_sem.at[1, 1], spot(after)
    )
    came[me] = local[part_of(mine)]
    decay[me] = total[:, part_of(mine)[1]]


    def plane_spot(c):
        return (c // 2, depth_at * 2 + lax.rem(c, 2))

    gathered[span_of(here, rows, rows), :] = tokens[...]

    tokens_on.wait()

    def owe_copy(i):
        return remote(owe.at[i], due.at[i], owe_sem.at[0, i], owe_sem.at[1, i], spot(before))

    def near(i):
        cut = span_of(i, lanes, lanes)
        pk = dot(prev[...], w[1, :, cut]).astype(BF16)
        pv = dot(prev[...], w[2, :, cut]).astype(BF16)
        values = near_pair(
            lin_scale, soft_scale, size, q[:, cut], k[:, cut], v[:, cut], g[:, cut], pk, pv,
            col[i], row[i], times[...],
        )
        for ref, value in zip((out, dq, own_k, own_v), values):
            ref[:, cut] = value
        owe[i] = values[4]
        owe_copy(i).start()

    each(0, steps // 2, near)

    all_sums.wait_recv()
    all_states.wait_recv()
    back_way = (lax.rem(mine, across) * tile) // size

    def scan(i, state):
        at = i + back_way * (devices - 1 - 2 * i)
        made[at] = state.astype(BF16)
        return jnp.exp(decay[at, :1, :]) * state + came[at].astype(F32)

    lax.fori_loop(0, devices, scan, jnp.zeros((tile, wide), F32))

    def send_carry(i):
        there = base + lax.rem(mine + i, blocks)
        remote(
            made.at[there], carry.at[part_of(mine)], carry_sem.at[0, 2], carry_sem.at[1, 2],
            spot(there),
        ).start()

    each(1, blocks, send_carry)

    def tokens_landed(c):
        token_copy(c, 0, y_spot).wait_recv()

    tokens_landed(c_y)
    token_copies[3].start()
    other_blocks = pl.ds(0, blocks - 1)
    all_carry = remote(
        came.at[other_blocks], came.at[other_blocks], carry_sem.at[0, 2], carry_sem.at[1, 2],
        spot(after),
    )
    carry[part_of(mine)] = made[me]
    each(steps // 2, steps - 1, near)
    tokens_landed(c_x)
    token_copies[4].start()
    token_copies[5].start()
    each(steps - 1, steps, near)
    all_carry.wait_recv()

    share = (packed_q, packed_kv)
    spreads = (spread_q, spread_kv)

    def delta_copy(n, c):
        return remote(
            share[n].at[c], spreads[n].at[span_of(here, rows, rows)], delta_sem.at[0, n],
            delta_sem.at[1, n], plane_spot(c),
        )

    def hand_out(n, i, deltas):
        for u in range(lanes // LANES):
            c = i * (lanes // LANES) + u
            for m, value in enumerate(deltas):
                share[n][c, :, m * LANES : (m + 1) * LANES] = value[:, u * LANES : (u + 1) * LANES]

            @pl.when(c != here)
            def _():
                delta_copy(n, c).start()

    def finish_query(i):
        cut = span_of(i, lanes, lanes)
        terms = query_terms(lin_scale, size, q[:, cut], g[:, cut], col[i], carry[:size, cut])
        layer[:, cut] = (out[:, cut] + terms[0]).astype(BF16)
        value = (dq[:, cut] + terms[1]).astype(BF16)
        delta[0, :, cut] = value
        hand_out(0, i, (value,))

    def finish_key_value(i):
        cut = span_of(i, lanes, lanes)
        terms = key_value_terms(size, k[:, cut], v[:, cut], col[i], carry[size:, cut])
        owe_copy(i).wait_recv()
        owed = due[i].astype(F32)
        values = [
            (own_k[:, cut] + terms[0] + owed[:, :lanes]).astype(BF16),
            (own_v[:, cut] + terms[1] + owed[:, lanes:]).astype(BF16),
        ]
        for m in range(2):
            delta[1 + m, :, cut] = values[m]
        hand_out(1, i, values)

    each(0, steps, finish_query)
    tokens_landed(c_xy)
    token_copies[6].start()
    each(0, steps, finish_key_value)
    for n in range(2):
        spreads[n][span_of(here, rows, rows), :] = share[n][here]

    def token_back(i):
        cut = span_of(i, lanes, lanes)
        back[:, cut] = (
            dot(delta[0], w[0, cut, :], COLS)
            + dot(delta[1], w[1, cut, :], COLS)
            + dot(delta[2], w[2, cut, :], COLS)
        ).astype(BF16)


    for c in (here, c_x, c_y, c_xy):
        tokens_landed(c + core_step)
    all_deltas = [
        remote(
            spreads[n].at[others_here], spreads[n].at[others_here], delta_sem.at[0, n],
            delta_sem.at[1, n], spot(after),
        )
        for n in range(2)
    ]
    tall = width // depth
    in_block = max(1, lanes // tall)
    grads = (grad_q, grad_k, grad_v)
    other_parts = pl.ds(0, depth - 1)

    def depth_spot(d):
        return (group_at, d * 2 + x_at)

    def part_copy(m, d):
        return remote(
            part.at[m, span_of(d, tall, tall)], parts_in.at[m, depth_at], part_sem.at[0, m],
            part_sem.at[1, m], depth_spot(d),
        )

    def block_at(n):
        b = lax.rem(depth_at // in_block + n, width // lanes)
        return b, span_of(b, lanes, lanes)

    def multiply_query(n):
        b, cut = block_at(n)
        part[0, cut, :] = dot(gathered[:, cut], spread_q[...], ROWS).astype(BF16)
        for u in range(in_block):
            d = b * in_block + u

            @pl.when(d != depth_at)
            def _():
                part_copy(0, d).start()

    def multiply_key_value(n):
        _, cut = block_at(n)
        product = dot(gathered[:, cut], spread_kv[...], ROWS).astype(BF16)
        for m in range(2):
            part[1 + m, cut, :] = product[:, m * LANES : (m + 1) * LANES]

    all_deltas[0].wait_recv()
    each(1, width // lanes + 1, multiply_query)
    each(0, width // lanes // 2, token_back)
    all_deltas[1].wait_recv()
    each(1, width // lanes + 1, multiply_key_value)
    each(width // lanes // 2, width // lanes, token_back)

    half = tall // 2
    ways = ((x_spot, c_x), (y_spot, c_y))
    pieces = ((0, 0, tall, 0), (1, 0, tall, 1), (2, 0, half, 0), (2, half, half, 1))

    def block(d, c, p):
        m, start, count, _ = pieces[p]
        down = pl.ds(pl.multiple_of(d * tall + start, 16), count)
        return grads[m].at[down, span_of(c, LANES, LANES)]

    def block_copy(d, c, p, leg, where):
        return remote(block(d, c, p), block(d, c, p), sent.at[p, leg], arrive.at[p, d, c], where)

    def hop_copy(d, p, way):
        to = depth_at + 1 - 2 * way
        return remote(
            block(d, here, p), block(d, here, p), hop_sem.at[p, way, d], arrive.at[p, d, here],
            depth_spot(to),
        )

    def landed(d, c, p):
        block_copy(d, c, p, 0, spot(after)).wait_recv()

    def hop(d, p, way, act):
        to = depth_at + 1 - 2 * way

        @pl.when(jnp.logical_and(to >= 0, to < depth))
        def _():
            act(hop_copy(d, p, way))

    def around(i, act):
        for way in range(2):
            d = depth_at - i * (1 - 2 * way)
            valid = jnp.logical_and(jnp.logical_and(d >= 0, d < depth), i >= way)

            @pl.when(valid)
            def _():
                act(d, way)

    def to_ways(d, p):
        one = pieces[p][3]
        block_copy(d, here, p, 0, ways[one][0]).start()
        block_copy(d, here, p, 1, ways[1 - one][0]).start()
        block_copy(d, here, p, 2, core_spot).start()

    def step(p, i):
        def act(d, way):
            landed(d, here, p)
            hop(d, p, way, lambda copy: copy.start())
            to_ways(d, p)

        around(i, act)

    def first_leg(p, i):
        one = pieces[p][3]

        def act(d, way):
            c = ways[one][1]
            landed(d, c, p)
            block_copy(d, c, p, 1, ways[1 - one][0]).start()
            block_copy(d, c, p, 2, core_spot).start()

        around(i, act)

    def second_leg(p, i):
        def act(d, way):
            for c in (ways[1 - pieces[p][3]][1], c_xy):
                landed(d, c, p)
                block_copy(d, c, p, 2, core_spot).start()

        around(i, act)

    all_parts = [
        remote(
            parts_in.at[m, other_parts], parts_in.at[m, other_parts], part_sem.at[0, m],
            part_sem.at[1, m], spot(after),
        )
        for m in range(3)
    ]

    def sum_parts(m):
        all_parts[m].wait_recv()
        if m < 2:
            each(1, depth, lambda i: part_copy(m + 1, lax.rem(depth_at + i, depth)).start())
        own = span_of(depth_at, tall, tall)
        parts_in[m, depth_at] = part[m, own, :]
        summed = lax.fori_loop(
            0, depth, lambda d, so_far: so_far + parts_in[m, d].astype(F32),
            jnp.zeros((tall, LANES), F32),
        )
        grads[m][own, span_of(here, LANES, LANES)] = (summed * norm).astype(BF16)
        for p, piece in enumerate(pieces):
            if piece[0] == m:
                for way in range(2):
                    hop(depth_at, p, way, lambda copy: copy.start())
                to_ways(depth_at, p)

    sum_parts(0)
    first_leg(0, 0)
    step(0, 1)
    sum_parts(1)
    first_leg(0, 1)
    second_leg(0, 0)
    step(0, 2)
    first_leg(1, 0)
    step(1, 1)
    sum_parts(2)

    def onward(n):
        for p, ahead in enumerate((2, 1, 0, 0)):
            i = n + ahead
            step(p, i)
            first_leg(p, i - 1)
            second_leg(p, i - 2)

    each(1, depth + 2, onward)

    def from_core(d):
        for p in range(len(pieces)):
            for c in (here, c_x, c_y, c_xy):
                landed(d, c + core_step, p)

    each(0, depth, from_core)

    tokens_on_rest = (all_sums, all_states, all_carry, *all_deltas, *all_parts, *token_copies)
    for copy in tokens_on_rest:
        copy.wait_send()
    each(0, steps, lambda i: owe_copy(i).wait_send())
    for p, (m, _, count, _) in enumerate(pieces):
        for leg, columns in enumerate((1, 2, 4)):
            ref = grads[m].at[pl.ds(0, depth * count), pl.ds(0, columns * LANES)]
            remote(ref, ref, sent.at[p, leg], arrive.at[p, 0, 0], spot(after)).wait_send()

    def hops_left(i):
        def act(d, way):
            for p in range(len(pieces)):
                hop(d, p, way, lambda copy: copy.wait_send())

        around(i, act)

    each(1, depth, hops_left)
    for p in range(len(pieces)):
        for way in range(2):
            hop(depth_at, p, way, lambda copy: copy.wait_send())


def leave_kernel(*refs):
    count = len(refs) // 2
    sem = refs[-1]
    copies = [pltpu.make_async_copy(refs[i], refs[count + i], sem.at[i]) for i in range(count)]
    for copy in copies:
        copy.start()
    for copy in copies:
        copy.wait()


def shards(tokens, query_weight, key_weight, value_weight, log_decay, neighbour_blocks, cotangent):
    rows, width = tokens.shape
    heads = log_decay.shape[0]
    size = width // heads
    pair = 256 // size
    steps = heads // pair
    lanes = pair * size
    sizes = tuple(lax.axis_size(name) for name in AXES)
    devices = sizes[0] * sizes[1]
    tile = 16
    blocks = min(devices, 2 * size // tile * (width // LANES))
    part = width // (blocks // (2 * size // tile))
    plane, depth = 2 * sizes[0], sizes[1] // 2

    norm = 1.0 / math.sqrt(rows * devices)

    vmem = pl.BlockSpec(memory_space=pltpu.VMEM)
    hbm = pl.BlockSpec(memory_space=pltpu.HBM)
    semaphores = pltpu.SemaphoreType.DMA
    results = pl.pallas_call(
        functools.partial(layer_kernel, sizes, size, norm),
        in_specs=[vmem] * 4 + [hbm] * 3,
        out_specs=[vmem] * 5,
        out_shape=[pltpu.VMEM((rows, width), BF16)] * 2 + [pltpu.VMEM((width, width), BF16)] * 3,
        scratch_shapes=[
            pltpu.VMEM((3, width, width), BF16),
            pltpu.VMEM((1, 2 * rows), F32),
            pltpu.VMEM((rows, width), BF16),
            pltpu.VMEM((rows, width), BF16),
            pltpu.VMEM((rows, width), BF16),
            pltpu.VMEM((rows, width), BF16),
            pltpu.VMEM((2 * size, width), BF16),
            pltpu.VMEM((8, width), F32),
            pltpu.VMEM((steps, rows, pair), F32),
            pltpu.VMEM((steps, pair, rows), F32),
            pltpu.VMEM((devices, tile, part), BF16),
            pltpu.VMEM((devices, 8, part), F32),
            pltpu.VMEM((devices, tile, part), BF16),
            pltpu.VMEM((2 * size, width), BF16),
            pltpu.VMEM((rows, width), F32),
            pltpu.VMEM((rows, width), F32),
            pltpu.VMEM((rows, width), F32),
            pltpu.VMEM((rows, width), F32),
            pltpu.VMEM((steps, rows, 2 * lanes), BF16),
            pltpu.VMEM((steps, rows, 2 * lanes), BF16),
            pltpu.VMEM((3, rows, width), BF16),
            pltpu.VMEM((plane, rows, LANES), BF16),
            pltpu.VMEM((plane, rows, 2 * LANES), BF16),
            pltpu.VMEM((plane * rows, LANES), BF16),
            pltpu.VMEM((plane * rows, 2 * LANES), BF16),
            pltpu.VMEM((plane * rows, width), BF16),
            pltpu.VMEM((3, width, LANES), BF16),
            pltpu.VMEM((3, depth, width // depth, LANES), BF16),
            semaphores((3,)),
            semaphores((2,)),
            semaphores((2, 3)),
            semaphores((2, steps)),
            semaphores((2, plane)),
            semaphores((2, 2)),
            semaphores((2, 3)),
            semaphores((4, depth, plane)),
            semaphores((4, 3)),
            semaphores((4, 2, depth)),
        ],
        compiler_params=pltpu.CompilerParams(
            collective_id=0, has_side_effects=True, vmem_limit_bytes=57 * 2**20
        ),
        cost_estimate=pl.CostEstimate(flops=10**9, bytes_accessed=10**8, transcendentals=0),
    )(
        tokens, cotangent, neighbour_blocks, log_decay,
        *(pltpu.with_memory_space_constraint(x, pltpu.HBM) for x in (query_weight, key_weight, value_weight)),
    )
    return pl.pallas_call(
        leave_kernel,
        in_specs=[vmem] * len(results),
        out_specs=[hbm] * len(results),
        out_shape=[jax.ShapeDtypeStruct(x.shape, x.dtype) for x in results],
        scratch_shapes=[semaphores((len(results),))],
        compiler_params=pltpu.CompilerParams(vmem_limit_bytes=2**20),
        cost_estimate=pl.CostEstimate(flops=0, bytes_accessed=10**7, transcendentals=0),
    )(*(pltpu.with_memory_space_constraint(x, pltpu.VMEM) for x in results))


def solution(mesh):
    return jax.shard_map(
        shards,
        mesh=mesh,
        in_specs=(
            P(AXES, None),
            P(),
            P(),
            P(),
            P(None, AXES),
            P(AXES, None),
            P(AXES, None),
        ),
        out_specs=(P(AXES, None), P(AXES, None), P(), P(), P()),
        check_vma=False,
    )
```

```python
import functools
import math

import jax
import jax.numpy as jnp
from jax import lax
from jax.experimental import pallas as pl
from jax.experimental.pallas import tpu as pltpu
from jax.sharding import PartitionSpec as P

AXES = ("group", "span")
F32 = jnp.float32
BF16 = jnp.bfloat16
ROWS = (((0,), (0,)), ((), ()))
COLS = (((1,), (1,)), ((), ()))
MESH = pl.DeviceIdType.MESH
LANES = 128


def dot(a, b, dims=(((1,), (0,)), ((), ())), precision=None):
    return lax.dot_general(a, b, dims, precision=precision, preferred_element_type=F32)


def summary_of(lin_scale, size, q, k, v, g, col):
    heads = q.shape[1] // size
    states, grads = [], []
    for j in range(heads):
        cut = slice(j * size, (j + 1) * size)
        run = col[:, j : j + 1]
        fading = jnp.exp(run[run.shape[0] - 1 :, :] - run)
        weighted = (v[:, cut].astype(F32) * fading).astype(BF16)
        scaled = (g[:, cut].astype(F32) * jnp.exp(run)).astype(BF16)
        states.append(dot(k[:, cut], weighted, ROWS))
        grads.append(lin_scale * dot(q[:, cut], scaled, ROWS))
    return jnp.concatenate(
        [jnp.concatenate(states, axis=1), jnp.concatenate(grads, axis=1)], axis=0
    ).astype(BF16)


def near_pair(lin_scale, soft_scale, size, q, k, v, g, pk, pv, col, row, times):
    rows = q.shape[0]
    heads = q.shape[1] // size
    t = lax.broadcasted_iota(jnp.int32, (rows, rows), 0)
    s = lax.broadcasted_iota(jnp.int32, (rows, rows), 1)
    lower = t >= s
    outs, dqs, dkv, dvv = [], [], [], []
    for j in range(heads):
        cut = slice(j * size, (j + 1) * size)
        qh, gh = q[:, cut], g[:, cut]
        kh = jnp.concatenate([k[:, cut], pk[:, cut]], axis=0)
        vh = jnp.concatenate([v[:, cut], pv[:, cut]], axis=0)
        decay = jnp.where(
            lower, jnp.exp(jnp.minimum(col[:, j : j + 1] - row[j : j + 1, :], 0.0)), 0.0
        ) * lin_scale
        score = dot(qh, kh, COLS)
        grad = dot(gh, vh, COLS)
        logits = jnp.where(times > 0.0, score * soft_scale, -1e30)
        peak = jnp.max(logits, axis=1, keepdims=True)
        terms = jnp.exp(logits - peak) * times
        probs = terms / jnp.sum(terms, axis=1, keepdims=True)
        inner = jnp.sum(probs * grad, axis=1, keepdims=True)
        dlogit = probs * (grad - inner) * soft_scale
        mix = jnp.concatenate(
            [probs[:, :rows] + score[:, :rows] * decay, probs[:, rows:]], axis=1
        ).astype(BF16)
        dmix = jnp.concatenate(
            [dlogit[:, :rows] + grad[:, :rows] * decay, dlogit[:, rows:]], axis=1
        ).astype(BF16)
        outs.append(dot(mix, vh))
        dqs.append(dot(dmix, kh))
        dkv.append(dot(dmix, qh, ROWS))
        dvv.append(dot(mix, gh, ROWS))
    dk = jnp.concatenate(dkv, axis=1)
    dv = jnp.concatenate(dvv, axis=1)
    return (
        jnp.concatenate(outs, axis=1),
        jnp.concatenate(dqs, axis=1),
        dk[:rows],
        dv[:rows],
        jnp.concatenate([dk[rows:], dv[rows:]], axis=1).astype(BF16),
    )


def query_terms(lin_scale, size, q, g, col, state):
    heads = q.shape[1] // size
    outs, dqs = [], []
    for j in range(heads):
        cut = slice(j * size, (j + 1) * size)
        growth = lin_scale * jnp.exp(col[:, j : j + 1])
        st = state[:, cut]
        outs.append(growth * dot(q[:, cut], st))
        dqs.append(growth * dot(g[:, cut], st, COLS))
    return jnp.concatenate(outs, axis=1), jnp.concatenate(dqs, axis=1)


def key_value_terms(size, k, v, col, later):
    heads = k.shape[1] // size
    dks, dvs = [], []
    for j in range(heads):
        cut = slice(j * size, (j + 1) * size)
        run = col[:, j : j + 1]
        fading = jnp.exp(run[run.shape[0] - 1 :, :] - run)
        lt = later[:, cut]
        dks.append(fading * dot(v[:, cut], lt, COLS))
        dvs.append(fading * dot(k[:, cut], lt))
    return jnp.concatenate(dks, axis=1), jnp.concatenate(dvs, axis=1)


def span_of(start, step, length):
    return pl.ds(pl.multiple_of(start * step, step), length)


def layer_kernel(
    sizes, size, norm,
    tokens, g, listed, rates, wq, wk, wv,
    layer, back, grad_q, grad_k, grad_v,
    w, times, q, k, v, prev, local, total, col, row,
    came, decay, made, carry, out, dq, own_k, own_v, owe, due, delta,
    packed_q, packed_kv, spread_q, spread_kv, gathered, part, parts_in,
    w_sem, prev_sem, carry_sem, owe_sem, token_sem, delta_sem, part_sem, arrive, sent, hop_sem,
):
    rows, width = tokens.shape
    steps, _, pair = col.shape
    lanes = pair * size
    devices, span = sizes[0] * sizes[1], sizes[1]
    group_at, span_at = lax.axis_index("group"), lax.axis_index("span")
    me = group_at * span + span_at
    depth_at, x_at = span_at // 2, lax.rem(span_at, 2)
    depth = span // 2
    plane = 2 * sizes[0]
    here = group_at * 2 + x_at
    core_at, y_at = lax.rem(group_at, 2), group_at // 2
    x_step, y_step, core_step = 1 - 2 * x_at, 4 * (1 - 2 * y_at), 2 * (1 - 2 * core_at)
    c_x, c_y = here + x_step, here + y_step
    c_xy = here + x_step + y_step
    x_spot = (group_at, span_at + x_step)
    y_spot = (group_at + 2 * (1 - 2 * y_at), span_at)
    core_spot = (group_at + 1 - 2 * core_at, span_at)
    lin_scale = 1.0 / (size * math.sqrt(rows))
    soft_scale = 1.0 / math.sqrt(size)
    high = lax.Precision.HIGHEST

    def spot(index):
        return (index // span, lax.rem(index, span))

    def remote(src, dst, send, recv, where):
        return pltpu.make_async_remote_copy(
            src_ref=src, dst_ref=dst, send_sem=send, recv_sem=recv,
            device_id=where, device_id_type=MESH,
        )

    def each(start, stop, act):
        def one(i, _):
            act(i)
            return 0

        lax.fori_loop(start, stop, one, 0)

    weights = [
        pltpu.make_async_copy(src, w.at[m], w_sem.at[m]) for m, src in enumerate((wq, wk, wv))
    ]
    for copy in weights:
        copy.start()
    barrier = pltpu.get_barrier_semaphore()
    each(
        1, devices,
        lambda i: pl.semaphore_signal(
            barrier, inc=1, device_id=spot(lax.rem(me + i, devices)), device_id_type=MESH
        ),
    )
    down = lax.broadcasted_iota(jnp.int32, (rows, rows), 0)
    along = lax.broadcasted_iota(jnp.int32, (rows, rows), 1)
    rate = rates[...]
    by_row = dot(rate, (down <= along).astype(F32), precision=high)
    by_col = dot((down >= along).astype(F32), rate, COLS, precision=high)
    for i in range(steps):
        col[i] = by_col[:, i * pair : (i + 1) * pair]
        row[i] = by_row[i * pair : (i + 1) * pair, :]
    head = lax.broadcasted_iota(jnp.int32, (steps * pair, width), 0)
    lane = lax.broadcasted_iota(jnp.int32, (steps * pair, width), 1)
    ours = jnp.logical_and(lane >= head * size, lane < (head + 1) * size).astype(F32)
    last = jnp.broadcast_to(by_col[rows - 1 :, :], (8, steps * pair))
    total[...] = dot(last, ours, precision=high)
    listed_own = jnp.sum((listed[...] == me).astype(F32), axis=1, keepdims=True)
    listed_prev = jnp.sum((listed[...] == me - 1).astype(F32), axis=1, keepdims=True)
    key_at = lax.broadcasted_iota(jnp.int32, (1, 2 * rows), 1)
    times[...] = jnp.where(key_at < rows, listed_own, listed_prev)
    pl.semaphore_wait(barrier, devices - 1)

    after = lax.rem(me + 1, devices)
    before = lax.rem(me + devices - 1, devices)
    tokens_on = remote(tokens, prev, prev_sem.at[0], prev_sem.at[1], spot(after))
    tokens_on.start()

    def token_copy(c, n, where):
        at = gathered.at[span_of(c, rows, rows)]
        return remote(tokens if c is here else at, at, token_sem.at[0, n], token_sem.at[1, c], where)

    token_copies = [
        token_copy(here, 0, y_spot), token_copy(here, 1, core_spot), token_copy(here, 2, x_spot),
        token_copy(c_y, 3, core_spot), token_copy(c_x, 4, y_spot), token_copy(c_x, 5, core_spot),
        token_copy(c_xy, 6, core_spot),
    ]
    others_here = pl.ds(0, (plane - 1) * rows)
    token_copies[0].start()
    token_copies[1].start()

    tile, wide = came.shape[1], came.shape[2]
    across = local.shape[0] // tile
    blocks = across * (width // wide)
    mine = lax.rem(me, blocks)
    base = me - mine

    def part_of(block):
        return span_of(lax.rem(block, across), tile, tile), span_of(block // across, wide, wide)

    one_row = pl.ds(0, 1)

    def send_sums(i):
        there = lax.rem(me + i, devices)
        remote(
            total.at[one_row, part_of(lax.rem(there, blocks))[1]], decay.at[me, one_row],
            carry_sem.at[0, 0], carry_sem.at[1, 0], spot(there),
        ).start()

    each(1, devices, send_sums)

    for copy in weights:
        copy.wait()

    def project(i):
        cut = span_of(i, lanes, lanes)
        left = tokens[...]
        q[:, cut] = dot(left, w[0, :, cut]).astype(BF16)
        k[:, cut] = dot(left, w[1, :, cut]).astype(BF16)
        v[:, cut] = dot(left, w[2, :, cut]).astype(BF16)
        local[:, cut] = summary_of(
            lin_scale, size, q[:, cut], k[:, cut], v[:, cut], g[:, cut], col[i]
        )

    each(0, steps // 2, project)
    token_copies[2].start()
    each(steps // 2, steps, project)

    def send_states(i):
        there = lax.rem(me + i, devices)
        at = part_of(lax.rem(there, blocks))
        remote(
            local.at[at], came.at[me], carry_sem.at[0, 1], carry_sem.at[1, 1], spot(there)
        ).start()

    each(1, devices, send_states)
    others = pl.ds(0, devices - 1)
    all_sums = remote(
        decay.at[others, one_row], decay.at[others, one_row],
        carry_sem.at[0, 0], carry_sem.at[1, 0], spot(after),
    )
    all_states = remote(
        came.at[others], came.at[others], carry_sem.at[0, 1], carry_sem.at[1, 1], spot(after)
    )
    came[me] = local[part_of(mine)]
    decay[me] = total[:, part_of(mine)[1]]


    def plane_spot(c):
        return (c // 2, depth_at * 2 + lax.rem(c, 2))

    gathered[span_of(here, rows, rows), :] = tokens[...]

    tokens_on.wait()

    def owe_copy(i):
        return remote(owe.at[i], due.at[i], owe_sem.at[0, i], owe_sem.at[1, i], spot(before))

    def near(i):
        cut = span_of(i, lanes, lanes)
        pk = dot(prev[...], w[1, :, cut]).astype(BF16)
        pv = dot(prev[...], w[2, :, cut]).astype(BF16)
        values = near_pair(
            lin_scale, soft_scale, size, q[:, cut], k[:, cut], v[:, cut], g[:, cut], pk, pv,
            col[i], row[i], times[...],
        )
        for ref, value in zip((out, dq, own_k, own_v), values):
            ref[:, cut] = value
        owe[i] = values[4]
        owe_copy(i).start()

    each(0, steps // 2, near)

    all_sums.wait_recv()
    all_states.wait_recv()
    back_way = (lax.rem(mine, across) * tile) // size

    def scan(i, state):
        at = i + back_way * (devices - 1 - 2 * i)
        made[at] = state.astype(BF16)
        return jnp.exp(decay[at, :1, :]) * state + came[at].astype(F32)

    lax.fori_loop(0, devices, scan, jnp.zeros((tile, wide), F32))

    def send_carry(i):
        there = base + lax.rem(mine + i, blocks)
        remote(
            made.at[there], carry.at[part_of(mine)], carry_sem.at[0, 2], carry_sem.at[1, 2],
            spot(there),
        ).start()

    each(1, blocks, send_carry)

    def tokens_landed(c):
        token_copy(c, 0, y_spot).wait_recv()

    tokens_landed(c_y)
    token_copies[3].start()
    other_blocks = pl.ds(0, blocks - 1)
    all_carry = remote(
        came.at[other_blocks], came.at[other_blocks], carry_sem.at[0, 2], carry_sem.at[1, 2],
        spot(after),
    )
    carry[part_of(mine)] = made[me]
    each(steps // 2, steps - 1, near)
    tokens_landed(c_x)
    token_copies[4].start()
    token_copies[5].start()
    each(steps - 1, steps, near)
    all_carry.wait_recv()

    share = (packed_q, packed_kv)
    spreads = (spread_q, spread_kv)

    def delta_copy(n, c):
        return remote(
            share[n].at[c], spreads[n].at[span_of(here, rows, rows)], delta_sem.at[0, n],
            delta_sem.at[1, n], plane_spot(c),
        )

    def hand_out(n, i, deltas):
        for u in range(lanes // LANES):
            c = i * (lanes // LANES) + u
            for m, value in enumerate(deltas):
                share[n][c, :, m * LANES : (m + 1) * LANES] = value[:, u * LANES : (u + 1) * LANES]

            @pl.when(c != here)
            def _():
                delta_copy(n, c).start()

    def finish_query(i):
        cut = span_of(i, lanes, lanes)
        terms = query_terms(lin_scale, size, q[:, cut], g[:, cut], col[i], carry[:size, cut])
        layer[:, cut] = (out[:, cut] + terms[0]).astype(BF16)
        value = (dq[:, cut] + terms[1]).astype(BF16)
        delta[0, :, cut] = value
        hand_out(0, i, (value,))

    def finish_key_value(i):
        cut = span_of(i, lanes, lanes)
        terms = key_value_terms(size, k[:, cut], v[:, cut], col[i], carry[size:, cut])
        owe_copy(i).wait_recv()
        owed = due[i].astype(F32)
        values = [
            (own_k[:, cut] + terms[0] + owed[:, :lanes]).astype(BF16),
            (own_v[:, cut] + terms[1] + owed[:, lanes:]).astype(BF16),
        ]
        for m in range(2):
            delta[1 + m, :, cut] = values[m]
        hand_out(1, i, values)

    each(0, steps, finish_query)
    tokens_landed(c_xy)
    token_copies[6].start()
    each(0, steps, finish_key_value)
    for n in range(2):
        spreads[n][span_of(here, rows, rows), :] = share[n][here]

    def token_back(i):
        cut = span_of(i, lanes, lanes)
        back[:, cut] = (
            dot(delta[0], w[0, cut, :], COLS)
            + dot(delta[1], w[1, cut, :], COLS)
            + dot(delta[2], w[2, cut, :], COLS)
        ).astype(BF16)


    for c in (here, c_x, c_y, c_xy):
        tokens_landed(c + core_step)
    all_deltas = [
        remote(
            spreads[n].at[others_here], spreads[n].at[others_here], delta_sem.at[0, n],
            delta_sem.at[1, n], spot(after),
        )
        for n in range(2)
    ]
    tall = width // depth
    in_block = max(1, lanes // tall)
    grads = (grad_q, grad_k, grad_v)
    other_parts = pl.ds(0, depth - 1)

    def depth_spot(d):
        return (group_at, d * 2 + x_at)

    def part_copy(m, d):
        return remote(
            part.at[m, span_of(d, tall, tall)], parts_in.at[m, depth_at], part_sem.at[0, m],
            part_sem.at[1, m], depth_spot(d),
        )

    def block_at(n):
        b = lax.rem(depth_at // in_block + n, width // lanes)
        return b, span_of(b, lanes, lanes)

    def send_parts(m, b):
        for u in range(in_block):
            d = b * in_block + u

            @pl.when(d != depth_at)
            def _():
                part_copy(m, d).start()

    def multiply_query(n):
        b, cut = block_at(n)
        part[0, cut, :] = dot(gathered[:, cut], spread_q[...], ROWS).astype(BF16)
        send_parts(0, b)

    def multiply_key_value(n):
        b, cut = block_at(n)
        product = dot(gathered[:, cut], spread_kv[...], ROWS).astype(BF16)
        for m in range(2):
            part[1 + m, cut, :] = product[:, m * LANES : (m + 1) * LANES]
        send_parts(1, b)

    all_deltas[0].wait_recv()
    each(1, width // lanes + 1, multiply_query)
    each(0, width // lanes // 2, token_back)
    all_deltas[1].wait_recv()
    each(1, width // lanes + 1, multiply_key_value)
    each(width // lanes // 2, width // lanes, token_back)

    half = tall // 2
    ways = ((x_spot, c_x), (y_spot, c_y))
    pieces = ((0, 0, tall, 0), (1, 0, tall, 1), (2, 0, half, 0), (2, half, half, 1))

    def block(d, c, p):
        m, start, count, _ = pieces[p]
        down = pl.ds(pl.multiple_of(d * tall + start, 16), count)
        return grads[m].at[down, span_of(c, LANES, LANES)]

    def block_copy(d, c, p, leg, where):
        return remote(block(d, c, p), block(d, c, p), sent.at[p, leg], arrive.at[p, d, c], where)

    def hop_copy(d, p, way):
        to = depth_at + 1 - 2 * way
        return remote(
            block(d, here, p), block(d, here, p), hop_sem.at[p, way, d], arrive.at[p, d, here],
            depth_spot(to),
        )

    def landed(d, c, p):
        block_copy(d, c, p, 0, spot(after)).wait_recv()

    def hop(d, p, way, act):
        to = depth_at + 1 - 2 * way

        @pl.when(jnp.logical_and(to >= 0, to < depth))
        def _():
            act(hop_copy(d, p, way))

    def around(i, act):
        for way in range(2):
            d = depth_at - i * (1 - 2 * way)
            valid = jnp.logical_and(jnp.logical_and(d >= 0, d < depth), i >= way)

            @pl.when(valid)
            def _():
                act(d, way)

    def to_ways(d, p):
        one = pieces[p][3]
        block_copy(d, here, p, 0, ways[one][0]).start()
        block_copy(d, here, p, 1, ways[1 - one][0]).start()
        block_copy(d, here, p, 2, core_spot).start()

    def step(p, i):
        def act(d, way):
            landed(d, here, p)
            hop(d, p, way, lambda copy: copy.start())
            to_ways(d, p)

        around(i, act)

    def first_leg(p, i):
        one = pieces[p][3]

        def act(d, way):
            c = ways[one][1]
            landed(d, c, p)
            block_copy(d, c, p, 1, ways[1 - one][0]).start()
            block_copy(d, c, p, 2, core_spot).start()

        around(i, act)

    def second_leg(p, i):
        def act(d, way):
            for c in (ways[1 - pieces[p][3]][1], c_xy):
                landed(d, c, p)
                block_copy(d, c, p, 2, core_spot).start()

        around(i, act)

    all_parts = [
        remote(
            parts_in.at[m, other_parts], parts_in.at[m, other_parts], part_sem.at[0, m],
            part_sem.at[1, m], spot(after),
        )
        for m in range(3)
    ]

    def sum_parts(m):
        all_parts[m].wait_recv()
        if m == 0:
            each(1, depth, lambda i: part_copy(2, lax.rem(depth_at + i, depth)).start())
        own = span_of(depth_at, tall, tall)
        parts_in[m, depth_at] = part[m, own, :]
        summed = lax.fori_loop(
            0, depth, lambda d, so_far: so_far + parts_in[m, d].astype(F32),
            jnp.zeros((tall, LANES), F32),
        )
        grads[m][own, span_of(here, LANES, LANES)] = (summed * norm).astype(BF16)
        for p, piece in enumerate(pieces):
            if piece[0] == m:
                for way in range(2):
                    hop(depth_at, p, way, lambda copy: copy.start())
                to_ways(depth_at, p)

    sum_parts(0)
    first_leg(0, 0)
    step(0, 1)
    sum_parts(1)
    first_leg(0, 1)
    second_leg(0, 0)
    step(0, 2)
    first_leg(1, 0)
    step(1, 1)
    sum_parts(2)

    def onward(n):
        for p, ahead in enumerate((2, 1, 0, 0)):
            i = n + ahead
            step(p, i)
            first_leg(p, i - 1)
            second_leg(p, i - 2)

    each(1, depth + 2, onward)

    def from_core(d):
        for p in range(len(pieces)):
            for c in (here, c_x, c_y, c_xy):
                landed(d, c + core_step, p)

    each(0, depth, from_core)

    tokens_on_rest = (all_sums, all_states, all_carry, *all_deltas, *all_parts, *token_copies)
    for copy in tokens_on_rest:
        copy.wait_send()
    each(0, steps, lambda i: owe_copy(i).wait_send())
    for p, (m, _, count, _) in enumerate(pieces):
        for leg, columns in enumerate((1, 2, 4)):
            ref = grads[m].at[pl.ds(0, depth * count), pl.ds(0, columns * LANES)]
            remote(ref, ref, sent.at[p, leg], arrive.at[p, 0, 0], spot(after)).wait_send()

    def hops_left(i):
        def act(d, way):
            for p in range(len(pieces)):
                hop(d, p, way, lambda copy: copy.wait_send())

        around(i, act)

    each(1, depth, hops_left)
    for p in range(len(pieces)):
        for way in range(2):
            hop(depth_at, p, way, lambda copy: copy.wait_send())


def leave_kernel(*refs):
    count = len(refs) // 2
    sem = refs[-1]
    copies = [pltpu.make_async_copy(refs[i], refs[count + i], sem.at[i]) for i in range(count)]
    for copy in copies:
        copy.start()
    for copy in copies:
        copy.wait()


def shards(tokens, query_weight, key_weight, value_weight, log_decay, neighbour_blocks, cotangent):
    rows, width = tokens.shape
    heads = log_decay.shape[0]
    size = width // heads
    pair = 256 // size
    steps = heads // pair
    lanes = pair * size
    sizes = tuple(lax.axis_size(name) for name in AXES)
    devices = sizes[0] * sizes[1]
    tile = 16
    blocks = min(devices, 2 * size // tile * (width // LANES))
    part = width // (blocks // (2 * size // tile))
    plane, depth = 2 * sizes[0], sizes[1] // 2

    norm = 1.0 / math.sqrt(rows * devices)

    vmem = pl.BlockSpec(memory_space=pltpu.VMEM)
    hbm = pl.BlockSpec(memory_space=pltpu.HBM)
    semaphores = pltpu.SemaphoreType.DMA
    results = pl.pallas_call(
        functools.partial(layer_kernel, sizes, size, norm),
        in_specs=[vmem] * 4 + [hbm] * 3,
        out_specs=[vmem] * 5,
        out_shape=[pltpu.VMEM((rows, width), BF16)] * 2 + [pltpu.VMEM((width, width), BF16)] * 3,
        scratch_shapes=[
            pltpu.VMEM((3, width, width), BF16),
            pltpu.VMEM((1, 2 * rows), F32),
            pltpu.VMEM((rows, width), BF16),
            pltpu.VMEM((rows, width), BF16),
            pltpu.VMEM((rows, width), BF16),
            pltpu.VMEM((rows, width), BF16),
            pltpu.VMEM((2 * size, width), BF16),
            pltpu.VMEM((8, width), F32),
            pltpu.VMEM((steps, rows, pair), F32),
            pltpu.VMEM((steps, pair, rows), F32),
            pltpu.VMEM((devices, tile, part), BF16),
            pltpu.VMEM((devices, 8, part), F32),
            pltpu.VMEM((devices, tile, part), BF16),
            pltpu.VMEM((2 * size, width), BF16),
            pltpu.VMEM((rows, width), F32),
            pltpu.VMEM((rows, width), F32),
            pltpu.VMEM((rows, width), F32),
            pltpu.VMEM((rows, width), F32),
            pltpu.VMEM((steps, rows, 2 * lanes), BF16),
            pltpu.VMEM((steps, rows, 2 * lanes), BF16),
            pltpu.VMEM((3, rows, width), BF16),
            pltpu.VMEM((plane, rows, LANES), BF16),
            pltpu.VMEM((plane, rows, 2 * LANES), BF16),
            pltpu.VMEM((plane * rows, LANES), BF16),
            pltpu.VMEM((plane * rows, 2 * LANES), BF16),
            pltpu.VMEM((plane * rows, width), BF16),
            pltpu.VMEM((3, width, LANES), BF16),
            pltpu.VMEM((3, depth, width // depth, LANES), BF16),
            semaphores((3,)),
            semaphores((2,)),
            semaphores((2, 3)),
            semaphores((2, steps)),
            semaphores((2, plane)),
            semaphores((2, 2)),
            semaphores((2, 3)),
            semaphores((4, depth, plane)),
            semaphores((4, 3)),
            semaphores((4, 2, depth)),
        ],
        compiler_params=pltpu.CompilerParams(
            collective_id=0, has_side_effects=True, vmem_limit_bytes=57 * 2**20
        ),
        cost_estimate=pl.CostEstimate(flops=10**9, bytes_accessed=10**8, transcendentals=0),
    )(
        tokens, cotangent, neighbour_blocks, log_decay,
        *(pltpu.with_memory_space_constraint(x, pltpu.HBM) for x in (query_weight, key_weight, value_weight)),
    )
    return pl.pallas_call(
        leave_kernel,
        in_specs=[vmem] * len(results),
        out_specs=[hbm] * len(results),
        out_shape=[jax.ShapeDtypeStruct(x.shape, x.dtype) for x in results],
        scratch_shapes=[semaphores((len(results),))],
        compiler_params=pltpu.CompilerParams(vmem_limit_bytes=2**20),
        cost_estimate=pl.CostEstimate(flops=0, bytes_accessed=10**7, transcendentals=0),
    )(*(pltpu.with_memory_space_constraint(x, pltpu.VMEM) for x in results))


def solution(mesh):
    return jax.shard_map(
        shards,
        mesh=mesh,
        in_specs=(
            P(AXES, None),
            P(),
            P(),
            P(),
            P(None, AXES),
            P(AXES, None),
            P(AXES, None),
        ),
        out_specs=(P(AXES, None), P(AXES, None), P(), P(), P()),
        check_vma=False,
    )
```

```python
import functools
import math

import jax
import jax.numpy as jnp
from jax import lax
from jax.experimental import pallas as pl
from jax.experimental.pallas import tpu as pltpu
from jax.sharding import PartitionSpec as P

AXES = ("group", "span")
F32 = jnp.float32
BF16 = jnp.bfloat16
ROWS = (((0,), (0,)), ((), ()))
COLS = (((1,), (1,)), ((), ()))
MESH = pl.DeviceIdType.MESH
LANES = 128


def dot(a, b, dims=(((1,), (0,)), ((), ())), precision=None):
    return lax.dot_general(a, b, dims, precision=precision, preferred_element_type=F32)


def summary_of(lin_scale, size, q, k, v, g, col):
    heads = q.shape[1] // size
    states, grads = [], []
    for j in range(heads):
        cut = slice(j * size, (j + 1) * size)
        run = col[:, j : j + 1]
        fading = jnp.exp(run[run.shape[0] - 1 :, :] - run)
        weighted = (v[:, cut].astype(F32) * fading).astype(BF16)
        scaled = (g[:, cut].astype(F32) * jnp.exp(run)).astype(BF16)
        states.append(dot(k[:, cut], weighted, ROWS))
        grads.append(lin_scale * dot(q[:, cut], scaled, ROWS))
    return jnp.concatenate(
        [jnp.concatenate(states, axis=1), jnp.concatenate(grads, axis=1)], axis=0
    ).astype(BF16)


def near_pair(lin_scale, soft_scale, size, q, k, v, g, pk, pv, col, row, times):
    rows = q.shape[0]
    heads = q.shape[1] // size
    t = lax.broadcasted_iota(jnp.int32, (rows, rows), 0)
    s = lax.broadcasted_iota(jnp.int32, (rows, rows), 1)
    lower = t >= s
    outs, dqs, dkv, dvv = [], [], [], []
    for j in range(heads):
        cut = slice(j * size, (j + 1) * size)
        qh, gh = q[:, cut], g[:, cut]
        kh = jnp.concatenate([k[:, cut], pk[:, cut]], axis=0)
        vh = jnp.concatenate([v[:, cut], pv[:, cut]], axis=0)
        decay = jnp.where(
            lower, jnp.exp(jnp.minimum(col[:, j : j + 1] - row[j : j + 1, :], 0.0)), 0.0
        ) * lin_scale
        score = dot(qh, kh, COLS)
        grad = dot(gh, vh, COLS)
        logits = jnp.where(times > 0.0, score * soft_scale, -1e30)
        peak = jnp.max(logits, axis=1, keepdims=True)
        terms = jnp.exp(logits - peak) * times
        probs = terms / jnp.sum(terms, axis=1, keepdims=True)
        inner = jnp.sum(probs * grad, axis=1, keepdims=True)
        dlogit = probs * (grad - inner) * soft_scale
        mix = jnp.concatenate(
            [probs[:, :rows] + score[:, :rows] * decay, probs[:, rows:]], axis=1
        ).astype(BF16)
        dmix = jnp.concatenate(
            [dlogit[:, :rows] + grad[:, :rows] * decay, dlogit[:, rows:]], axis=1
        ).astype(BF16)
        outs.append(dot(mix, vh))
        dqs.append(dot(dmix, kh))
        dkv.append(dot(dmix, qh, ROWS))
        dvv.append(dot(mix, gh, ROWS))
    dk = jnp.concatenate(dkv, axis=1)
    dv = jnp.concatenate(dvv, axis=1)
    return (
        jnp.concatenate(outs, axis=1),
        jnp.concatenate(dqs, axis=1),
        dk[:rows],
        dv[:rows],
        jnp.concatenate([dk[rows:], dv[rows:]], axis=1).astype(BF16),
    )


def query_terms(lin_scale, size, q, g, col, state):
    heads = q.shape[1] // size
    outs, dqs = [], []
    for j in range(heads):
        cut = slice(j * size, (j + 1) * size)
        growth = lin_scale * jnp.exp(col[:, j : j + 1])
        st = state[:, cut]
        outs.append(growth * dot(q[:, cut], st))
        dqs.append(growth * dot(g[:, cut], st, COLS))
    return jnp.concatenate(outs, axis=1), jnp.concatenate(dqs, axis=1)


def key_value_terms(size, k, v, col, later):
    heads = k.shape[1] // size
    dks, dvs = [], []
    for j in range(heads):
        cut = slice(j * size, (j + 1) * size)
        run = col[:, j : j + 1]
        fading = jnp.exp(run[run.shape[0] - 1 :, :] - run)
        lt = later[:, cut]
        dks.append(fading * dot(v[:, cut], lt, COLS))
        dvs.append(fading * dot(k[:, cut], lt))
    return jnp.concatenate(dks, axis=1), jnp.concatenate(dvs, axis=1)


def span_of(start, step, length):
    return pl.ds(pl.multiple_of(start * step, step), length)


def layer_kernel(
    sizes, size, norm,
    tokens, g, listed, rates, wq, wk, wv,
    layer, back, grad_q, grad_k, grad_v,
    w, times, q, k, v, prev, local, total, col, row,
    came, decay, made, carry, out, dq, own_k, own_v, owe, due, delta,
    packed_q, packed_kv, spread_q, spread_kv, gathered, part, parts_in,
    w_sem, prev_sem, carry_sem, owe_sem, token_sem, delta_sem, part_sem, arrive, sent, hop_sem,
):
    rows, width = tokens.shape
    steps, _, pair = col.shape
    lanes = pair * size
    devices, span = sizes[0] * sizes[1], sizes[1]
    group_at, span_at = lax.axis_index("group"), lax.axis_index("span")
    me = group_at * span + span_at
    depth_at, x_at = span_at // 2, lax.rem(span_at, 2)
    depth = span // 2
    plane = 2 * sizes[0]
    here = group_at * 2 + x_at
    core_at, y_at = lax.rem(group_at, 2), group_at // 2
    x_step, y_step, core_step = 1 - 2 * x_at, 4 * (1 - 2 * y_at), 2 * (1 - 2 * core_at)
    c_x, c_y = here + x_step, here + y_step
    c_xy = here + x_step + y_step
    x_spot = (group_at, span_at + x_step)
    y_spot = (group_at + 2 * (1 - 2 * y_at), span_at)
    core_spot = (group_at + 1 - 2 * core_at, span_at)
    lin_scale = 1.0 / (size * math.sqrt(rows))
    soft_scale = 1.0 / math.sqrt(size)
    high = lax.Precision.HIGHEST

    def spot(index):
        return (index // span, lax.rem(index, span))

    def remote(src, dst, send, recv, where):
        return pltpu.make_async_remote_copy(
            src_ref=src, dst_ref=dst, send_sem=send, recv_sem=recv,
            device_id=where, device_id_type=MESH,
        )

    def each(start, stop, act):
        def one(i, _):
            act(i)
            return 0

        lax.fori_loop(start, stop, one, 0)

    weights = [
        pltpu.make_async_copy(src, w.at[m], w_sem.at[m]) for m, src in enumerate((wq, wk, wv))
    ]
    for copy in weights:
        copy.start()
    barrier = pltpu.get_barrier_semaphore()
    each(
        1, devices,
        lambda i: pl.semaphore_signal(
            barrier, inc=1, device_id=spot(lax.rem(me + i, devices)), device_id_type=MESH
        ),
    )
    down = lax.broadcasted_iota(jnp.int32, (rows, rows), 0)
    along = lax.broadcasted_iota(jnp.int32, (rows, rows), 1)
    rate = rates[...]
    by_row = dot(rate, (down <= along).astype(F32), precision=high)
    by_col = dot((down >= along).astype(F32), rate, COLS, precision=high)
    for i in range(steps):
        col[i] = by_col[:, i * pair : (i + 1) * pair]
        row[i] = by_row[i * pair : (i + 1) * pair, :]
    head = lax.broadcasted_iota(jnp.int32, (steps * pair, width), 0)
    lane = lax.broadcasted_iota(jnp.int32, (steps * pair, width), 1)
    ours = jnp.logical_and(lane >= head * size, lane < (head + 1) * size).astype(F32)
    last = jnp.broadcast_to(by_col[rows - 1 :, :], (8, steps * pair))
    total[...] = dot(last, ours, precision=high)
    listed_own = jnp.sum((listed[...] == me).astype(F32), axis=1, keepdims=True)
    listed_prev = jnp.sum((listed[...] == me - 1).astype(F32), axis=1, keepdims=True)
    key_at = lax.broadcasted_iota(jnp.int32, (1, 2 * rows), 1)
    times[...] = jnp.where(key_at < rows, listed_own, listed_prev)
    pl.semaphore_wait(barrier, devices - 1)

    after = lax.rem(me + 1, devices)
    before = lax.rem(me + devices - 1, devices)
    tokens_on = remote(tokens, prev, prev_sem.at[0], prev_sem.at[1], spot(after))
    tokens_on.start()

    def token_copy(c, n, where):
        at = gathered.at[span_of(c, rows, rows)]
        return remote(tokens if c is here else at, at, token_sem.at[0, n], token_sem.at[1, c], where)

    token_copies = [
        token_copy(here, 0, y_spot), token_copy(here, 1, core_spot), token_copy(here, 2, x_spot),
        token_copy(c_y, 3, core_spot), token_copy(c_x, 4, y_spot), token_copy(c_x, 5, core_spot),
        token_copy(c_xy, 6, core_spot),
    ]
    others_here = pl.ds(0, (plane - 1) * rows)
    token_copies[0].start()
    token_copies[1].start()

    tile, wide = came.shape[1], came.shape[2]
    across = local.shape[0] // tile
    blocks = across * (width // wide)
    mine = lax.rem(me, blocks)
    base = me - mine

    def part_of(block):
        return span_of(lax.rem(block, across), tile, tile), span_of(block // across, wide, wide)

    one_row = pl.ds(0, 1)

    def send_sums(i):
        there = lax.rem(me + i, devices)
        remote(
            total.at[one_row, part_of(lax.rem(there, blocks))[1]], decay.at[me, one_row],
            carry_sem.at[0, 0], carry_sem.at[1, 0], spot(there),
        ).start()

    each(1, devices, send_sums)

    for copy in weights:
        copy.wait()

    def project(i):
        cut = span_of(i, lanes, lanes)
        left = tokens[...]
        q[:, cut] = dot(left, w[0, :, cut]).astype(BF16)
        k[:, cut] = dot(left, w[1, :, cut]).astype(BF16)
        v[:, cut] = dot(left, w[2, :, cut]).astype(BF16)
        local[:, cut] = summary_of(
            lin_scale, size, q[:, cut], k[:, cut], v[:, cut], g[:, cut], col[i]
        )

    each(0, steps // 2, project)
    token_copies[2].start()
    each(steps // 2, steps, project)

    def send_states(i):
        there = lax.rem(me + i, devices)
        at = part_of(lax.rem(there, blocks))
        remote(
            local.at[at], came.at[me], carry_sem.at[0, 1], carry_sem.at[1, 1], spot(there)
        ).start()

    each(1, devices, send_states)
    others = pl.ds(0, devices - 1)
    all_sums = remote(
        decay.at[others, one_row], decay.at[others, one_row],
        carry_sem.at[0, 0], carry_sem.at[1, 0], spot(after),
    )
    all_states = remote(
        came.at[others], came.at[others], carry_sem.at[0, 1], carry_sem.at[1, 1], spot(after)
    )
    came[me] = local[part_of(mine)]
    decay[me] = total[:, part_of(mine)[1]]
    all_sums.wait_recv()
    decay[:, :1, :] = jnp.exp(decay[:, :1, :])


    def plane_spot(c):
        return (c // 2, depth_at * 2 + lax.rem(c, 2))

    gathered[span_of(here, rows, rows), :] = tokens[...]

    tokens_on.wait()

    def owe_copy(i):
        return remote(owe.at[i], due.at[i], owe_sem.at[0, i], owe_sem.at[1, i], spot(before))

    def near(i):
        cut = span_of(i, lanes, lanes)
        pk = dot(prev[...], w[1, :, cut]).astype(BF16)
        pv = dot(prev[...], w[2, :, cut]).astype(BF16)
        values = near_pair(
            lin_scale, soft_scale, size, q[:, cut], k[:, cut], v[:, cut], g[:, cut], pk, pv,
            col[i], row[i], times[...],
        )
        for ref, value in zip((out, dq, own_k, own_v), values):
            ref[:, cut] = value
        owe[i] = values[4]

    each(0, steps // 2, near)

    all_states.wait_recv()
    back_way = (lax.rem(mine, across) * tile) // size

    def scan(i, state):
        at = i + back_way * (devices - 1 - 2 * i)
        made[at] = state.astype(BF16)
        return decay[at, :1, :] * state + came[at].astype(F32)

    lax.fori_loop(0, devices, scan, jnp.zeros((tile, wide), F32), unroll=8)

    def send_carry(i):
        there = base + lax.rem(mine + i, blocks)
        remote(
            made.at[there], carry.at[part_of(mine)], carry_sem.at[0, 2], carry_sem.at[1, 2],
            spot(there),
        ).start()

    each(1, blocks, send_carry)
    each(0, steps // 2, lambda i: owe_copy(i).start())

    def tokens_landed(c):
        token_copy(c, 0, y_spot).wait_recv()

    tokens_landed(c_y)
    token_copies[3].start()
    other_blocks = pl.ds(0, blocks - 1)
    all_carry = remote(
        came.at[other_blocks], came.at[other_blocks], carry_sem.at[0, 2], carry_sem.at[1, 2],
        spot(after),
    )
    carry[part_of(mine)] = made[me]
    each(steps // 2, steps - 1, near)
    owe_copy(steps - 2).start()
    tokens_landed(c_x)
    token_copies[4].start()
    token_copies[5].start()
    each(steps - 1, steps, near)
    owe_copy(steps - 1).start()
    all_carry.wait_recv()

    share = (packed_q, packed_kv)
    spreads = (spread_q, spread_kv)

    def delta_copy(n, c):
        return remote(
            share[n].at[c], spreads[n].at[span_of(here, rows, rows)], delta_sem.at[0, n],
            delta_sem.at[1, n], plane_spot(c),
        )

    def hand_out(n, i, deltas):
        for u in range(lanes // LANES):
            c = i * (lanes // LANES) + u
            for m, value in enumerate(deltas):
                share[n][c, :, m * LANES : (m + 1) * LANES] = value[:, u * LANES : (u + 1) * LANES]

            @pl.when(c != here)
            def _():
                delta_copy(n, c).start()

    def finish_query(i):
        cut = span_of(i, lanes, lanes)
        terms = query_terms(lin_scale, size, q[:, cut], g[:, cut], col[i], carry[:size, cut])
        layer[:, cut] = (out[:, cut] + terms[0]).astype(BF16)
        value = (dq[:, cut] + terms[1]).astype(BF16)
        delta[0, :, cut] = value
        hand_out(0, i, (value,))

    def finish_key_value(i):
        cut = span_of(i, lanes, lanes)
        terms = key_value_terms(size, k[:, cut], v[:, cut], col[i], carry[size:, cut])
        owe_copy(i).wait_recv()
        owed = due[i].astype(F32)
        values = [
            (own_k[:, cut] + terms[0] + owed[:, :lanes]).astype(BF16),
            (own_v[:, cut] + terms[1] + owed[:, lanes:]).astype(BF16),
        ]
        for m in range(2):
            delta[1 + m, :, cut] = values[m]
        hand_out(1, i, values)

    each(0, steps, finish_query)
    tokens_landed(c_xy)
    token_copies[6].start()
    each(0, steps, finish_key_value)
    for n in range(2):
        spreads[n][span_of(here, rows, rows), :] = share[n][here]

    def token_back(i):
        cut = span_of(i, lanes, lanes)
        back[:, cut] = (
            dot(delta[0], w[0, cut, :], COLS)
            + dot(delta[1], w[1, cut, :], COLS)
            + dot(delta[2], w[2, cut, :], COLS)
        ).astype(BF16)


    for c in (here, c_x, c_y, c_xy):
        tokens_landed(c + core_step)
    all_deltas = [
        remote(
            spreads[n].at[others_here], spreads[n].at[others_here], delta_sem.at[0, n],
            delta_sem.at[1, n], spot(after),
        )
        for n in range(2)
    ]
    tall = width // depth
    in_block = max(1, lanes // tall)
    grads = (grad_q, grad_k, grad_v)
    other_parts = pl.ds(0, depth - 1)

    def depth_spot(d):
        return (group_at, d * 2 + x_at)

    def part_copy(m, d):
        return remote(
            part.at[m, span_of(d, tall, tall)], parts_in.at[m, depth_at], part_sem.at[0, m],
            part_sem.at[1, m], depth_spot(d),
        )

    def block_at(n):
        b = lax.rem(depth_at // in_block + n, width // lanes)
        return b, span_of(b, lanes, lanes)

    def send_parts(m, b):
        for u in range(in_block):
            d = b * in_block + u

            @pl.when(d != depth_at)
            def _():
                part_copy(m, d).start()

    def multiply_query(n):
        b, cut = block_at(n)
        part[0, cut, :] = dot(gathered[:, cut], spread_q[...], ROWS).astype(BF16)
        send_parts(0, b)

    def multiply_key_value(n):
        b, cut = block_at(n)
        product = dot(gathered[:, cut], spread_kv[...], ROWS).astype(BF16)
        for m in range(2):
            part[1 + m, cut, :] = product[:, m * LANES : (m + 1) * LANES]
        send_parts(1, b)

    all_deltas[0].wait_recv()
    each(1, width // lanes + 1, multiply_query)
    each(0, width // lanes // 2, token_back)
    all_deltas[1].wait_recv()
    each(1, width // lanes + 1, multiply_key_value)
    each(width // lanes // 2, width // lanes, token_back)

    half = tall // 2
    ways = ((x_spot, c_x), (y_spot, c_y))
    pieces = ((0, 0, tall, 0), (1, 0, tall, 1), (2, 0, half, 0), (2, half, half, 1))

    def block(d, c, p):
        m, start, count, _ = pieces[p]
        down = pl.ds(pl.multiple_of(d * tall + start, 16), count)
        return grads[m].at[down, span_of(c, LANES, LANES)]

    def block_copy(d, c, p, leg, where):
        return remote(block(d, c, p), block(d, c, p), sent.at[p, leg], arrive.at[p, d, c], where)

    def hop_copy(d, p, way):
        to = depth_at + 1 - 2 * way
        return remote(
            block(d, here, p), block(d, here, p), hop_sem.at[p, way, d], arrive.at[p, d, here],
            depth_spot(to),
        )

    def landed(d, c, p):
        block_copy(d, c, p, 0, spot(after)).wait_recv()

    def hop(d, p, way, act):
        to = depth_at + 1 - 2 * way

        @pl.when(jnp.logical_and(to >= 0, to < depth))
        def _():
            act(hop_copy(d, p, way))

    def around(i, act):
        for way in range(2):
            d = depth_at - i * (1 - 2 * way)
            valid = jnp.logical_and(jnp.logical_and(d >= 0, d < depth), i >= way)

            @pl.when(valid)
            def _():
                act(d, way)

    def to_ways(d, p):
        one = pieces[p][3]
        block_copy(d, here, p, 0, ways[one][0]).start()
        block_copy(d, here, p, 1, ways[1 - one][0]).start()
        block_copy(d, here, p, 2, core_spot).start()

    def step(p, i):
        def act(d, way):
            landed(d, here, p)
            hop(d, p, way, lambda copy: copy.start())
            to_ways(d, p)

        around(i, act)

    def first_leg(p, i):
        one = pieces[p][3]

        def act(d, way):
            c = ways[one][1]
            landed(d, c, p)
            block_copy(d, c, p, 1, ways[1 - one][0]).start()
            block_copy(d, c, p, 2, core_spot).start()

        around(i, act)

    def second_leg(p, i):
        def act(d, way):
            for c in (ways[1 - pieces[p][3]][1], c_xy):
                landed(d, c, p)
                block_copy(d, c, p, 2, core_spot).start()

        around(i, act)

    all_parts = [
        remote(
            parts_in.at[m, other_parts], parts_in.at[m, other_parts], part_sem.at[0, m],
            part_sem.at[1, m], spot(after),
        )
        for m in range(3)
    ]

    def sum_parts(m):
        all_parts[m].wait_recv()
        if m == 0:
            each(1, depth, lambda i: part_copy(2, lax.rem(depth_at + i, depth)).start())
        own = span_of(depth_at, tall, tall)
        parts_in[m, depth_at] = part[m, own, :]
        summed = lax.fori_loop(
            0, depth, lambda d, so_far: so_far + parts_in[m, d].astype(F32),
            jnp.zeros((tall, LANES), F32),
        )
        grads[m][own, span_of(here, LANES, LANES)] = (summed * norm).astype(BF16)
        for p, piece in enumerate(pieces):
            if piece[0] == m:
                for way in range(2):
                    hop(depth_at, p, way, lambda copy: copy.start())
                to_ways(depth_at, p)

    sum_parts(0)
    first_leg(0, 0)
    step(0, 1)
    sum_parts(1)
    first_leg(0, 1)
    second_leg(0, 0)
    step(0, 2)
    first_leg(1, 0)
    step(1, 1)
    sum_parts(2)

    def onward(n):
        for p, ahead in enumerate((2, 1, 0, 0)):
            i = n + ahead
            step(p, i)
            first_leg(p, i - 1)
            second_leg(p, i - 2)

    each(1, depth + 2, onward)

    def from_core(d):
        for p in range(len(pieces)):
            for c in (here, c_x, c_y, c_xy):
                landed(d, c + core_step, p)

    each(0, depth, from_core)

    tokens_on_rest = (all_sums, all_states, all_carry, *all_deltas, *all_parts, *token_copies)
    for copy in tokens_on_rest:
        copy.wait_send()
    each(0, steps, lambda i: owe_copy(i).wait_send())
    for p, (m, _, count, _) in enumerate(pieces):
        for leg, columns in enumerate((1, 2, 4)):
            ref = grads[m].at[pl.ds(0, depth * count), pl.ds(0, columns * LANES)]
            remote(ref, ref, sent.at[p, leg], arrive.at[p, 0, 0], spot(after)).wait_send()

    def hops_left(i):
        def act(d, way):
            for p in range(len(pieces)):
                hop(d, p, way, lambda copy: copy.wait_send())

        around(i, act)

    each(1, depth, hops_left)
    for p in range(len(pieces)):
        for way in range(2):
            hop(depth_at, p, way, lambda copy: copy.wait_send())


def leave_kernel(*refs):
    count = len(refs) // 2
    sem = refs[-1]
    copies = [pltpu.make_async_copy(refs[i], refs[count + i], sem.at[i]) for i in range(count)]
    for copy in copies:
        copy.start()
    for copy in copies:
        copy.wait()


def shards(tokens, query_weight, key_weight, value_weight, log_decay, neighbour_blocks, cotangent):
    rows, width = tokens.shape
    heads = log_decay.shape[0]
    size = width // heads
    pair = 256 // size
    steps = heads // pair
    lanes = pair * size
    sizes = tuple(lax.axis_size(name) for name in AXES)
    devices = sizes[0] * sizes[1]
    tile = 16
    blocks = min(devices, 2 * size // tile * (width // LANES))
    part = width // (blocks // (2 * size // tile))
    plane, depth = 2 * sizes[0], sizes[1] // 2

    norm = 1.0 / math.sqrt(rows * devices)

    vmem = pl.BlockSpec(memory_space=pltpu.VMEM)
    hbm = pl.BlockSpec(memory_space=pltpu.HBM)
    semaphores = pltpu.SemaphoreType.DMA
    results = pl.pallas_call(
        functools.partial(layer_kernel, sizes, size, norm),
        in_specs=[vmem] * 4 + [hbm] * 3,
        out_specs=[vmem] * 5,
        out_shape=[pltpu.VMEM((rows, width), BF16)] * 2 + [pltpu.VMEM((width, width), BF16)] * 3,
        scratch_shapes=[
            pltpu.VMEM((3, width, width), BF16),
            pltpu.VMEM((1, 2 * rows), F32),
            pltpu.VMEM((rows, width), BF16),
            pltpu.VMEM((rows, width), BF16),
            pltpu.VMEM((rows, width), BF16),
            pltpu.VMEM((rows, width), BF16),
            pltpu.VMEM((2 * size, width), BF16),
            pltpu.VMEM((8, width), F32),
            pltpu.VMEM((steps, rows, pair), F32),
            pltpu.VMEM((steps, pair, rows), F32),
            pltpu.VMEM((devices, tile, part), BF16),
            pltpu.VMEM((devices, 8, part), F32),
            pltpu.VMEM((devices, tile, part), BF16),
            pltpu.VMEM((2 * size, width), BF16),
            pltpu.VMEM((rows, width), F32),
            pltpu.VMEM((rows, width), F32),
            pltpu.VMEM((rows, width), F32),
            pltpu.VMEM((rows, width), F32),
            pltpu.VMEM((steps, rows, 2 * lanes), BF16),
            pltpu.VMEM((steps, rows, 2 * lanes), BF16),
            pltpu.VMEM((3, rows, width), BF16),
            pltpu.VMEM((plane, rows, LANES), BF16),
            pltpu.VMEM((plane, rows, 2 * LANES), BF16),
            pltpu.VMEM((plane * rows, LANES), BF16),
            pltpu.VMEM((plane * rows, 2 * LANES), BF16),
            pltpu.VMEM((plane * rows, width), BF16),
            pltpu.VMEM((3, width, LANES), BF16),
            pltpu.VMEM((3, depth, width // depth, LANES), BF16),
            semaphores((3,)),
            semaphores((2,)),
            semaphores((2, 3)),
            semaphores((2, steps)),
            semaphores((2, plane)),
            semaphores((2, 2)),
            semaphores((2, 3)),
            semaphores((4, depth, plane)),
            semaphores((4, 3)),
            semaphores((4, 2, depth)),
        ],
        compiler_params=pltpu.CompilerParams(
            collective_id=0, has_side_effects=True, vmem_limit_bytes=57 * 2**20
        ),
        cost_estimate=pl.CostEstimate(flops=10**9, bytes_accessed=10**8, transcendentals=0),
    )(
        tokens, cotangent, neighbour_blocks, log_decay,
        *(pltpu.with_memory_space_constraint(x, pltpu.HBM) for x in (query_weight, key_weight, value_weight)),
    )
    return pl.pallas_call(
        leave_kernel,
        in_specs=[vmem] * len(results),
        out_specs=[hbm] * len(results),
        out_shape=[jax.ShapeDtypeStruct(x.shape, x.dtype) for x in results],
        scratch_shapes=[semaphores((len(results),))],
        compiler_params=pltpu.CompilerParams(vmem_limit_bytes=2**20),
        cost_estimate=pl.CostEstimate(flops=0, bytes_accessed=10**7, transcendentals=0),
    )(*(pltpu.with_memory_space_constraint(x, pltpu.VMEM) for x in results))


def solution(mesh):
    return jax.shard_map(
        shards,
        mesh=mesh,
        in_specs=(
            P(AXES, None),
            P(),
            P(),
            P(),
            P(None, AXES),
            P(AXES, None),
            P(AXES, None),
        ),
        out_specs=(P(AXES, None), P(AXES, None), P(), P(), P()),
        check_vma=False,
    )
```

```python
import functools
import math

import jax
import jax.numpy as jnp
from jax import lax
from jax.experimental import pallas as pl
from jax.experimental.pallas import tpu as pltpu
from jax.sharding import PartitionSpec as P

AXES = ("group", "span")
F32 = jnp.float32
BF16 = jnp.bfloat16
ROWS = (((0,), (0,)), ((), ()))
COLS = (((1,), (1,)), ((), ()))
MESH = pl.DeviceIdType.MESH
LANES = 128


def dot(a, b, dims=(((1,), (0,)), ((), ())), precision=None):
    return lax.dot_general(a, b, dims, precision=precision, preferred_element_type=F32)


def summary_of(lin_scale, size, q, k, v, g, col):
    heads = q.shape[1] // size
    states, grads = [], []
    for j in range(heads):
        cut = slice(j * size, (j + 1) * size)
        run = col[:, j : j + 1]
        fading = jnp.exp(run[run.shape[0] - 1 :, :] - run)
        weighted = (v[:, cut].astype(F32) * fading).astype(BF16)
        scaled = (g[:, cut].astype(F32) * jnp.exp(run)).astype(BF16)
        states.append(dot(k[:, cut], weighted, ROWS))
        grads.append(lin_scale * dot(q[:, cut], scaled, ROWS))
    return jnp.concatenate(
        [jnp.concatenate(states, axis=1), jnp.concatenate(grads, axis=1)], axis=0
    ).astype(BF16)


def near_pair(lin_scale, soft_scale, size, q, k, v, g, pk, pv, col, row, times):
    rows = q.shape[0]
    heads = q.shape[1] // size
    t = lax.broadcasted_iota(jnp.int32, (rows, rows), 0)
    s = lax.broadcasted_iota(jnp.int32, (rows, rows), 1)
    lower = t >= s
    outs, dqs, dkv, dvv = [], [], [], []
    for j in range(heads):
        cut = slice(j * size, (j + 1) * size)
        qh, gh = q[:, cut], g[:, cut]
        kh = jnp.concatenate([k[:, cut], pk[:, cut]], axis=0)
        vh = jnp.concatenate([v[:, cut], pv[:, cut]], axis=0)
        decay = jnp.where(
            lower, jnp.exp(jnp.minimum(col[:, j : j + 1] - row[j : j + 1, :], 0.0)), 0.0
        ) * lin_scale
        score = dot(qh, kh, COLS)
        grad = dot(gh, vh, COLS)
        logits = jnp.where(times > 0.0, score * soft_scale, -1e30)
        peak = jnp.max(logits, axis=1, keepdims=True)
        terms = jnp.exp(logits - peak) * times
        probs = terms / jnp.sum(terms, axis=1, keepdims=True)
        inner = jnp.sum(probs * grad, axis=1, keepdims=True)
        dlogit = probs * (grad - inner) * soft_scale
        mix = jnp.concatenate(
            [probs[:, :rows] + score[:, :rows] * decay, probs[:, rows:]], axis=1
        ).astype(BF16)
        dmix = jnp.concatenate(
            [dlogit[:, :rows] + grad[:, :rows] * decay, dlogit[:, rows:]], axis=1
        ).astype(BF16)
        outs.append(dot(mix, vh))
        dqs.append(dot(dmix, kh))
        dkv.append(dot(dmix, qh, ROWS))
        dvv.append(dot(mix, gh, ROWS))
    dk = jnp.concatenate(dkv, axis=1)
    dv = jnp.concatenate(dvv, axis=1)
    return (
        jnp.concatenate(outs, axis=1),
        jnp.concatenate(dqs, axis=1),
        dk[:rows],
        dv[:rows],
        jnp.concatenate([dk[rows:], dv[rows:]], axis=1).astype(BF16),
    )


def query_terms(lin_scale, size, q, g, col, state):
    heads = q.shape[1] // size
    outs, dqs = [], []
    for j in range(heads):
        cut = slice(j * size, (j + 1) * size)
        growth = lin_scale * jnp.exp(col[:, j : j + 1])
        st = state[:, cut]
        outs.append(growth * dot(q[:, cut], st))
        dqs.append(growth * dot(g[:, cut], st, COLS))
    return jnp.concatenate(outs, axis=1), jnp.concatenate(dqs, axis=1)


def key_value_terms(size, k, v, col, later):
    heads = k.shape[1] // size
    dks, dvs = [], []
    for j in range(heads):
        cut = slice(j * size, (j + 1) * size)
        run = col[:, j : j + 1]
        fading = jnp.exp(run[run.shape[0] - 1 :, :] - run)
        lt = later[:, cut]
        dks.append(fading * dot(v[:, cut], lt, COLS))
        dvs.append(fading * dot(k[:, cut], lt))
    return jnp.concatenate(dks, axis=1), jnp.concatenate(dvs, axis=1)


def span_of(start, step, length):
    return pl.ds(pl.multiple_of(start * step, step), length)


def layer_kernel(
    sizes, size, norm,
    tokens, g, listed, rates, wq, wk, wv,
    layer, back, grad_q, grad_k, grad_v,
    w, times, q, k, v, prev, local, total, col, row,
    came, decay, made, carry, out, dq, own_k, own_v, owe, due, delta,
    packed_q, packed_kv, spread_q, spread_kv, gathered, part, parts_in,
    w_sem, prev_sem, carry_sem, owe_sem, token_sem, delta_sem, part_sem, arrive, sent, hop_sem,
):
    rows, width = tokens.shape
    steps, _, pair = col.shape
    lanes = pair * size
    devices, span = sizes[0] * sizes[1], sizes[1]
    group_at, span_at = lax.axis_index("group"), lax.axis_index("span")
    me = group_at * span + span_at
    depth_at, x_at = span_at // 2, lax.rem(span_at, 2)
    depth = span // 2
    plane = 2 * sizes[0]
    here = group_at * 2 + x_at
    core_at, y_at = lax.rem(group_at, 2), group_at // 2
    x_step, y_step, core_step = 1 - 2 * x_at, 4 * (1 - 2 * y_at), 2 * (1 - 2 * core_at)
    c_x, c_y = here + x_step, here + y_step
    c_xy = here + x_step + y_step
    x_spot = (group_at, span_at + x_step)
    y_spot = (group_at + 2 * (1 - 2 * y_at), span_at)
    core_spot = (group_at + 1 - 2 * core_at, span_at)
    lin_scale = 1.0 / (size * math.sqrt(rows))
    soft_scale = 1.0 / math.sqrt(size)
    high = lax.Precision.HIGHEST

    def spot(index):
        return (index // span, lax.rem(index, span))

    def remote(src, dst, send, recv, where):
        return pltpu.make_async_remote_copy(
            src_ref=src, dst_ref=dst, send_sem=send, recv_sem=recv,
            device_id=where, device_id_type=MESH,
        )

    def each(start, stop, act):
        def one(i, _):
            act(i)
            return 0

        lax.fori_loop(start, stop, one, 0)

    weights = [
        pltpu.make_async_copy(src, w.at[m], w_sem.at[m]) for m, src in enumerate((wq, wk, wv))
    ]
    for copy in weights:
        copy.start()
    barrier = pltpu.get_barrier_semaphore()
    each(
        1, devices,
        lambda i: pl.semaphore_signal(
            barrier, inc=1, device_id=spot(lax.rem(me + i, devices)), device_id_type=MESH
        ),
    )
    down = lax.broadcasted_iota(jnp.int32, (rows, rows), 0)
    along = lax.broadcasted_iota(jnp.int32, (rows, rows), 1)
    rate = rates[...]
    by_row = dot(rate, (down <= along).astype(F32), precision=high)
    by_col = dot((down >= along).astype(F32), rate, COLS, precision=high)
    for i in range(steps):
        col[i] = by_col[:, i * pair : (i + 1) * pair]
        row[i] = by_row[i * pair : (i + 1) * pair, :]
    head = lax.broadcasted_iota(jnp.int32, (steps * pair, width), 0)
    lane = lax.broadcasted_iota(jnp.int32, (steps * pair, width), 1)
    ours = jnp.logical_and(lane >= head * size, lane < (head + 1) * size).astype(F32)
    last = jnp.broadcast_to(by_col[rows - 1 :, :], (8, steps * pair))
    total[...] = dot(last, ours, precision=high)
    listed_own = jnp.sum((listed[...] == me).astype(F32), axis=1, keepdims=True)
    listed_prev = jnp.sum((listed[...] == me - 1).astype(F32), axis=1, keepdims=True)
    key_at = lax.broadcasted_iota(jnp.int32, (1, 2 * rows), 1)
    times[...] = jnp.where(key_at < rows, listed_own, listed_prev)
    pl.semaphore_wait(barrier, devices - 1)

    after = lax.rem(me + 1, devices)
    before = lax.rem(me + devices - 1, devices)
    tokens_on = remote(tokens, prev, prev_sem.at[0], prev_sem.at[1], spot(after))
    tokens_on.start()

    def token_copy(c, n, where):
        at = gathered.at[span_of(c, rows, rows)]
        return remote(tokens if c is here else at, at, token_sem.at[0, n], token_sem.at[1, c], where)

    token_copies = [
        token_copy(here, 0, y_spot), token_copy(here, 1, core_spot), token_copy(here, 2, x_spot),
        token_copy(c_y, 3, core_spot), token_copy(c_x, 4, y_spot), token_copy(c_x, 5, core_spot),
        token_copy(c_xy, 6, core_spot),
    ]
    others_here = pl.ds(0, (plane - 1) * rows)
    token_copies[0].start()
    token_copies[1].start()

    tile, wide = came.shape[1], came.shape[2]
    across = local.shape[0] // tile
    blocks = across * (width // wide)
    mine = lax.rem(me, blocks)
    base = me - mine

    def part_of(block):
        return span_of(lax.rem(block, across), tile, tile), span_of(block // across, wide, wide)

    one_row = pl.ds(0, 1)

    def send_sums(i):
        there = lax.rem(me + i, devices)
        remote(
            total.at[one_row, part_of(lax.rem(there, blocks))[1]], decay.at[me, one_row],
            carry_sem.at[0, 0], carry_sem.at[1, 0], spot(there),
        ).start()

    each(1, devices, send_sums)

    for copy in weights:
        copy.wait()

    def project(i):
        cut = span_of(i, lanes, lanes)
        left = tokens[...]
        q[:, cut] = dot(left, w[0, :, cut]).astype(BF16)
        k[:, cut] = dot(left, w[1, :, cut]).astype(BF16)
        v[:, cut] = dot(left, w[2, :, cut]).astype(BF16)
        local[:, cut] = summary_of(
            lin_scale, size, q[:, cut], k[:, cut], v[:, cut], g[:, cut], col[i]
        )

    each(0, steps // 2, project)
    token_copies[2].start()
    each(steps // 2, steps, project)

    def send_states(i):
        there = lax.rem(me + i, devices)
        at = part_of(lax.rem(there, blocks))
        remote(
            local.at[at], came.at[me], carry_sem.at[0, 1], carry_sem.at[1, 1], spot(there)
        ).start()

    each(1, devices, send_states)
    others = pl.ds(0, devices - 1)
    all_sums = remote(
        decay.at[others, one_row], decay.at[others, one_row],
        carry_sem.at[0, 0], carry_sem.at[1, 0], spot(after),
    )
    all_states = remote(
        came.at[others], came.at[others], carry_sem.at[0, 1], carry_sem.at[1, 1], spot(after)
    )
    came[me] = local[part_of(mine)]
    decay[me] = total[:, part_of(mine)[1]]
    all_sums.wait_recv()
    decay[:, :1, :] = jnp.exp(decay[:, :1, :])


    def plane_spot(c):
        return (c // 2, depth_at * 2 + lax.rem(c, 2))

    gathered[span_of(here, rows, rows), :] = tokens[...]

    tokens_on.wait()

    def owe_copy(i):
        return remote(owe.at[i], due.at[i], owe_sem.at[0, i], owe_sem.at[1, i], spot(before))

    def near(i):
        cut = span_of(i, lanes, lanes)
        pk = dot(prev[...], w[1, :, cut]).astype(BF16)
        pv = dot(prev[...], w[2, :, cut]).astype(BF16)
        values = near_pair(
            lin_scale, soft_scale, size, q[:, cut], k[:, cut], v[:, cut], g[:, cut], pk, pv,
            col[i], row[i], times[...],
        )
        for ref, value in zip((out, dq, own_k, own_v), values):
            ref[:, cut] = value
        owe[i] = values[4]

    each(0, steps // 2, near)

    all_states.wait_recv()
    back_way = (lax.rem(mine, across) * tile) // size

    def scan(i, state):
        at = i + back_way * (devices - 1 - 2 * i)
        made[at] = state.astype(BF16)
        return decay[at, :1, :] * state + came[at].astype(F32)

    lax.fori_loop(0, devices, scan, jnp.zeros((tile, wide), F32), unroll=8)

    def send_carry(i):
        there = base + lax.rem(mine + i, blocks)
        remote(
            made.at[there], carry.at[part_of(mine)], carry_sem.at[0, 2], carry_sem.at[1, 2],
            spot(there),
        ).start()

    each(1, blocks, send_carry)
    each(0, steps // 2, lambda i: owe_copy(i).start())

    def tokens_landed(c):
        token_copy(c, 0, y_spot).wait_recv()

    tokens_landed(c_y)
    token_copies[3].start()
    other_blocks = pl.ds(0, blocks - 1)
    all_carry = remote(
        came.at[other_blocks], came.at[other_blocks], carry_sem.at[0, 2], carry_sem.at[1, 2],
        spot(after),
    )
    carry[part_of(mine)] = made[me]
    each(steps // 2, steps - 1, near)
    owe_copy(steps - 2).start()
    tokens_landed(c_x)
    token_copies[4].start()
    token_copies[5].start()
    each(steps - 1, steps, near)
    owe_copy(steps - 1).start()
    all_carry.wait_recv()

    share = (packed_q, packed_kv)
    spreads = (spread_q, spread_kv)

    def delta_copy(n, c):
        return remote(
            share[n].at[c], spreads[n].at[span_of(here, rows, rows)], delta_sem.at[0, n],
            delta_sem.at[1, n], plane_spot(c),
        )

    def hand_out(n, i, deltas):
        for u in range(lanes // LANES):
            c = i * (lanes // LANES) + u
            for m, value in enumerate(deltas):
                share[n][c, :, m * LANES : (m + 1) * LANES] = value[:, u * LANES : (u + 1) * LANES]

            @pl.when(c != here)
            def _():
                delta_copy(n, c).start()

    def finish_query(i):
        cut = span_of(i, lanes, lanes)
        terms = query_terms(lin_scale, size, q[:, cut], g[:, cut], col[i], carry[:size, cut])
        layer[:, cut] = (out[:, cut] + terms[0]).astype(BF16)
        value = (dq[:, cut] + terms[1]).astype(BF16)
        delta[0, :, cut] = value
        hand_out(0, i, (value,))

    def finish_key_value(i):
        cut = span_of(i, lanes, lanes)
        terms = key_value_terms(size, k[:, cut], v[:, cut], col[i], carry[size:, cut])
        owe_copy(i).wait_recv()
        owed = due[i].astype(F32)
        values = [
            (own_k[:, cut] + terms[0] + owed[:, :lanes]).astype(BF16),
            (own_v[:, cut] + terms[1] + owed[:, lanes:]).astype(BF16),
        ]
        for m in range(2):
            delta[1 + m, :, cut] = values[m]
        hand_out(1, i, values)

    each(0, steps, finish_query)
    tokens_landed(c_xy)
    token_copies[6].start()
    each(0, steps, finish_key_value)
    for n in range(2):
        spreads[n][span_of(here, rows, rows), :] = share[n][here]

    def token_back(i):
        cut = span_of(i, lanes, lanes)
        back[:, cut] = (
            dot(delta[0], w[0, cut, :], COLS)
            + dot(delta[1], w[1, cut, :], COLS)
            + dot(delta[2], w[2, cut, :], COLS)
        ).astype(BF16)


    for c in (here, c_x, c_y, c_xy):
        tokens_landed(c + core_step)
    all_deltas = [
        remote(
            spreads[n].at[others_here], spreads[n].at[others_here], delta_sem.at[0, n],
            delta_sem.at[1, n], spot(after),
        )
        for n in range(2)
    ]
    tall = width // depth
    in_block = max(1, lanes // tall)
    grads = (grad_q, grad_k, grad_v)
    other_parts = pl.ds(0, depth - 1)

    def depth_spot(d):
        return (group_at, d * 2 + x_at)

    def part_copy(m, d):
        return remote(
            part.at[m, span_of(d, tall, tall)], parts_in.at[m, depth_at], part_sem.at[0, m],
            part_sem.at[1, m], depth_spot(d),
        )

    def block_at(n):
        b = lax.rem(depth_at // in_block + n, width // lanes)
        return b, span_of(b, lanes, lanes)

    def send_parts(m, b):
        for u in range(in_block):
            d = b * in_block + u

            @pl.when(d != depth_at)
            def _():
                part_copy(m, d).start()

    def multiply_query(n):
        b, cut = block_at(n)
        part[0, cut, :] = dot(gathered[:, cut], spread_q[...], ROWS).astype(BF16)
        send_parts(0, b)

    def multiply_key_value(n):
        b, cut = block_at(n)
        product = dot(gathered[:, cut], spread_kv[...], ROWS).astype(BF16)
        for m in range(2):
            part[1 + m, cut, :] = product[:, m * LANES : (m + 1) * LANES]
        send_parts(1, b)

    all_deltas[0].wait_recv()
    each(1, width // lanes + 1, multiply_query)
    each(0, width // lanes // 2, token_back)
    all_deltas[1].wait_recv()
    each(1, width // lanes + 1, multiply_key_value)
    each(width // lanes // 2, width // lanes, token_back)

    half = tall // 2
    ways = ((x_spot, c_x), (y_spot, c_y))
    pieces = ((0, 0, tall, 0), (1, 0, tall, 1), (2, 0, half, 0), (2, half, half, 1))

    def block(d, c, p):
        m, start, count, _ = pieces[p]
        down = pl.ds(pl.multiple_of(d * tall + start, 16), count)
        return grads[m].at[down, span_of(c, LANES, LANES)]

    def block_copy(d, c, p, leg, where):
        return remote(block(d, c, p), block(d, c, p), sent.at[p, leg], arrive.at[p, d, c], where)

    def hop_copy(d, p, way):
        to = depth_at + 1 - 2 * way
        return remote(
            block(d, here, p), block(d, here, p), hop_sem.at[p, way, d], arrive.at[p, d, here],
            depth_spot(to),
        )

    def landed(d, c, p):
        block_copy(d, c, p, 0, spot(after)).wait_recv()

    def hop(d, p, way, act):
        to = depth_at + 1 - 2 * way

        @pl.when(jnp.logical_and(to >= 0, to < depth))
        def _():
            act(hop_copy(d, p, way))

    def around(i, act):
        for way in range(2):
            d = depth_at - i * (1 - 2 * way)
            valid = jnp.logical_and(jnp.logical_and(d >= 0, d < depth), i >= way)

            @pl.when(valid)
            def _():
                act(d, way)

    def to_ways(d, p):
        one = pieces[p][3]
        block_copy(d, here, p, 0, ways[one][0]).start()
        block_copy(d, here, p, 1, ways[1 - one][0]).start()
        block_copy(d, here, p, 2, core_spot).start()

    def step(p, i):
        def act(d, way):
            landed(d, here, p)
            hop(d, p, way, lambda copy: copy.start())
            to_ways(d, p)

        around(i, act)

    def first_leg(p, i):
        one = pieces[p][3]

        def act(d, way):
            c = ways[one][1]
            landed(d, c, p)
            block_copy(d, c, p, 1, ways[1 - one][0]).start()
            block_copy(d, c, p, 2, core_spot).start()

        around(i, act)

    def second_leg(p, i):
        def act(d, way):
            for c in (ways[1 - pieces[p][3]][1], c_xy):
                landed(d, c, p)
                block_copy(d, c, p, 2, core_spot).start()

        around(i, act)

    all_parts = [
        remote(
            parts_in.at[m, other_parts], parts_in.at[m, other_parts], part_sem.at[0, m],
            part_sem.at[1, m], spot(after),
        )
        for m in range(3)
    ]

    def sum_parts(m):
        all_parts[m].wait_recv()
        if m == 0:
            each(1, depth, lambda i: part_copy(2, lax.rem(depth_at + i, depth)).start())
        own = span_of(depth_at, tall, tall)
        parts_in[m, depth_at] = part[m, own, :]
        summed = lax.fori_loop(
            0, depth, lambda d, so_far: so_far + parts_in[m, d].astype(F32),
            jnp.zeros((tall, LANES), F32),
        )
        grads[m][own, span_of(here, LANES, LANES)] = (summed * norm).astype(BF16)
        for p, piece in enumerate(pieces):
            if piece[0] == m:
                for way in range(2):
                    hop(depth_at, p, way, lambda copy: copy.start())
                to_ways(depth_at, p)

    sum_parts(0)
    first_leg(0, 0)
    sum_parts(1)
    step(0, 1)
    first_leg(1, 0)
    sum_parts(2)
    first_leg(0, 1)
    second_leg(0, 0)
    step(0, 2)
    step(1, 1)

    def onward(n):
        for p, ahead in enumerate((2, 1, 0, 0)):
            i = n + ahead
            step(p, i)
            first_leg(p, i - 1)
            second_leg(p, i - 2)

    each(1, depth + 2, onward)

    def from_core(d):
        for p in range(len(pieces)):
            for c in (here, c_x, c_y, c_xy):
                landed(d, c + core_step, p)

    each(0, depth, from_core)

    tokens_on_rest = (all_sums, all_states, all_carry, *all_deltas, *all_parts, *token_copies)
    for copy in tokens_on_rest:
        copy.wait_send()
    each(0, steps, lambda i: owe_copy(i).wait_send())
    for p, (m, _, count, _) in enumerate(pieces):
        for leg, columns in enumerate((1, 2, 4)):
            ref = grads[m].at[pl.ds(0, depth * count), pl.ds(0, columns * LANES)]
            remote(ref, ref, sent.at[p, leg], arrive.at[p, 0, 0], spot(after)).wait_send()

    def hops_left(i):
        def act(d, way):
            for p in range(len(pieces)):
                hop(d, p, way, lambda copy: copy.wait_send())

        around(i, act)

    each(1, depth, hops_left)
    for p in range(len(pieces)):
        for way in range(2):
            hop(depth_at, p, way, lambda copy: copy.wait_send())


def leave_kernel(*refs):
    count = len(refs) // 2
    sem = refs[-1]
    copies = [pltpu.make_async_copy(refs[i], refs[count + i], sem.at[i]) for i in range(count)]
    for copy in copies:
        copy.start()
    for copy in copies:
        copy.wait()


def shards(tokens, query_weight, key_weight, value_weight, log_decay, neighbour_blocks, cotangent):
    rows, width = tokens.shape
    heads = log_decay.shape[0]
    size = width // heads
    pair = 256 // size
    steps = heads // pair
    lanes = pair * size
    sizes = tuple(lax.axis_size(name) for name in AXES)
    devices = sizes[0] * sizes[1]
    tile = 16
    blocks = min(devices, 2 * size // tile * (width // LANES))
    part = width // (blocks // (2 * size // tile))
    plane, depth = 2 * sizes[0], sizes[1] // 2

    norm = 1.0 / math.sqrt(rows * devices)

    vmem = pl.BlockSpec(memory_space=pltpu.VMEM)
    hbm = pl.BlockSpec(memory_space=pltpu.HBM)
    semaphores = pltpu.SemaphoreType.DMA
    results = pl.pallas_call(
        functools.partial(layer_kernel, sizes, size, norm),
        in_specs=[vmem] * 4 + [hbm] * 3,
        out_specs=[vmem] * 5,
        out_shape=[pltpu.VMEM((rows, width), BF16)] * 2 + [pltpu.VMEM((width, width), BF16)] * 3,
        scratch_shapes=[
            pltpu.VMEM((3, width, width), BF16),
            pltpu.VMEM((1, 2 * rows), F32),
            pltpu.VMEM((rows, width), BF16),
            pltpu.VMEM((rows, width), BF16),
            pltpu.VMEM((rows, width), BF16),
            pltpu.VMEM((rows, width), BF16),
            pltpu.VMEM((2 * size, width), BF16),
            pltpu.VMEM((8, width), F32),
            pltpu.VMEM((steps, rows, pair), F32),
            pltpu.VMEM((steps, pair, rows), F32),
            pltpu.VMEM((devices, tile, part), BF16),
            pltpu.VMEM((devices, 8, part), F32),
            pltpu.VMEM((devices, tile, part), BF16),
            pltpu.VMEM((2 * size, width), BF16),
            pltpu.VMEM((rows, width), F32),
            pltpu.VMEM((rows, width), F32),
            pltpu.VMEM((rows, width), F32),
            pltpu.VMEM((rows, width), F32),
            pltpu.VMEM((steps, rows, 2 * lanes), BF16),
            pltpu.VMEM((steps, rows, 2 * lanes), BF16),
            pltpu.VMEM((3, rows, width), BF16),
            pltpu.VMEM((plane, rows, LANES), BF16),
            pltpu.VMEM((plane, rows, 2 * LANES), BF16),
            pltpu.VMEM((plane * rows, LANES), BF16),
            pltpu.VMEM((plane * rows, 2 * LANES), BF16),
            pltpu.VMEM((plane * rows, width), BF16),
            pltpu.VMEM((3, width, LANES), BF16),
            pltpu.VMEM((3, depth, width // depth, LANES), BF16),
            semaphores((3,)),
            semaphores((2,)),
            semaphores((2, 3)),
            semaphores((2, steps)),
            semaphores((2, plane)),
            semaphores((2, 2)),
            semaphores((2, 3)),
            semaphores((4, depth, plane)),
            semaphores((4, 3)),
            semaphores((4, 2, depth)),
        ],
        compiler_params=pltpu.CompilerParams(
            collective_id=0, has_side_effects=True, vmem_limit_bytes=57 * 2**20
        ),
        cost_estimate=pl.CostEstimate(flops=10**9, bytes_accessed=10**8, transcendentals=0),
    )(
        tokens, cotangent, neighbour_blocks, log_decay,
        *(pltpu.with_memory_space_constraint(x, pltpu.HBM) for x in (query_weight, key_weight, value_weight)),
    )
    return pl.pallas_call(
        leave_kernel,
        in_specs=[vmem] * len(results),
        out_specs=[hbm] * len(results),
        out_shape=[jax.ShapeDtypeStruct(x.shape, x.dtype) for x in results],
        scratch_shapes=[semaphores((len(results),))],
        compiler_params=pltpu.CompilerParams(vmem_limit_bytes=2**20),
        cost_estimate=pl.CostEstimate(flops=0, bytes_accessed=10**7, transcendentals=0),
    )(*(pltpu.with_memory_space_constraint(x, pltpu.VMEM) for x in results))


def solution(mesh):
    return jax.shard_map(
        shards,
        mesh=mesh,
        in_specs=(
            P(AXES, None),
            P(),
            P(),
            P(),
            P(None, AXES),
            P(AXES, None),
            P(AXES, None),
        ),
        out_specs=(P(AXES, None), P(AXES, None), P(), P(), P()),
        check_vma=False,
    )
```

```python
import functools
import math

import jax
import jax.numpy as jnp
from jax import lax
from jax.experimental import pallas as pl
from jax.experimental.pallas import tpu as pltpu
from jax.sharding import PartitionSpec as P

AXES = ("group", "span")
F32 = jnp.float32
BF16 = jnp.bfloat16
ROWS = (((0,), (0,)), ((), ()))
COLS = (((1,), (1,)), ((), ()))
MESH = pl.DeviceIdType.MESH
LANES = 128


def dot(a, b, dims=(((1,), (0,)), ((), ())), precision=None):
    return lax.dot_general(a, b, dims, precision=precision, preferred_element_type=F32)


def summary_of(lin_scale, size, q, k, v, g, col):
    heads = q.shape[1] // size
    states, grads = [], []
    for j in range(heads):
        cut = slice(j * size, (j + 1) * size)
        run = col[:, j : j + 1]
        fading = jnp.exp(run[run.shape[0] - 1 :, :] - run)
        weighted = (v[:, cut].astype(F32) * fading).astype(BF16)
        scaled = (g[:, cut].astype(F32) * jnp.exp(run)).astype(BF16)
        states.append(dot(k[:, cut], weighted, ROWS))
        grads.append(lin_scale * dot(q[:, cut], scaled, ROWS))
    return jnp.concatenate(
        [jnp.concatenate(states, axis=1), jnp.concatenate(grads, axis=1)], axis=0
    ).astype(BF16)


def near_pair(lin_scale, soft_scale, size, q, k, v, g, pk, pv, col, row, times):
    rows = q.shape[0]
    heads = q.shape[1] // size
    t = lax.broadcasted_iota(jnp.int32, (rows, rows), 0)
    s = lax.broadcasted_iota(jnp.int32, (rows, rows), 1)
    lower = t >= s
    outs, dqs, dkv, dvv = [], [], [], []
    for j in range(heads):
        cut = slice(j * size, (j + 1) * size)
        qh, gh = q[:, cut], g[:, cut]
        kh = jnp.concatenate([k[:, cut], pk[:, cut]], axis=0)
        vh = jnp.concatenate([v[:, cut], pv[:, cut]], axis=0)
        decay = jnp.where(
            lower, jnp.exp(jnp.minimum(col[:, j : j + 1] - row[j : j + 1, :], 0.0)), 0.0
        ) * lin_scale
        score = dot(qh, kh, COLS)
        grad = dot(gh, vh, COLS)
        logits = jnp.where(times > 0.0, score * soft_scale, -1e30)
        peak = jnp.max(logits, axis=1, keepdims=True)
        terms = jnp.exp(logits - peak) * times
        probs = terms / jnp.sum(terms, axis=1, keepdims=True)
        inner = jnp.sum(probs * grad, axis=1, keepdims=True)
        dlogit = probs * (grad - inner) * soft_scale
        mix = jnp.concatenate(
            [probs[:, :rows] + score[:, :rows] * decay, probs[:, rows:]], axis=1
        ).astype(BF16)
        dmix = jnp.concatenate(
            [dlogit[:, :rows] + grad[:, :rows] * decay, dlogit[:, rows:]], axis=1
        ).astype(BF16)
        outs.append(dot(mix, vh))
        dqs.append(dot(dmix, kh))
        dkv.append(dot(dmix, qh, ROWS))
        dvv.append(dot(mix, gh, ROWS))
    dk = jnp.concatenate(dkv, axis=1)
    dv = jnp.concatenate(dvv, axis=1)
    return (
        jnp.concatenate(outs, axis=1),
        jnp.concatenate(dqs, axis=1),
        dk[:rows],
        dv[:rows],
        jnp.concatenate([dk[rows:], dv[rows:]], axis=1).astype(BF16),
    )


def query_terms(lin_scale, size, q, g, col, state):
    heads = q.shape[1] // size
    outs, dqs = [], []
    for j in range(heads):
        cut = slice(j * size, (j + 1) * size)
        growth = lin_scale * jnp.exp(col[:, j : j + 1])
        st = state[:, cut]
        outs.append(growth * dot(q[:, cut], st))
        dqs.append(growth * dot(g[:, cut], st, COLS))
    return jnp.concatenate(outs, axis=1), jnp.concatenate(dqs, axis=1)


def key_value_terms(size, k, v, col, later):
    heads = k.shape[1] // size
    dks, dvs = [], []
    for j in range(heads):
        cut = slice(j * size, (j + 1) * size)
        run = col[:, j : j + 1]
        fading = jnp.exp(run[run.shape[0] - 1 :, :] - run)
        lt = later[:, cut]
        dks.append(fading * dot(v[:, cut], lt, COLS))
        dvs.append(fading * dot(k[:, cut], lt))
    return jnp.concatenate(dks, axis=1), jnp.concatenate(dvs, axis=1)


def span_of(start, step, length):
    return pl.ds(pl.multiple_of(start * step, step), length)


def layer_kernel(
    sizes, size, norm,
    tokens, g, listed, rates, wq, wk, wv,
    layer, back, grad_q, grad_k, grad_v,
    w, times, q, k, v, prev, local, total, col, row,
    came, decay, made, carry, out, dq, own_k, own_v, owe, due, delta,
    packed_q, packed_kv, spread_q, spread_kv, gathered, part, parts_in,
    w_sem, prev_sem, carry_sem, owe_sem, token_sem, delta_sem, part_sem, arrive, sent, hop_sem,
):
    rows, width = tokens.shape
    steps, _, pair = col.shape
    lanes = pair * size
    devices, span = sizes[0] * sizes[1], sizes[1]
    group_at, span_at = lax.axis_index("group"), lax.axis_index("span")
    me = group_at * span + span_at
    depth_at, x_at = span_at // 2, lax.rem(span_at, 2)
    depth = span // 2
    plane = 2 * sizes[0]
    here = group_at * 2 + x_at
    core_at, y_at = lax.rem(group_at, 2), group_at // 2
    x_step, y_step, core_step = 1 - 2 * x_at, 4 * (1 - 2 * y_at), 2 * (1 - 2 * core_at)
    c_x, c_y = here + x_step, here + y_step
    c_xy = here + x_step + y_step
    x_spot = (group_at, span_at + x_step)
    y_spot = (group_at + 2 * (1 - 2 * y_at), span_at)
    core_spot = (group_at + 1 - 2 * core_at, span_at)
    lin_scale = 1.0 / (size * math.sqrt(rows))
    soft_scale = 1.0 / math.sqrt(size)
    high = lax.Precision.HIGHEST

    def spot(index):
        return (index // span, lax.rem(index, span))

    def remote(src, dst, send, recv, where):
        return pltpu.make_async_remote_copy(
            src_ref=src, dst_ref=dst, send_sem=send, recv_sem=recv,
            device_id=where, device_id_type=MESH,
        )

    def each(start, stop, act):
        def one(i, _):
            act(i)
            return 0

        lax.fori_loop(start, stop, one, 0)

    weights = [
        pltpu.make_async_copy(src, w.at[m], w_sem.at[m]) for m, src in enumerate((wq, wk, wv))
    ]
    for copy in weights:
        copy.start()
    barrier = pltpu.get_barrier_semaphore()
    each(
        1, devices,
        lambda i: pl.semaphore_signal(
            barrier, inc=1, device_id=spot(lax.rem(me + i, devices)), device_id_type=MESH
        ),
    )
    down = lax.broadcasted_iota(jnp.int32, (rows, rows), 0)
    along = lax.broadcasted_iota(jnp.int32, (rows, rows), 1)
    rate = rates[...]
    by_row = dot(rate, (down <= along).astype(F32), precision=high)
    by_col = dot((down >= along).astype(F32), rate, COLS, precision=high)
    for i in range(steps):
        col[i] = by_col[:, i * pair : (i + 1) * pair]
        row[i] = by_row[i * pair : (i + 1) * pair, :]
    head = lax.broadcasted_iota(jnp.int32, (steps * pair, width), 0)
    lane = lax.broadcasted_iota(jnp.int32, (steps * pair, width), 1)
    ours = jnp.logical_and(lane >= head * size, lane < (head + 1) * size).astype(F32)
    last = jnp.broadcast_to(by_col[rows - 1 :, :], (8, steps * pair))
    total[...] = dot(last, ours, precision=high)
    listed_own = jnp.sum((listed[...] == me).astype(F32), axis=1, keepdims=True)
    listed_prev = jnp.sum((listed[...] == me - 1).astype(F32), axis=1, keepdims=True)
    key_at = lax.broadcasted_iota(jnp.int32, (1, 2 * rows), 1)
    times[...] = jnp.where(key_at < rows, listed_own, listed_prev)
    pl.semaphore_wait(barrier, devices - 1)

    after = lax.rem(me + 1, devices)
    before = lax.rem(me + devices - 1, devices)
    tokens_on = remote(tokens, prev, prev_sem.at[0], prev_sem.at[1], spot(after))
    tokens_on.start()

    def token_copy(c, n, where):
        at = gathered.at[span_of(c, rows, rows)]
        return remote(tokens if c is here else at, at, token_sem.at[0, n], token_sem.at[1, c], where)

    token_copies = [
        token_copy(here, 0, y_spot), token_copy(here, 1, core_spot), token_copy(here, 2, x_spot),
        token_copy(c_y, 3, core_spot), token_copy(c_x, 4, y_spot), token_copy(c_x, 5, core_spot),
        token_copy(c_xy, 6, core_spot),
    ]
    others_here = pl.ds(0, (plane - 1) * rows)
    token_copies[0].start()
    token_copies[1].start()

    tile, wide = came.shape[1], came.shape[2]
    across = local.shape[0] // tile
    blocks = across * (width // wide)
    mine = lax.rem(me, blocks)
    base = me - mine

    def part_of(block):
        return span_of(lax.rem(block, across), tile, tile), span_of(block // across, wide, wide)

    one_row = pl.ds(0, 1)

    def send_sums(i):
        there = lax.rem(me + i, devices)
        remote(
            total.at[one_row, part_of(lax.rem(there, blocks))[1]], decay.at[me, one_row],
            carry_sem.at[0, 0], carry_sem.at[1, 0], spot(there),
        ).start()

    each(1, devices, send_sums)

    for copy in weights:
        copy.wait()

    in_step = lanes // wide * across

    def send_states(i):
        def one(u):
            there = u // in_step * blocks + i * in_step + lax.rem(u + span_at, in_step)

            @pl.when(there != me)
            def _():
                remote(
                    local.at[part_of(lax.rem(there, blocks))], came.at[me], carry_sem.at[0, 1],
                    carry_sem.at[1, 1], spot(there),
                ).start()

        each(0, devices // blocks * in_step, one)

    def project(i):
        cut = span_of(i, lanes, lanes)
        left = tokens[...]
        q[:, cut] = dot(left, w[0, :, cut]).astype(BF16)
        k[:, cut] = dot(left, w[1, :, cut]).astype(BF16)
        v[:, cut] = dot(left, w[2, :, cut]).astype(BF16)
        local[:, cut] = summary_of(
            lin_scale, size, q[:, cut], k[:, cut], v[:, cut], g[:, cut], col[i]
        )
        send_states(i)

    each(0, steps // 2, project)
    each(steps // 2, steps, project)
    token_copies[2].start()

    others = pl.ds(0, devices - 1)
    all_sums = remote(
        decay.at[others, one_row], decay.at[others, one_row],
        carry_sem.at[0, 0], carry_sem.at[1, 0], spot(after),
    )
    all_states = remote(
        came.at[others], came.at[others], carry_sem.at[0, 1], carry_sem.at[1, 1], spot(after)
    )
    came[me] = local[part_of(mine)]
    decay[me] = total[:, part_of(mine)[1]]
    all_sums.wait_recv()
    decay[:, :1, :] = jnp.exp(decay[:, :1, :])


    def plane_spot(c):
        return (c // 2, depth_at * 2 + lax.rem(c, 2))

    gathered[span_of(here, rows, rows), :] = tokens[...]

    tokens_on.wait()

    def owe_copy(i):
        return remote(owe.at[i], due.at[i], owe_sem.at[0, i], owe_sem.at[1, i], spot(before))

    def near(i):
        cut = span_of(i, lanes, lanes)
        pk = dot(prev[...], w[1, :, cut]).astype(BF16)
        pv = dot(prev[...], w[2, :, cut]).astype(BF16)
        values = near_pair(
            lin_scale, soft_scale, size, q[:, cut], k[:, cut], v[:, cut], g[:, cut], pk, pv,
            col[i], row[i], times[...],
        )
        for ref, value in zip((out, dq, own_k, own_v), values):
            ref[:, cut] = value
        owe[i] = values[4]

    each(0, steps // 2, near)

    all_states.wait_recv()
    back_way = (lax.rem(mine, across) * tile) // size

    def scan(i, state):
        at = i + back_way * (devices - 1 - 2 * i)
        made[at] = state.astype(BF16)
        return decay[at, :1, :] * state + came[at].astype(F32)

    lax.fori_loop(0, devices, scan, jnp.zeros((tile, wide), F32), unroll=8)

    def send_carry(i):
        there = base + lax.rem(mine + i, blocks)
        remote(
            made.at[there], carry.at[part_of(mine)], carry_sem.at[0, 2], carry_sem.at[1, 2],
            spot(there),
        ).start()

    each(1, blocks, send_carry)
    each(0, steps // 2, lambda i: owe_copy(i).start())

    def tokens_landed(c):
        token_copy(c, 0, y_spot).wait_recv()

    tokens_landed(c_y)
    token_copies[3].start()
    other_blocks = pl.ds(0, blocks - 1)
    all_carry = remote(
        came.at[other_blocks], came.at[other_blocks], carry_sem.at[0, 2], carry_sem.at[1, 2],
        spot(after),
    )
    carry[part_of(mine)] = made[me]
    each(steps // 2, steps - 1, near)
    owe_copy(steps - 2).start()
    tokens_landed(c_x)
    token_copies[4].start()
    token_copies[5].start()
    each(steps - 1, steps, near)
    owe_copy(steps - 1).start()
    all_carry.wait_recv()

    share = (packed_q, packed_kv)
    spreads = (spread_q, spread_kv)

    def delta_copy(n, c):
        return remote(
            share[n].at[c], spreads[n].at[span_of(here, rows, rows)], delta_sem.at[0, n],
            delta_sem.at[1, n], plane_spot(c),
        )

    def hand_out(n, i, deltas):
        for u in range(lanes // LANES):
            c = i * (lanes // LANES) + u
            for m, value in enumerate(deltas):
                share[n][c, :, m * LANES : (m + 1) * LANES] = value[:, u * LANES : (u + 1) * LANES]

            @pl.when(c != here)
            def _():
                delta_copy(n, c).start()

    def finish_query(i):
        cut = span_of(i, lanes, lanes)
        terms = query_terms(lin_scale, size, q[:, cut], g[:, cut], col[i], carry[:size, cut])
        layer[:, cut] = (out[:, cut] + terms[0]).astype(BF16)
        value = (dq[:, cut] + terms[1]).astype(BF16)
        delta[0, :, cut] = value
        hand_out(0, i, (value,))

    def finish_key_value(i):
        cut = span_of(i, lanes, lanes)
        terms = key_value_terms(size, k[:, cut], v[:, cut], col[i], carry[size:, cut])
        owe_copy(i).wait_recv()
        owed = due[i].astype(F32)
        values = [
            (own_k[:, cut] + terms[0] + owed[:, :lanes]).astype(BF16),
            (own_v[:, cut] + terms[1] + owed[:, lanes:]).astype(BF16),
        ]
        for m in range(2):
            delta[1 + m, :, cut] = values[m]
        hand_out(1, i, values)

    each(0, steps, finish_query)
    tokens_landed(c_xy)
    token_copies[6].start()
    each(0, steps, finish_key_value)
    for n in range(2):
        spreads[n][span_of(here, rows, rows), :] = share[n][here]

    def token_back(i):
        cut = span_of(i, lanes, lanes)
        back[:, cut] = (
            dot(delta[0], w[0, cut, :], COLS)
            + dot(delta[1], w[1, cut, :], COLS)
            + dot(delta[2], w[2, cut, :], COLS)
        ).astype(BF16)


    for c in (here, c_x, c_y, c_xy):
        tokens_landed(c + core_step)
    all_deltas = [
        remote(
            spreads[n].at[others_here], spreads[n].at[others_here], delta_sem.at[0, n],
            delta_sem.at[1, n], spot(after),
        )
        for n in range(2)
    ]
    tall = width // depth
    in_block = max(1, lanes // tall)
    grads = (grad_q, grad_k, grad_v)
    other_parts = pl.ds(0, depth - 1)

    def depth_spot(d):
        return (group_at, d * 2 + x_at)

    def part_copy(m, d):
        return remote(
            part.at[m, span_of(d, tall, tall)], parts_in.at[m, depth_at], part_sem.at[0, m],
            part_sem.at[1, m], depth_spot(d),
        )

    def block_at(n):
        b = lax.rem(depth_at // in_block + n, width // lanes)
        return b, span_of(b, lanes, lanes)

    def send_parts(m, b):
        for u in range(in_block):
            d = b * in_block + u

            @pl.when(d != depth_at)
            def _():
                part_copy(m, d).start()

    def multiply_query(n):
        b, cut = block_at(n)
        part[0, cut, :] = dot(gathered[:, cut], spread_q[...], ROWS).astype(BF16)
        send_parts(0, b)

    def multiply_key_value(n):
        b, cut = block_at(n)
        product = dot(gathered[:, cut], spread_kv[...], ROWS).astype(BF16)
        for m in range(2):
            part[1 + m, cut, :] = product[:, m * LANES : (m + 1) * LANES]
        send_parts(1, b)

    all_deltas[0].wait_recv()
    each(1, width // lanes + 1, multiply_query)
    each(0, width // lanes // 2, token_back)
    all_deltas[1].wait_recv()
    each(1, width // lanes + 1, multiply_key_value)
    each(width // lanes // 2, width // lanes, token_back)

    half = tall // 2
    ways = ((x_spot, c_x), (y_spot, c_y))
    pieces = ((0, 0, tall, 0), (1, 0, tall, 1), (2, 0, half, 0), (2, half, half, 1))

    def block(d, c, p):
        m, start, count, _ = pieces[p]
        down = pl.ds(pl.multiple_of(d * tall + start, 16), count)
        return grads[m].at[down, span_of(c, LANES, LANES)]

    def block_copy(d, c, p, leg, where):
        return remote(block(d, c, p), block(d, c, p), sent.at[p, leg], arrive.at[p, d, c], where)

    def hop_copy(d, p, way):
        to = depth_at + 1 - 2 * way
        return remote(
            block(d, here, p), block(d, here, p), hop_sem.at[p, way, d], arrive.at[p, d, here],
            depth_spot(to),
        )

    def landed(d, c, p):
        block_copy(d, c, p, 0, spot(after)).wait_recv()

    def hop(d, p, way, act):
        to = depth_at + 1 - 2 * way

        @pl.when(jnp.logical_and(to >= 0, to < depth))
        def _():
            act(hop_copy(d, p, way))

    def around(i, act):
        for way in range(2):
            d = depth_at - i * (1 - 2 * way)
            valid = jnp.logical_and(jnp.logical_and(d >= 0, d < depth), i >= way)

            @pl.when(valid)
            def _():
                act(d, way)

    def to_ways(d, p):
        one = pieces[p][3]
        block_copy(d, here, p, 0, ways[one][0]).start()
        block_copy(d, here, p, 1, ways[1 - one][0]).start()
        block_copy(d, here, p, 2, core_spot).start()

    def step(p, i):
        def act(d, way):
            landed(d, here, p)
            hop(d, p, way, lambda copy: copy.start())
            to_ways(d, p)

        around(i, act)

    def first_leg(p, i):
        one = pieces[p][3]

        def act(d, way):
            c = ways[one][1]
            landed(d, c, p)
            block_copy(d, c, p, 1, ways[1 - one][0]).start()
            block_copy(d, c, p, 2, core_spot).start()

        around(i, act)

    def second_leg(p, i):
        def act(d, way):
            for c in (ways[1 - pieces[p][3]][1], c_xy):
                landed(d, c, p)
                block_copy(d, c, p, 2, core_spot).start()

        around(i, act)

    all_parts = [
        remote(
            parts_in.at[m, other_parts], parts_in.at[m, other_parts], part_sem.at[0, m],
            part_sem.at[1, m], spot(after),
        )
        for m in range(3)
    ]

    def sum_parts(m):
        all_parts[m].wait_recv()
        if m == 0:
            each(1, depth, lambda i: part_copy(2, lax.rem(depth_at + i, depth)).start())
        own = span_of(depth_at, tall, tall)
        parts_in[m, depth_at] = part[m, own, :]
        summed = lax.fori_loop(
            0, depth, lambda d, so_far: so_far + parts_in[m, d].astype(F32),
            jnp.zeros((tall, LANES), F32),
        )
        grads[m][own, span_of(here, LANES, LANES)] = (summed * norm).astype(BF16)
        for p, piece in enumerate(pieces):
            if piece[0] == m:
                for way in range(2):
                    hop(depth_at, p, way, lambda copy: copy.start())
                to_ways(depth_at, p)

    sum_parts(0)
    first_leg(0, 0)
    sum_parts(1)
    step(0, 1)
    first_leg(1, 0)
    sum_parts(2)
    first_leg(0, 1)
    second_leg(0, 0)
    step(0, 2)
    step(1, 1)

    def onward(n):
        for p, ahead in enumerate((2, 1, 0, 0)):
            i = n + ahead
            step(p, i)
            first_leg(p, i - 1)
            second_leg(p, i - 2)

    each(1, depth + 2, onward)

    def from_core(d):
        for p in range(len(pieces)):
            for c in (here, c_x, c_y, c_xy):
                landed(d, c + core_step, p)

    each(0, depth, from_core)

    tokens_on_rest = (all_sums, all_states, all_carry, *all_deltas, *all_parts, *token_copies)
    for copy in tokens_on_rest:
        copy.wait_send()
    each(0, steps, lambda i: owe_copy(i).wait_send())
    for p, (m, _, count, _) in enumerate(pieces):
        for leg, columns in enumerate((1, 2, 4)):
            ref = grads[m].at[pl.ds(0, depth * count), pl.ds(0, columns * LANES)]
            remote(ref, ref, sent.at[p, leg], arrive.at[p, 0, 0], spot(after)).wait_send()

    def hops_left(i):
        def act(d, way):
            for p in range(len(pieces)):
                hop(d, p, way, lambda copy: copy.wait_send())

        around(i, act)

    each(1, depth, hops_left)
    for p in range(len(pieces)):
        for way in range(2):
            hop(depth_at, p, way, lambda copy: copy.wait_send())


def leave_kernel(*refs):
    count = len(refs) // 2
    sem = refs[-1]
    copies = [pltpu.make_async_copy(refs[i], refs[count + i], sem.at[i]) for i in range(count)]
    for copy in copies:
        copy.start()
    for copy in copies:
        copy.wait()


def shards(tokens, query_weight, key_weight, value_weight, log_decay, neighbour_blocks, cotangent):
    rows, width = tokens.shape
    heads = log_decay.shape[0]
    size = width // heads
    pair = 256 // size
    steps = heads // pair
    lanes = pair * size
    sizes = tuple(lax.axis_size(name) for name in AXES)
    devices = sizes[0] * sizes[1]
    tile = 16
    blocks = min(devices, 2 * size // tile * (width // LANES))
    part = width // (blocks // (2 * size // tile))
    plane, depth = 2 * sizes[0], sizes[1] // 2

    norm = 1.0 / math.sqrt(rows * devices)

    vmem = pl.BlockSpec(memory_space=pltpu.VMEM)
    hbm = pl.BlockSpec(memory_space=pltpu.HBM)
    semaphores = pltpu.SemaphoreType.DMA
    results = pl.pallas_call(
        functools.partial(layer_kernel, sizes, size, norm),
        in_specs=[vmem] * 4 + [hbm] * 3,
        out_specs=[vmem] * 5,
        out_shape=[pltpu.VMEM((rows, width), BF16)] * 2 + [pltpu.VMEM((width, width), BF16)] * 3,
        scratch_shapes=[
            pltpu.VMEM((3, width, width), BF16),
            pltpu.VMEM((1, 2 * rows), F32),
            pltpu.VMEM((rows, width), BF16),
            pltpu.VMEM((rows, width), BF16),
            pltpu.VMEM((rows, width), BF16),
            pltpu.VMEM((rows, width), BF16),
            pltpu.VMEM((2 * size, width), BF16),
            pltpu.VMEM((8, width), F32),
            pltpu.VMEM((steps, rows, pair), F32),
            pltpu.VMEM((steps, pair, rows), F32),
            pltpu.VMEM((devices, tile, part), BF16),
            pltpu.VMEM((devices, 8, part), F32),
            pltpu.VMEM((devices, tile, part), BF16),
            pltpu.VMEM((2 * size, width), BF16),
            pltpu.VMEM((rows, width), F32),
            pltpu.VMEM((rows, width), F32),
            pltpu.VMEM((rows, width), F32),
            pltpu.VMEM((rows, width), F32),
            pltpu.VMEM((steps, rows, 2 * lanes), BF16),
            pltpu.VMEM((steps, rows, 2 * lanes), BF16),
            pltpu.VMEM((3, rows, width), BF16),
            pltpu.VMEM((plane, rows, LANES), BF16),
            pltpu.VMEM((plane, rows, 2 * LANES), BF16),
            pltpu.VMEM((plane * rows, LANES), BF16),
            pltpu.VMEM((plane * rows, 2 * LANES), BF16),
            pltpu.VMEM((plane * rows, width), BF16),
            pltpu.VMEM((3, width, LANES), BF16),
            pltpu.VMEM((3, depth, width // depth, LANES), BF16),
            semaphores((3,)),
            semaphores((2,)),
            semaphores((2, 3)),
            semaphores((2, steps)),
            semaphores((2, plane)),
            semaphores((2, 2)),
            semaphores((2, 3)),
            semaphores((4, depth, plane)),
            semaphores((4, 3)),
            semaphores((4, 2, depth)),
        ],
        compiler_params=pltpu.CompilerParams(
            collective_id=0, has_side_effects=True, vmem_limit_bytes=57 * 2**20
        ),
        cost_estimate=pl.CostEstimate(flops=10**9, bytes_accessed=10**8, transcendentals=0),
    )(
        tokens, cotangent, neighbour_blocks, log_decay,
        *(pltpu.with_memory_space_constraint(x, pltpu.HBM) for x in (query_weight, key_weight, value_weight)),
    )
    return pl.pallas_call(
        leave_kernel,
        in_specs=[vmem] * len(results),
        out_specs=[hbm] * len(results),
        out_shape=[jax.ShapeDtypeStruct(x.shape, x.dtype) for x in results],
        scratch_shapes=[semaphores((len(results),))],
        compiler_params=pltpu.CompilerParams(vmem_limit_bytes=2**20),
        cost_estimate=pl.CostEstimate(flops=0, bytes_accessed=10**7, transcendentals=0),
    )(*(pltpu.with_memory_space_constraint(x, pltpu.VMEM) for x in results))


def solution(mesh):
    return jax.shard_map(
        shards,
        mesh=mesh,
        in_specs=(
            P(AXES, None),
            P(),
            P(),
            P(),
            P(None, AXES),
            P(AXES, None),
            P(AXES, None),
        ),
        out_specs=(P(AXES, None), P(AXES, None), P(), P(), P()),
        check_vma=False,
    )
```
